256 devices in a mesh: var: 4 (over x_hi, core), ty: 8 (over x_lo, y), tx: 8 (over z).
Axes of the slice: x: 4 (x_hi: 2, x_lo: 2; x = x_hi * 2 + x_lo), y: 4, z: 8, core: 2. Of those that a mesh axis runs over, the one named last changes fastest.
Arguments:
- features: bfloat16 [256, 256, 180], P('ty', 'tx'), may hold values from -6 to 6
- labels: int32 [256, 256], P('ty', 'tx'), may hold values from 1 to 4
- qkv_weight: bfloat16 [2, 180, 540], replicated, may hold values from -0.4375 to 0.4375
- proj_weight: bfloat16 [2, 180, 180], replicated, may hold values from -0.4375 to 0.4375
- up_weight: bfloat16 [2, 180, 360], replicated, may hold values from -0.4375 to 0.4375
- down_weight: bfloat16 [2, 360, 180], replicated, may hold values from -0.3125 to 0.3125
- swin_bias: float32 [2, 6, 225], replicated, may hold values from -340 to 340
- recon_weight: bfloat16 [9, 180, 48], replicated, may hold values from -0.3125 to 0.3125
- refine_qkv: bfloat16 [48, 144], replicated, may hold values from -0.875 to 0.875
- refine_proj: bfloat16 [48, 48], replicated, may hold values from -0.875 to 0.875
- refine_bias: float32 [2, 225], replicated, may hold values from -340 to 340
Outputs:
- restored: float32 [3, 1024, 1024], P(None, 'ty', 'tx')
The draws below stay inside these ranges and needn't reach their ends.
All inputs are finite; a program needn't handle non-finite values.
Results may differ from the reference program's by a relative error of at most 0.015.
Values may be sent and summed in bfloat16 or wider, within the bound.
A program may use at most 128 MiB of HBM per device.

```python
import jax
import jax.numpy as jnp
from jax import lax

C = 180
HEADS = 6
HID = 360
WIN = 8
SHIFT = 4
SCALE = 4
OUTC = 48
RHEADS = 2
IMAGE = 256


def drawn_bias(key, leading):
    count = (2 * WIN - 1) * (2 * WIN - 1)
    sample = jax.random.normal(jax.random.fold_in(key, 13), leading + (count,), jnp.float32)
    return 1.5 * jnp.clip(sample, -3.0, 3.0)


def draw_swin_bias(key, part):
    return drawn_bias(key, (2, HEADS))


def draw_refine_bias(key, part):
    return drawn_bias(key, (RHEADS,))


def band_steps(key):
    positions = jnp.arange(IMAGE, dtype=jnp.int32)
    cuts = jax.random.randint(key, (IMAGE,), 0, 24) == 0
    cuts = cuts | (positions == IMAGE // 2)
    cuts = jnp.where(positions == 0, False, cuts)
    return jnp.cumsum(cuts.astype(jnp.int32))


def draw_labels(key, part):
    row_band = band_steps(jax.random.fold_in(key, 21))
    col_band = band_steps(jax.random.fold_in(key, 22))
    return (1 + (row_band[:, None] + 2 * col_band[None, :]) % 4).astype(jnp.int32)


def steps_of(key, dims, shards, least, high):
    factor_of, own = 1.0, jax.random.fold_in(key, 6)
    for dim, blocks in shards:
        draws = jnp.exp(jax.random.uniform(jax.random.fold_in(own, dim), (blocks,), jnp.float32, least / len(shards), high / len(shards)))
        factor_of = factor_of * jnp.repeat(draws, dims[dim] // blocks).reshape([-1 if axis == dim else 1 for axis in range(len(dims))])
    return factor_of


def normal_values(stream_key, shape, scale, reach, pieces=(), held_as=jnp.bfloat16):
    values = jax.random.normal(stream_key, shape, jnp.float32) * scale
    if len(pieces) > 0:
        values = steps_of(stream_key, shape, pieces, -0.22, 0.18) * values
    return jnp.clip(values, min=-reach, max=reach).astype(held_as)


def setup_inputs(seed: int = 0) -> dict:
    seeds = jax.random.split(jax.random.key(seed), 12)
    return {
        "features": normal_values(seeds[0], (IMAGE, IMAGE, C), 1.0, 6.0, ((0, 8), (1, 8))),
        "labels": draw_labels(jax.random.fold_in(seeds[11], 71), 0),
        "qkv_weight": normal_values(seeds[2], (2, C, 3 * C), C ** -0.5, 0.4375),
        "proj_weight": normal_values(seeds[3], (2, C, C), C ** -0.5, 0.4375),
        "up_weight": normal_values(seeds[4], (2, C, HID), C ** -0.5, 0.4375),
        "down_weight": normal_values(seeds[5], (2, HID, C), HID ** -0.5, 0.3125),
        "swin_bias": draw_swin_bias(jax.random.fold_in(seeds[11], 71), 0),
        "recon_weight": normal_values(seeds[7], (9, C, OUTC), (9 * C // 4) ** -0.5, 0.3125),
        "refine_qkv": normal_values(seeds[8], (OUTC, 3 * OUTC), OUTC ** -0.5, 0.875),
        "refine_proj": normal_values(seeds[9], (OUTC, OUTC), OUTC ** -0.5, 0.875),
        "refine_bias": draw_refine_bias(jax.random.fold_in(seeds[11], 71), 0),
    }


EPSILON = 1e-05
MASKED = -1e+30

def normalize(values):
    values = values.astype(jnp.float32)
    average = lax.optimization_barrier(jnp.mean(values, axis=-1, keepdims=True))
    centred = values - average
    spread = lax.optimization_barrier(jnp.mean(centred * centred, axis=-1, keepdims=True))
    return centred * lax.rsqrt(spread + EPSILON)

def to_windows(grid):
    leading, height, breadth, channels = grid.shape
    grid = grid.reshape(leading, height // WIN, WIN, breadth // WIN, WIN, channels)
    grid = grid.transpose(0, 1, 3, 2, 4, 5)
    return grid.reshape(leading, height // WIN * (breadth // WIN), WIN * WIN, channels)

def from_windows(windows, height, breadth):
    leading, window_count, cells, channels = windows.shape
    windows = windows.reshape(leading, height // WIN, breadth // WIN, WIN, WIN, channels)
    windows = windows.transpose(0, 1, 3, 2, 4, 5)
    return windows.reshape(leading, height, breadth, channels)

def bias_table(offset_table, variant_codes):
    position = jnp.arange(WIN * WIN, dtype=jnp.int32)
    row_step = (position // WIN)[:, None] - (position // WIN)[None, :]
    across = (position % WIN)[:, None] - (position % WIN)[None, :]
    transpose_bit = (variant_codes // 4)[:, None, None]
    flip_rows = (variant_codes // 2 % 2)[:, None, None]
    flip_cols = (variant_codes % 2)[:, None, None]
    row_moved = jnp.where(flip_rows == 1, -row_step, row_step)
    col_moved = jnp.where(flip_cols == 1, -across, across)
    leading_step = jnp.where(transpose_bit == 1, col_moved, row_moved)
    trailing_step = jnp.where(transpose_bit == 1, row_moved, col_moved)
    table_index = (leading_step + WIN - 1) * (2 * WIN - 1) + trailing_step + WIN - 1
    slots = jnp.arange((2 * WIN - 1) * (2 * WIN - 1), dtype=jnp.int32)
    one_hot = (table_index[..., None] == slots).astype(jnp.float32)
    return jnp.einsum('vqkt,ht->vhqk', one_hot, offset_table, precision=lax.Precision.HIGHEST)

def attend(normed, region, w_qkv, w_proj, bias_grid):
    head_count = bias_grid.shape[1]
    leading, window_count, cells, channels = normed.shape
    head_width = channels // head_count
    projected = jnp.einsum('lnsc,ce->lnse', normed.astype(jnp.float32), w_qkv.astype(jnp.float32)).astype(jnp.bfloat16)
    projected = projected.reshape(leading, window_count, cells, 3, head_count, head_width)
    queries = projected[:, :, :, 0].astype(jnp.float32)
    key_part = projected[:, :, :, 1].astype(jnp.float32)
    value_part = projected[:, :, :, 2]
    scores = jnp.einsum('lnqhd,lnkhd->lnhqk', queries, key_part)
    scores = scores * head_width ** (-0.5) + bias_grid[:, None]
    matches = region[:, None, :, None] == region[:, None, None, :]
    scores = jnp.where(matches[None], scores, MASKED)
    largest = lax.optimization_barrier(jnp.max(scores, axis=-1, keepdims=True))
    weights = jnp.exp(scores - largest)
    probabilities = (weights / lax.optimization_barrier(jnp.sum(weights, axis=-1, keepdims=True))).astype(jnp.bfloat16)
    value_part = jnp.broadcast_to(value_part, (probabilities.shape[0],) + value_part.shape[1:])
    mixed = jnp.einsum('lnhqk,lnkhd->lnqhd', probabilities.astype(jnp.float32), value_part.astype(jnp.float32)).astype(jnp.bfloat16)
    mixed = mixed.reshape(probabilities.shape[0], window_count, cells, channels)
    return jnp.einsum('lnsc,ce->lnse', mixed.astype(jnp.float32), w_proj.astype(jnp.float32))

def attention_half(tokens, region, w_qkv, w_proj, bias_grid):
    height, breadth = (tokens.shape[1], tokens.shape[2])
    windows = to_windows(tokens)
    region_windows = to_windows(region[None, :, :, None])[0, :, :, 0]
    normed = normalize(windows).astype(jnp.bfloat16)
    branch = attend(normed, region_windows, w_qkv, w_proj, bias_grid)
    result = (windows.astype(jnp.float32) + branch).astype(jnp.bfloat16)
    return from_windows(result, height, breadth)

def feed_forward(tokens, w_up, w_down):
    normed = normalize(tokens).astype(jnp.bfloat16)
    hidden = jnp.einsum('...c,ce->...e', normed.astype(jnp.float32), w_up.astype(jnp.float32))
    hidden = jax.nn.gelu(hidden, approximate=False).astype(jnp.bfloat16)
    output = tokens.astype(jnp.float32) + jnp.einsum('...e,ec->...c', hidden.astype(jnp.float32), w_down.astype(jnp.float32))
    return output.astype(jnp.bfloat16)

def reconstruct(padded, kernels, height, breadth):
    accumulated = jnp.zeros((padded.shape[0], height, breadth, kernels.shape[-1]), jnp.float32)
    for kernel_spot in range(9):
        spot_row, spot_col = (kernel_spot // 3, kernel_spot % 3)
        window = padded[:, spot_row:spot_row + height, spot_col:spot_col + breadth]
        accumulated = accumulated + jnp.einsum('vrcd,vde->vrce', window.astype(jnp.float32), kernels[:, kernel_spot].astype(jnp.float32))
    return accumulated

def forward(picture, transpose_bit, flip_rows, flip_cols):
    picture = jnp.where(flip_rows == 1, jnp.flip(picture, 0), picture)
    picture = jnp.where(flip_cols == 1, jnp.flip(picture, 1), picture)
    return jnp.where(transpose_bit == 1, jnp.swapaxes(picture, 0, 1), picture)

def reference(features, labels, qkv_weight, proj_weight, up_weight, down_weight, swin_bias, recon_weight, refine_qkv, refine_proj, refine_bias):
    extent = features.shape[0]
    identity = jnp.zeros((1,), jnp.int32)
    first_bias = bias_table(swin_bias[0], identity)
    second_bias = bias_table(swin_bias[1], identity)

    def one_variant(accumulated, variant_code):
        transpose_bit = variant_code // 4
        flip_rows = variant_code // 2 % 2
        flip_cols = variant_code % 2
        picture = forward(features, transpose_bit, flip_rows, flip_cols)
        region = forward(labels, transpose_bit, flip_rows, flip_cols)
        block_one = attention_half(picture[None], region, qkv_weight[0], proj_weight[0], first_bias)
        block_one = feed_forward(block_one, up_weight[0], down_weight[0])
        padded = jnp.pad(block_one, ((0, 0), (SHIFT, SHIFT), (SHIFT, SHIFT), (0, 0)))
        padded_region = jnp.pad(region, SHIFT)
        block_two = attention_half(padded, padded_region, qkv_weight[1], proj_weight[1], second_bias)
        block_two = feed_forward(block_two[:, SHIFT:-SHIFT, SHIFT:-SHIFT], up_weight[1], down_weight[1])
        bordered = jnp.pad(block_two, ((0, 0), (1, 1), (1, 1), (0, 0)))
        convolved = reconstruct(bordered, recon_weight[None], extent, extent)[0]
        upscaled = convolved.reshape(extent, extent, 3, SCALE, SCALE).transpose(2, 0, 3, 1, 4)
        upscaled = upscaled.reshape(3, SCALE * extent, SCALE * extent)
        upscaled = jnp.where(transpose_bit == 1, jnp.swapaxes(upscaled, 1, 2), upscaled)
        upscaled = jnp.where(flip_rows == 1, jnp.flip(upscaled, 1), upscaled)
        upscaled = jnp.where(flip_cols == 1, jnp.flip(upscaled, 2), upscaled)
        return (accumulated + upscaled, variant_code)
    start_sum = jnp.zeros((3, SCALE * extent, SCALE * extent), jnp.float32)
    accumulated, leftover = lax.scan(one_variant, start_sum, jnp.arange(8, dtype=jnp.int32))
    average = accumulated / 8.0
    grid = average.reshape(3, extent, SCALE, extent, SCALE).transpose(1, 3, 0, 2, 4)
    grid = grid.reshape(extent, extent, 3 * SCALE * SCALE)
    windows = to_windows(grid[None])
    region_windows = to_windows(labels[None, :, :, None])[0, :, :, 0]
    normed = normalize(windows).astype(jnp.bfloat16)
    refine_grid = bias_table(refine_bias, identity)
    refined = windows + attend(normed, region_windows, refine_qkv, refine_proj, refine_grid)
    refined = from_windows(refined, extent, extent)[0]
    picture = refined.reshape(extent, extent, 3, SCALE, SCALE).transpose(2, 0, 3, 1, 4)
    return picture.reshape(3, SCALE * extent, SCALE * extent)
```

```python
import functools

import jax
import jax.numpy as jnp
from jax import lax
from jax.experimental import pallas as pl
from jax.experimental.pallas import tpu as pltpu
from jax.sharding import PartitionSpec as P

MESH = pl.DeviceIdType.MESH

WIN = 8
SHIFT = 4
SCALE = 4
VAR_DEV = 2


EPSILON = 1e-05
MASKED = -1e30


def extended(cells, sides, width):
    for axis, dim in sides:
        count = lax.axis_size(axis)
        ends = count - 1
        head = lax.slice_in_dim(cells, 0, width, axis=dim)
        tail = lax.slice_in_dim(cells, cells.shape[dim] - width, cells.shape[dim], axis=dim)
        cells = jnp.concatenate(
            [
                lax.ppermute(tail, axis, [(i, (i + 1) % count) for i in range(ends)]),
                cells,
                lax.ppermute(head, axis, [((i + 1) % count, i) for i in range(ends)]),
            ],
            axis=dim,
        )
    return cells


def var_sum_kernel(count, part_ref, out_ref, held, send_sem, recv_sem, own_sem):
    me = lax.axis_index("var")
    barrier = pltpu.get_barrier_semaphore()
    for step in range(1, count):
        peer = lax.rem(me + step, count)
        pl.semaphore_signal(barrier, inc=1, device_id={"var": peer}, device_id_type=MESH)
    pl.semaphore_wait(barrier, count - 1)
    own = pltpu.make_async_copy(part_ref, held.at[me], own_sem)
    own.start()
    sends = []
    for step in range(1, count):
        peer = lax.rem(me + step, count)
        copy = pltpu.make_async_remote_copy(
            src_ref=part_ref,
            dst_ref=held.at[me],
            send_sem=send_sem.at[step - 1],
            recv_sem=recv_sem.at[me],
            device_id={"var": peer},
            device_id_type=MESH,
        )
        copy.start()
        sends.append(copy)
    own.wait()
    for copy in sends:
        copy.wait_send()
    for step in range(1, count):
        source = lax.rem(me + count - step, count)
        pltpu.make_async_remote_copy(
            src_ref=part_ref,
            dst_ref=held.at[source],
            send_sem=send_sem.at[step - 1],
            recv_sem=recv_sem.at[source],
            device_id={"var": source},
            device_id_type=MESH,
        ).wait_recv()
    total = held[0].astype(jnp.float32)
    for index in range(1, count):
        total = total + held[index].astype(jnp.float32)
    out_ref[...] = total


def var_sum(part):
    count = lax.axis_size("var")
    return pl.pallas_call(
        functools.partial(var_sum_kernel, count),
        out_shape=jax.ShapeDtypeStruct(part.shape, jnp.float32),
        in_specs=[pl.BlockSpec(memory_space=pltpu.VMEM)],
        out_specs=pl.BlockSpec(memory_space=pltpu.VMEM),
        scratch_shapes=[
            pltpu.VMEM((count,) + part.shape, part.dtype),
            pltpu.SemaphoreType.DMA((count - 1,)),
            pltpu.SemaphoreType.DMA((count,)),
            pltpu.SemaphoreType.DMA(()),
        ],
        compiler_params=pltpu.CompilerParams(collective_id=0, has_side_effects=True),
    )(part)


def normalize(values):
    values = values.astype(jnp.float32)
    average = jnp.mean(values, axis=-1, keepdims=True)
    centred = values - average
    spread = jnp.mean(centred * centred, axis=-1, keepdims=True)
    return centred * lax.rsqrt(spread + EPSILON)


def to_windows(grid):
    leading, height, breadth, channels = grid.shape
    grid = grid.reshape(leading, height // WIN, WIN, breadth // WIN, WIN, channels)
    grid = grid.transpose(0, 1, 3, 2, 4, 5)
    return grid.reshape(leading, height // WIN * (breadth // WIN), WIN * WIN, channels)


def from_windows(windows, height, breadth):
    leading, window_count, cells, channels = windows.shape
    windows = windows.reshape(leading, height // WIN, breadth // WIN, WIN, WIN, channels)
    windows = windows.transpose(0, 1, 3, 2, 4, 5)
    return windows.reshape(leading, height, breadth, channels)


def bias_table(offset_table, variant_codes):
    position = jnp.arange(WIN * WIN, dtype=jnp.int32)
    row_step = (position // WIN)[:, None] - (position // WIN)[None, :]
    across = (position % WIN)[:, None] - (position % WIN)[None, :]
    transpose_bit = (variant_codes // 4)[:, None, None]
    flip_rows = (variant_codes // 2 % 2)[:, None, None]
    flip_cols = (variant_codes % 2)[:, None, None]
    row_moved = jnp.where(flip_rows == 1, -row_step, row_step)
    col_moved = jnp.where(flip_cols == 1, -across, across)
    leading_step = jnp.where(transpose_bit == 1, col_moved, row_moved)
    trailing_step = jnp.where(transpose_bit == 1, row_moved, col_moved)
    table_index = (leading_step + WIN - 1) * (2 * WIN - 1) + trailing_step + WIN - 1
    slots = jnp.arange((2 * WIN - 1) * (2 * WIN - 1), dtype=jnp.int32)
    one_hot = (table_index[..., None] == slots).astype(jnp.float32)
    return jnp.einsum("vqkt,ht->vhqk", one_hot, offset_table, precision=lax.Precision.HIGHEST)


def variant_kernels(kernel, variant_codes):
    transpose_bit = (variant_codes // 4)[:, None]
    flip_rows = (variant_codes // 2 % 2)[:, None]
    flip_cols = (variant_codes % 2)[:, None]
    kernel_spot = jnp.arange(9, dtype=jnp.int32)
    step_row = (kernel_spot // 3 - 1)[None, :]
    step_col = (kernel_spot % 3 - 1)[None, :]
    row_moved = jnp.where(flip_rows == 1, -step_row, step_row)
    col_moved = jnp.where(flip_cols == 1, -step_col, step_col)
    source_row = jnp.where(transpose_bit == 1, col_moved, row_moved)
    source_col = jnp.where(transpose_bit == 1, row_moved, col_moved)
    source = (source_row + 1) * 3 + source_col + 1
    pick_place = (source[:, :, None] == kernel_spot[None, None, :]).astype(jnp.bfloat16)
    channel = jnp.arange(kernel.shape[-1], dtype=jnp.int32)
    colour = (channel // (SCALE * SCALE))[None, :]
    sub_row = (channel % (SCALE * SCALE) // SCALE)[None, :]
    sub_col = (channel % SCALE)[None, :]
    sub_row_moved = jnp.where(flip_rows == 1, SCALE - 1 - sub_row, sub_row)
    sub_col_moved = jnp.where(flip_cols == 1, SCALE - 1 - sub_col, sub_col)
    anchor_row = jnp.where(transpose_bit == 1, sub_col_moved, sub_row_moved)
    anchor_col = jnp.where(transpose_bit == 1, sub_row_moved, sub_col_moved)
    anchor = colour * SCALE * SCALE + anchor_row * SCALE + anchor_col
    pick_channel = (channel[None, :, None] == anchor[:, None, :]).astype(jnp.bfloat16)
    placed = jnp.einsum(
        "vpq,qcs->vpcs", pick_place, kernel, preferred_element_type=jnp.float32
    ).astype(jnp.bfloat16)
    return jnp.einsum(
        "vpcs,vso->vpco", placed, pick_channel, preferred_element_type=jnp.float32
    ).astype(jnp.bfloat16)


def attend(normed, region, w_qkv, w_proj, bias_grid):
    head_count = bias_grid.shape[1]
    leading, window_count, cells, channels = normed.shape
    head_width = channels // head_count
    projected = jnp.einsum(
        "lnsc,ce->lnse", normed, w_qkv, preferred_element_type=jnp.float32
    ).astype(jnp.bfloat16)
    projected = projected.reshape(leading, window_count, cells, 3, head_count, head_width)
    queries = projected[:, :, :, 0]
    key_part = projected[:, :, :, 1]
    value_part = projected[:, :, :, 2]
    scores = jnp.einsum("lnqhd,lnkhd->lnhqk", queries, key_part, preferred_element_type=jnp.float32)
    scores = scores * head_width ** (-0.5) + bias_grid[:, None]
    matches = region[:, None, :, None] == region[:, None, None, :]
    scores = jnp.where(matches[None], scores, MASKED)
    largest = jnp.max(scores, axis=-1, keepdims=True)
    weights = jnp.exp(scores - largest)
    probabilities = (weights / jnp.sum(weights, axis=-1, keepdims=True)).astype(jnp.bfloat16)
    value_part = jnp.broadcast_to(value_part, (probabilities.shape[0],) + value_part.shape[1:])
    mixed = jnp.einsum(
        "lnhqk,lnkhd->lnqhd", probabilities, value_part, preferred_element_type=jnp.float32
    ).astype(jnp.bfloat16)
    mixed = mixed.reshape(probabilities.shape[0], window_count, cells, channels)
    return jnp.einsum("lnsc,ce->lnse", mixed, w_proj, preferred_element_type=jnp.float32)


def attention_half(tokens, region, w_qkv, w_proj, bias_grid):
    height, breadth = (tokens.shape[1], tokens.shape[2])
    windows = to_windows(tokens)
    region_windows = to_windows(region[None, :, :, None])[0, :, :, 0]
    normed = normalize(windows).astype(jnp.bfloat16)
    branch = attend(normed, region_windows, w_qkv, w_proj, bias_grid)
    result = (windows.astype(jnp.float32) + branch).astype(jnp.bfloat16)
    return from_windows(result, height, breadth)


def feed_forward(tokens, w_up, w_down):
    normed = normalize(tokens).astype(jnp.bfloat16)
    hidden = jnp.einsum("...c,ce->...e", normed, w_up, preferred_element_type=jnp.float32)
    hidden = jax.nn.gelu(hidden, approximate=False).astype(jnp.bfloat16)
    output = tokens.astype(jnp.float32) + jnp.einsum(
        "...e,ec->...c", hidden, w_down, preferred_element_type=jnp.float32
    )
    return output.astype(jnp.bfloat16)


def reconstruct(padded, kernels, height, breadth):
    accumulated = jnp.zeros((padded.shape[0], height, breadth, kernels.shape[-1]), jnp.float32)
    for kernel_spot in range(9):
        spot_row, spot_col = (kernel_spot // 3, kernel_spot % 3)
        window = padded[:, spot_row : spot_row + height, spot_col : spot_col + breadth]
        accumulated = accumulated + jnp.einsum(
            "vrcd,vde->vrce", window, kernels[:, kernel_spot], preferred_element_type=jnp.float32
        )
    return accumulated


def refine(average, region, w_qkv, w_proj, bias_grid):
    normed = normalize(average).astype(jnp.bfloat16)[None]
    return average + attend(normed, region, w_qkv, w_proj, bias_grid)[0]


def local(
    features,
    labels,
    qkv_weight,
    proj_weight,
    up_weight,
    down_weight,
    swin_bias,
    recon_weight,
    refine_qkv,
    refine_proj,
    refine_bias,
):
    height, breadth, channels = features.shape
    variant_codes = lax.axis_index("var") * VAR_DEV + jnp.arange(VAR_DEV, dtype=jnp.int32)
    first_bias = bias_table(swin_bias[0], variant_codes)
    second_bias = bias_table(swin_bias[1], variant_codes)
    region = extended(labels, (("ty", 0), ("tx", 1)), SHIFT)
    block_one = attention_half(features[None], labels, qkv_weight[0], proj_weight[0], first_bias)
    block_one = feed_forward(block_one, up_weight[0], down_weight[0])
    shifted = extended(block_one, (("ty", 1), ("tx", 2)), SHIFT)
    block_two = attention_half(shifted, region, qkv_weight[1], proj_weight[1], second_bias)
    own_tile = feed_forward(block_two[:, SHIFT:-SHIFT, SHIFT:-SHIFT], up_weight[1], down_weight[1])
    padded = extended(own_tile, (("ty", 1), ("tx", 2)), 1)
    kernels = variant_kernels(recon_weight, variant_codes)
    summed = jnp.sum(reconstruct(padded, kernels, height, breadth), axis=0)
    region_windows = to_windows(labels[None, :, :, None])[0, :, :, 0]
    refine_grid = bias_table(refine_bias, jnp.zeros((1,), jnp.int32))
    rows, cols, depth = summed.shape
    combined = var_sum(summed.astype(jnp.bfloat16).reshape(rows * cols, depth)).reshape(rows, cols, depth)
    refined = refine(
        to_windows(combined[None])[0] / 8.0, region_windows, refine_qkv, refine_proj, refine_grid
    )
    refined_grid = from_windows(refined[None], height, breadth)[0]
    picture = refined_grid.reshape(height, breadth, 3, SCALE, SCALE).transpose(2, 0, 3, 1, 4)
    return picture.reshape(3, SCALE * height, SCALE * breadth)


def solution(mesh):
    placed = (P("ty", "tx", None), P("ty", "tx"), P(), P(), P(), P(), P(), P(), P(), P(), P())
    return jax.shard_map(
        local, mesh=mesh, in_specs=placed, out_specs=P(None, "ty", "tx"), check_vma=False
    )
```

```python
import functools

import jax
import jax.numpy as jnp
from jax import lax
from jax.experimental import pallas as pl
from jax.experimental.pallas import tpu as pltpu
from jax.sharding import PartitionSpec as P

MESH = pl.DeviceIdType.MESH

WIN = 8
SHIFT = 4
SCALE = 4
VAR_DEV = 2


EPSILON = 1e-05
MASKED = -1e30


def extended(cells, sides, width):
    for axis, dim in sides:
        count = lax.axis_size(axis)
        ends = count - 1
        head = lax.slice_in_dim(cells, 0, width, axis=dim)
        tail = lax.slice_in_dim(cells, cells.shape[dim] - width, cells.shape[dim], axis=dim)
        cells = jnp.concatenate(
            [
                lax.ppermute(tail, axis, [(i, (i + 1) % count) for i in range(ends)]),
                cells,
                lax.ppermute(head, axis, [((i + 1) % count, i) for i in range(ends)]),
            ],
            axis=dim,
        )
    return cells


def var_sum_kernel(count, part_ref, out_ref, held, send_sem, recv_sem, own_sem):
    me = lax.axis_index("var")
    barrier = pltpu.get_barrier_semaphore()
    for step in range(1, count):
        peer = lax.rem(me + step, count)
        pl.semaphore_signal(barrier, inc=1, device_id={"var": peer}, device_id_type=MESH)
    pl.semaphore_wait(barrier, count - 1)
    own = pltpu.make_async_copy(part_ref, held.at[me], own_sem)
    own.start()
    sends = []
    for step in range(1, count):
        peer = lax.rem(me + step, count)
        copy = pltpu.make_async_remote_copy(
            src_ref=part_ref,
            dst_ref=held.at[me],
            send_sem=send_sem.at[step - 1],
            recv_sem=recv_sem.at[me],
            device_id={"var": peer},
            device_id_type=MESH,
        )
        copy.start()
        sends.append(copy)
    own.wait()
    for copy in sends:
        copy.wait_send()
    for step in range(1, count):
        source = lax.rem(me + count - step, count)
        pltpu.make_async_remote_copy(
            src_ref=part_ref,
            dst_ref=held.at[source],
            send_sem=send_sem.at[step - 1],
            recv_sem=recv_sem.at[source],
            device_id={"var": source},
            device_id_type=MESH,
        ).wait_recv()
    total = held[0].astype(jnp.float32)
    for index in range(1, count):
        total = total + held[index].astype(jnp.float32)
    out_ref[...] = total


def var_sum(part):
    count = lax.axis_size("var")
    return pl.pallas_call(
        functools.partial(var_sum_kernel, count),
        out_shape=jax.ShapeDtypeStruct(part.shape, jnp.float32),
        in_specs=[pl.BlockSpec(memory_space=pltpu.VMEM)],
        out_specs=pl.BlockSpec(memory_space=pltpu.VMEM),
        scratch_shapes=[
            pltpu.VMEM((count,) + part.shape, part.dtype),
            pltpu.SemaphoreType.DMA((count - 1,)),
            pltpu.SemaphoreType.DMA((count,)),
            pltpu.SemaphoreType.DMA(()),
        ],
        compiler_params=pltpu.CompilerParams(collective_id=0, has_side_effects=True),
    )(part)


GROUP = 4
LANE = 128


def block_kernel(
    variants, heads, scale, x_ref, labq_ref, labk_ref, bias_ref, wqkv_ref, wp_ref, wup_ref, wdown_ref, out_ref
):
    inputs = x_ref.shape[0]
    tokens = x_ref.shape[2]
    labq = labq_ref[0]
    labk = labk_ref[0]
    slot_q = lax.broadcasted_iota(jnp.int32, (tokens, tokens), 0) // (WIN * WIN)
    slot_k = lax.broadcasted_iota(jnp.int32, (tokens, tokens), 1) // (WIN * WIN)
    match = (labq == labk) & (slot_q == slot_k)
    projected = []
    for index in range(inputs):
        normed = normalize(x_ref[index, 0]).astype(jnp.bfloat16)
        projected.append(
            jnp.dot(normed, wqkv_ref[...], preferred_element_type=jnp.float32).astype(jnp.bfloat16)
        )
    for variant in range(variants):
        source = variant if inputs > 1 else 0
        qkv = projected[source]
        mixed = []
        for head in range(heads):
            base = head * 3 * LANE
            query = qkv[:, base : base + LANE]
            key = qkv[:, base + LANE : base + 2 * LANE]
            value = qkv[:, base + 2 * LANE : base + 3 * LANE]
            scores = lax.dot_general(
                query, key, (((1,), (1,)), ((), ())), preferred_element_type=jnp.float32
            )
            scores = scores * scale + bias_ref[variant, head]
            scores = jnp.where(match, scores, MASKED)
            largest = jnp.max(scores, axis=-1, keepdims=True)
            weights = jnp.exp(scores - largest)
            probabilities = (weights / jnp.sum(weights, axis=-1, keepdims=True)).astype(jnp.bfloat16)
            mixed.append(
                jnp.dot(probabilities, value, preferred_element_type=jnp.float32).astype(jnp.bfloat16)
            )
        mixed = jnp.concatenate(mixed, axis=-1)
        branch = jnp.dot(mixed, wp_ref[...], preferred_element_type=jnp.float32)
        own = x_ref[source, 0].astype(jnp.float32)
        hidden_in = (own + branch).astype(jnp.bfloat16)
        normed = normalize(hidden_in).astype(jnp.bfloat16)
        hidden = jnp.dot(normed, wup_ref[...], preferred_element_type=jnp.float32)
        hidden = (0.5 * hidden * (1.0 + lax.erf(hidden * (2.0 ** -0.5)))).astype(jnp.bfloat16)
        result = hidden_in.astype(jnp.float32) + jnp.dot(
            hidden, wdown_ref[...], preferred_element_type=jnp.float32
        )
        out_ref[variant, 0] = result.astype(jnp.bfloat16)


def padded_weights(w_qkv, w_proj, heads):
    channels = w_proj.shape[0]
    width = channels // heads
    columns = []
    for head in range(heads):
        for part in range(3):
            start = part * channels + head * width
            columns.append(jnp.pad(w_qkv[:, start : start + width], ((0, 0), (0, LANE - width))))
    rows = [
        jnp.pad(w_proj[head * width : (head + 1) * width], ((0, LANE - width), (0, 0)))
        for head in range(heads)
    ]
    return jnp.concatenate(columns, axis=1), jnp.concatenate(rows, axis=0)


def swin_block(windows, region, w_qkv, w_proj, w_up, w_down, bias_grid):
    inputs, count, cells, channels = windows.shape
    variants, heads = bias_grid.shape[:2]
    groups = -(-count // GROUP)
    extra = groups * GROUP - count
    windows = jnp.pad(windows, ((0, 0), (0, extra), (0, 0), (0, 0)))
    region = jnp.pad(region, ((0, extra), (0, 0)))
    tokens = GROUP * cells
    x = windows.reshape(inputs, groups, tokens, channels)
    labq = region.reshape(groups, tokens, 1)
    labk = region.reshape(groups, 1, tokens)
    bias = jnp.tile(bias_grid, (1, 1, GROUP, GROUP))
    wqkv, wp = padded_weights(w_qkv, w_proj, heads)
    scale = (channels // heads) ** (-0.5)
    whole = lambda shape: pl.BlockSpec(shape, lambda g: (0,) * len(shape))
    out = pl.pallas_call(
        functools.partial(block_kernel, variants, heads, scale),
        out_shape=jax.ShapeDtypeStruct((variants, groups, tokens, channels), jnp.bfloat16),
        grid=(groups,),
        in_specs=[
            pl.BlockSpec((inputs, 1, tokens, channels), lambda g: (0, g, 0, 0)),
            pl.BlockSpec((1, tokens, 1), lambda g: (g, 0, 0)),
            pl.BlockSpec((1, 1, tokens), lambda g: (g, 0, 0)),
            whole(bias.shape),
            whole(wqkv.shape),
            whole(wp.shape),
            whole(w_up.shape),
            whole(w_down.shape),
        ],
        out_specs=pl.BlockSpec((variants, 1, tokens, channels), lambda g: (0, g, 0, 0)),
        compiler_params=pltpu.CompilerParams(vmem_limit_bytes=48 * 1024 * 1024),
    )(x, labq, labk, bias, wqkv, wp, w_up, w_down)
    out = out.reshape(variants, groups * GROUP, cells, channels)
    return out[:, :count]


def block_on_grid(tokens, region, w_qkv, w_proj, w_up, w_down, bias_grid):
    height, breadth = tokens.shape[1], tokens.shape[2]
    windows = to_windows(tokens)
    region_windows = to_windows(region[None, :, :, None])[0, :, :, 0]
    out = swin_block(windows, region_windows, w_qkv, w_proj, w_up, w_down, bias_grid)
    return from_windows(out, height, breadth)


def normalize(values):
    values = values.astype(jnp.float32)
    average = jnp.mean(values, axis=-1, keepdims=True)
    centred = values - average
    spread = jnp.mean(centred * centred, axis=-1, keepdims=True)
    return centred * lax.rsqrt(spread + EPSILON)


def to_windows(grid):
    leading, height, breadth, channels = grid.shape
    grid = grid.reshape(leading, height // WIN, WIN, breadth // WIN, WIN, channels)
    grid = grid.transpose(0, 1, 3, 2, 4, 5)
    return grid.reshape(leading, height // WIN * (breadth // WIN), WIN * WIN, channels)


def from_windows(windows, height, breadth):
    leading, window_count, cells, channels = windows.shape
    windows = windows.reshape(leading, height // WIN, breadth // WIN, WIN, WIN, channels)
    windows = windows.transpose(0, 1, 3, 2, 4, 5)
    return windows.reshape(leading, height, breadth, channels)


def bias_table(offset_table, variant_codes):
    position = jnp.arange(WIN * WIN, dtype=jnp.int32)
    row_step = (position // WIN)[:, None] - (position // WIN)[None, :]
    across = (position % WIN)[:, None] - (position % WIN)[None, :]
    transpose_bit = (variant_codes // 4)[:, None, None]
    flip_rows = (variant_codes // 2 % 2)[:, None, None]
    flip_cols = (variant_codes % 2)[:, None, None]
    row_moved = jnp.where(flip_rows == 1, -row_step, row_step)
    col_moved = jnp.where(flip_cols == 1, -across, across)
    leading_step = jnp.where(transpose_bit == 1, col_moved, row_moved)
    trailing_step = jnp.where(transpose_bit == 1, row_moved, col_moved)
    table_index = (leading_step + WIN - 1) * (2 * WIN - 1) + trailing_step + WIN - 1
    slots = jnp.arange((2 * WIN - 1) * (2 * WIN - 1), dtype=jnp.int32)
    one_hot = (table_index[..., None] == slots).astype(jnp.float32)
    return jnp.einsum("vqkt,ht->vhqk", one_hot, offset_table, precision=lax.Precision.HIGHEST)


def variant_kernels(kernel, variant_codes):
    transpose_bit = (variant_codes // 4)[:, None]
    flip_rows = (variant_codes // 2 % 2)[:, None]
    flip_cols = (variant_codes % 2)[:, None]
    kernel_spot = jnp.arange(9, dtype=jnp.int32)
    step_row = (kernel_spot // 3 - 1)[None, :]
    step_col = (kernel_spot % 3 - 1)[None, :]
    row_moved = jnp.where(flip_rows == 1, -step_row, step_row)
    col_moved = jnp.where(flip_cols == 1, -step_col, step_col)
    source_row = jnp.where(transpose_bit == 1, col_moved, row_moved)
    source_col = jnp.where(transpose_bit == 1, row_moved, col_moved)
    source = (source_row + 1) * 3 + source_col + 1
    pick_place = (source[:, :, None] == kernel_spot[None, None, :]).astype(jnp.bfloat16)
    channel = jnp.arange(kernel.shape[-1], dtype=jnp.int32)
    colour = (channel // (SCALE * SCALE))[None, :]
    sub_row = (channel % (SCALE * SCALE) // SCALE)[None, :]
    sub_col = (channel % SCALE)[None, :]
    sub_row_moved = jnp.where(flip_rows == 1, SCALE - 1 - sub_row, sub_row)
    sub_col_moved = jnp.where(flip_cols == 1, SCALE - 1 - sub_col, sub_col)
    anchor_row = jnp.where(transpose_bit == 1, sub_col_moved, sub_row_moved)
    anchor_col = jnp.where(transpose_bit == 1, sub_row_moved, sub_col_moved)
    anchor = colour * SCALE * SCALE + anchor_row * SCALE + anchor_col
    pick_channel = (channel[None, :, None] == anchor[:, None, :]).astype(jnp.bfloat16)
    placed = jnp.einsum(
        "vpq,qcs->vpcs", pick_place, kernel, preferred_element_type=jnp.float32
    ).astype(jnp.bfloat16)
    return jnp.einsum(
        "vpcs,vso->vpco", placed, pick_channel, preferred_element_type=jnp.float32
    ).astype(jnp.bfloat16)


def attend(normed, region, w_qkv, w_proj, bias_grid):
    head_count = bias_grid.shape[1]
    leading, window_count, cells, channels = normed.shape
    head_width = channels // head_count
    projected = jnp.einsum(
        "lnsc,ce->lnse", normed, w_qkv, preferred_element_type=jnp.float32
    ).astype(jnp.bfloat16)
    projected = projected.reshape(leading, window_count, cells, 3, head_count, head_width)
    queries = projected[:, :, :, 0]
    key_part = projected[:, :, :, 1]
    value_part = projected[:, :, :, 2]
    scores = jnp.einsum("lnqhd,lnkhd->lnhqk", queries, key_part, preferred_element_type=jnp.float32)
    scores = scores * head_width ** (-0.5) + bias_grid[:, None]
    matches = region[:, None, :, None] == region[:, None, None, :]
    scores = jnp.where(matches[None], scores, MASKED)
    largest = jnp.max(scores, axis=-1, keepdims=True)
    weights = jnp.exp(scores - largest)
    probabilities = (weights / jnp.sum(weights, axis=-1, keepdims=True)).astype(jnp.bfloat16)
    value_part = jnp.broadcast_to(value_part, (probabilities.shape[0],) + value_part.shape[1:])
    mixed = jnp.einsum(
        "lnhqk,lnkhd->lnqhd", probabilities, value_part, preferred_element_type=jnp.float32
    ).astype(jnp.bfloat16)
    mixed = mixed.reshape(probabilities.shape[0], window_count, cells, channels)
    return jnp.einsum("lnsc,ce->lnse", mixed, w_proj, preferred_element_type=jnp.float32)


def attention_half(tokens, region, w_qkv, w_proj, bias_grid):
    height, breadth = (tokens.shape[1], tokens.shape[2])
    windows = to_windows(tokens)
    region_windows = to_windows(region[None, :, :, None])[0, :, :, 0]
    normed = normalize(windows).astype(jnp.bfloat16)
    branch = attend(normed, region_windows, w_qkv, w_proj, bias_grid)
    result = (windows.astype(jnp.float32) + branch).astype(jnp.bfloat16)
    return from_windows(result, height, breadth)


def feed_forward(tokens, w_up, w_down):
    normed = normalize(tokens).astype(jnp.bfloat16)
    hidden = jnp.einsum("...c,ce->...e", normed, w_up, preferred_element_type=jnp.float32)
    hidden = jax.nn.gelu(hidden, approximate=False).astype(jnp.bfloat16)
    output = tokens.astype(jnp.float32) + jnp.einsum(
        "...e,ec->...c", hidden, w_down, preferred_element_type=jnp.float32
    )
    return output.astype(jnp.bfloat16)


def reconstruct(padded, kernels, height, breadth):
    accumulated = jnp.zeros((padded.shape[0], height, breadth, kernels.shape[-1]), jnp.float32)
    for kernel_spot in range(9):
        spot_row, spot_col = (kernel_spot // 3, kernel_spot % 3)
        window = padded[:, spot_row : spot_row + height, spot_col : spot_col + breadth]
        accumulated = accumulated + jnp.einsum(
            "vrcd,vde->vrce", window, kernels[:, kernel_spot], preferred_element_type=jnp.float32
        )
    return accumulated


def refine(average, region, w_qkv, w_proj, bias_grid):
    normed = normalize(average).astype(jnp.bfloat16)[None]
    return average + attend(normed, region, w_qkv, w_proj, bias_grid)[0]


def local(
    features,
    labels,
    qkv_weight,
    proj_weight,
    up_weight,
    down_weight,
    swin_bias,
    recon_weight,
    refine_qkv,
    refine_proj,
    refine_bias,
):
    height, breadth, channels = features.shape
    variant_codes = lax.axis_index("var") * VAR_DEV + jnp.arange(VAR_DEV, dtype=jnp.int32)
    first_bias = bias_table(swin_bias[0], variant_codes)
    second_bias = bias_table(swin_bias[1], variant_codes)
    region = extended(labels, (("ty", 0), ("tx", 1)), SHIFT)
    block_one = block_on_grid(
        features[None], labels, qkv_weight[0], proj_weight[0], up_weight[0], down_weight[0], first_bias
    )
    shifted = extended(block_one, (("ty", 1), ("tx", 2)), SHIFT)
    block_two = block_on_grid(
        shifted, region, qkv_weight[1], proj_weight[1], up_weight[1], down_weight[1], second_bias
    )
    own_tile = block_two[:, SHIFT:-SHIFT, SHIFT:-SHIFT]
    padded = extended(own_tile, (("ty", 1), ("tx", 2)), 1)
    kernels = variant_kernels(recon_weight, variant_codes)
    summed = jnp.sum(reconstruct(padded, kernels, height, breadth), axis=0)
    region_windows = to_windows(labels[None, :, :, None])[0, :, :, 0]
    refine_grid = bias_table(refine_bias, jnp.zeros((1,), jnp.int32))
    rows, cols, depth = summed.shape
    combined = var_sum(summed.astype(jnp.bfloat16).reshape(rows * cols, depth)).reshape(rows, cols, depth)
    refined = refine(
        to_windows(combined[None])[0] / 8.0, region_windows, refine_qkv, refine_proj, refine_grid
    )
    refined_grid = from_windows(refined[None], height, breadth)[0]
    picture = refined_grid.reshape(height, breadth, 3, SCALE, SCALE).transpose(2, 0, 3, 1, 4)
    return picture.reshape(3, SCALE * height, SCALE * breadth)


def solution(mesh):
    placed = (P("ty", "tx", None), P("ty", "tx"), P(), P(), P(), P(), P(), P(), P(), P(), P())
    return jax.shard_map(
        local, mesh=mesh, in_specs=placed, out_specs=P(None, "ty", "tx"), check_vma=False
    )
```

```python
import functools

import jax
import jax.numpy as jnp
from jax import lax
from jax.experimental import pallas as pl
from jax.experimental.pallas import tpu as pltpu
from jax.sharding import PartitionSpec as P

MESH = pl.DeviceIdType.MESH

WIN = 8
SHIFT = 4
SCALE = 4
VAR_DEV = 2


EPSILON = 1e-05
MASKED = -1e30


def extended(cells, sides, width):
    for axis, dim in sides:
        count = lax.axis_size(axis)
        ends = count - 1
        head = lax.slice_in_dim(cells, 0, width, axis=dim)
        tail = lax.slice_in_dim(cells, cells.shape[dim] - width, cells.shape[dim], axis=dim)
        cells = jnp.concatenate(
            [
                lax.ppermute(tail, axis, [(i, (i + 1) % count) for i in range(ends)]),
                cells,
                lax.ppermute(head, axis, [((i + 1) % count, i) for i in range(ends)]),
            ],
            axis=dim,
        )
    return cells


def var_sum_kernel(count, part_ref, out_ref, held, send_sem, recv_sem, own_sem):
    me = lax.axis_index("var")
    barrier = pltpu.get_barrier_semaphore()
    for step in range(1, count):
        peer = lax.rem(me + step, count)
        pl.semaphore_signal(barrier, inc=1, device_id={"var": peer}, device_id_type=MESH)
    pl.semaphore_wait(barrier, count - 1)
    own = pltpu.make_async_copy(part_ref, held.at[me], own_sem)
    own.start()
    sends = []
    for step in range(1, count):
        peer = lax.rem(me + step, count)
        copy = pltpu.make_async_remote_copy(
            src_ref=part_ref,
            dst_ref=held.at[me],
            send_sem=send_sem.at[step - 1],
            recv_sem=recv_sem.at[me],
            device_id={"var": peer},
            device_id_type=MESH,
        )
        copy.start()
        sends.append(copy)
    own.wait()
    for copy in sends:
        copy.wait_send()
    for step in range(1, count):
        source = lax.rem(me + count - step, count)
        pltpu.make_async_remote_copy(
            src_ref=part_ref,
            dst_ref=held.at[source],
            send_sem=send_sem.at[step - 1],
            recv_sem=recv_sem.at[source],
            device_id={"var": source},
            device_id_type=MESH,
        ).wait_recv()
    total = held[0].astype(jnp.float32)
    for index in range(1, count):
        total = total + held[index].astype(jnp.float32)
    out_ref[...] = total


def var_sum(part):
    count = lax.axis_size("var")
    return pl.pallas_call(
        functools.partial(var_sum_kernel, count),
        out_shape=jax.ShapeDtypeStruct(part.shape, jnp.float32),
        in_specs=[pl.BlockSpec(memory_space=pltpu.VMEM)],
        out_specs=pl.BlockSpec(memory_space=pltpu.VMEM),
        scratch_shapes=[
            pltpu.VMEM((count,) + part.shape, part.dtype),
            pltpu.SemaphoreType.DMA((count - 1,)),
            pltpu.SemaphoreType.DMA((count,)),
            pltpu.SemaphoreType.DMA(()),
        ],
        compiler_params=pltpu.CompilerParams(collective_id=0, has_side_effects=True),
    )(part)


GROUP = 2
LANE = 128


def block_kernel(
    variants, heads, scale, x_ref, labq_ref, labk_ref, bias_ref, wqkv_ref, wp_ref, wup_ref, wdown_ref, out_ref
):
    inputs = x_ref.shape[0]
    tokens = x_ref.shape[2]
    labq = labq_ref[0]
    labk = labk_ref[0]
    slot_q = lax.broadcasted_iota(jnp.int32, (tokens, tokens), 0) // (WIN * WIN)
    slot_k = lax.broadcasted_iota(jnp.int32, (tokens, tokens), 1) // (WIN * WIN)
    match = (labq == labk) & (slot_q == slot_k)
    projected = []
    for index in range(inputs):
        normed = normalize(x_ref[index, 0]).astype(jnp.bfloat16)
        projected.append(
            jnp.dot(normed, wqkv_ref[...], preferred_element_type=jnp.float32).astype(jnp.bfloat16)
        )
    for variant in range(variants):
        source = variant if inputs > 1 else 0
        qkv = projected[source]
        mixed = []
        for head in range(heads):
            base = head * 3 * LANE
            query = qkv[:, base : base + LANE]
            key = qkv[:, base + LANE : base + 2 * LANE]
            value = qkv[:, base + 2 * LANE : base + 3 * LANE]
            scores = lax.dot_general(
                query, key, (((1,), (1,)), ((), ())), preferred_element_type=jnp.float32
            )
            scores = scores * scale + bias_ref[variant, head]
            scores = jnp.where(match, scores, MASKED)
            largest = jnp.max(scores, axis=-1, keepdims=True)
            weights = jnp.exp(scores - largest)
            probabilities = (weights / jnp.sum(weights, axis=-1, keepdims=True)).astype(jnp.bfloat16)
            mixed.append(
                jnp.dot(probabilities, value, preferred_element_type=jnp.float32).astype(jnp.bfloat16)
            )
        mixed = jnp.concatenate(mixed, axis=-1)
        branch = jnp.dot(mixed, wp_ref[...], preferred_element_type=jnp.float32)
        own = x_ref[source, 0].astype(jnp.float32)
        hidden_in = (own + branch).astype(jnp.bfloat16)
        normed = normalize(hidden_in).astype(jnp.bfloat16)
        hidden = jnp.dot(normed, wup_ref[...], preferred_element_type=jnp.float32)
        hidden = (0.5 * hidden * (1.0 + lax.erf(hidden * (2.0 ** -0.5)))).astype(jnp.bfloat16)
        result = hidden_in.astype(jnp.float32) + jnp.dot(
            hidden, wdown_ref[...], preferred_element_type=jnp.float32
        )
        out_ref[variant, 0] = result.astype(jnp.bfloat16)


def padded_weights(w_qkv, w_proj, heads):
    channels = w_proj.shape[0]
    width = channels // heads
    columns = []
    for head in range(heads):
        for part in range(3):
            start = part * channels + head * width
            columns.append(jnp.pad(w_qkv[:, start : start + width], ((0, 0), (0, LANE - width))))
    rows = [
        jnp.pad(w_proj[head * width : (head + 1) * width], ((0, LANE - width), (0, 0)))
        for head in range(heads)
    ]
    return jnp.concatenate(columns, axis=1), jnp.concatenate(rows, axis=0)


def swin_block(windows, region, w_qkv, w_proj, w_up, w_down, bias_grid):
    inputs, count, cells, channels = windows.shape
    variants, heads = bias_grid.shape[:2]
    groups = -(-count // GROUP)
    extra = groups * GROUP - count
    windows = jnp.pad(windows, ((0, 0), (0, extra), (0, 0), (0, 0)))
    region = jnp.pad(region, ((0, extra), (0, 0)))
    tokens = GROUP * cells
    x = windows.reshape(inputs, groups, tokens, channels)
    labq = region.reshape(groups, tokens, 1)
    labk = region.reshape(groups, 1, tokens)
    bias = jnp.tile(bias_grid, (1, 1, GROUP, GROUP))
    wqkv, wp = padded_weights(w_qkv, w_proj, heads)
    scale = (channels // heads) ** (-0.5)
    whole = lambda shape: pl.BlockSpec(shape, lambda g: (0,) * len(shape))
    out = pl.pallas_call(
        functools.partial(block_kernel, variants, heads, scale),
        out_shape=jax.ShapeDtypeStruct((variants, groups, tokens, channels), jnp.bfloat16),
        grid=(groups,),
        in_specs=[
            pl.BlockSpec((inputs, 1, tokens, channels), lambda g: (0, g, 0, 0)),
            pl.BlockSpec((1, tokens, 1), lambda g: (g, 0, 0)),
            pl.BlockSpec((1, 1, tokens), lambda g: (g, 0, 0)),
            whole(bias.shape),
            whole(wqkv.shape),
            whole(wp.shape),
            whole(w_up.shape),
            whole(w_down.shape),
        ],
        out_specs=pl.BlockSpec((variants, 1, tokens, channels), lambda g: (0, g, 0, 0)),
        compiler_params=pltpu.CompilerParams(vmem_limit_bytes=48 * 1024 * 1024),
    )(x, labq, labk, bias, wqkv, wp, w_up, w_down)
    out = out.reshape(variants, groups * GROUP, cells, channels)
    return out[:, :count]


def block_on_grid(tokens, region, w_qkv, w_proj, w_up, w_down, bias_grid):
    height, breadth = tokens.shape[1], tokens.shape[2]
    windows = to_windows(tokens)
    region_windows = to_windows(region[None, :, :, None])[0, :, :, 0]
    out = swin_block(windows, region_windows, w_qkv, w_proj, w_up, w_down, bias_grid)
    return from_windows(out, height, breadth)


def normalize(values):
    values = values.astype(jnp.float32)
    average = jnp.mean(values, axis=-1, keepdims=True)
    centred = values - average
    spread = jnp.mean(centred * centred, axis=-1, keepdims=True)
    return centred * lax.rsqrt(spread + EPSILON)


def to_windows(grid):
    leading, height, breadth, channels = grid.shape
    grid = grid.reshape(leading, height // WIN, WIN, breadth // WIN, WIN, channels)
    grid = grid.transpose(0, 1, 3, 2, 4, 5)
    return grid.reshape(leading, height // WIN * (breadth // WIN), WIN * WIN, channels)


def from_windows(windows, height, breadth):
    leading, window_count, cells, channels = windows.shape
    windows = windows.reshape(leading, height // WIN, breadth // WIN, WIN, WIN, channels)
    windows = windows.transpose(0, 1, 3, 2, 4, 5)
    return windows.reshape(leading, height, breadth, channels)


def bias_table(offset_table, variant_codes):
    position = jnp.arange(WIN * WIN, dtype=jnp.int32)
    row_step = (position // WIN)[:, None] - (position // WIN)[None, :]
    across = (position % WIN)[:, None] - (position % WIN)[None, :]
    transpose_bit = (variant_codes // 4)[:, None, None]
    flip_rows = (variant_codes // 2 % 2)[:, None, None]
    flip_cols = (variant_codes % 2)[:, None, None]
    row_moved = jnp.where(flip_rows == 1, -row_step, row_step)
    col_moved = jnp.where(flip_cols == 1, -across, across)
    leading_step = jnp.where(transpose_bit == 1, col_moved, row_moved)
    trailing_step = jnp.where(transpose_bit == 1, row_moved, col_moved)
    table_index = (leading_step + WIN - 1) * (2 * WIN - 1) + trailing_step + WIN - 1
    slots = jnp.arange((2 * WIN - 1) * (2 * WIN - 1), dtype=jnp.int32)
    one_hot = (table_index[..., None] == slots).astype(jnp.float32)
    return jnp.einsum("vqkt,ht->vhqk", one_hot, offset_table, precision=lax.Precision.HIGHEST)


def variant_kernels(kernel, variant_codes):
    transpose_bit = (variant_codes // 4)[:, None]
    flip_rows = (variant_codes // 2 % 2)[:, None]
    flip_cols = (variant_codes % 2)[:, None]
    kernel_spot = jnp.arange(9, dtype=jnp.int32)
    step_row = (kernel_spot // 3 - 1)[None, :]
    step_col = (kernel_spot % 3 - 1)[None, :]
    row_moved = jnp.where(flip_rows == 1, -step_row, step_row)
    col_moved = jnp.where(flip_cols == 1, -step_col, step_col)
    source_row = jnp.where(transpose_bit == 1, col_moved, row_moved)
    source_col = jnp.where(transpose_bit == 1, row_moved, col_moved)
    source = (source_row + 1) * 3 + source_col + 1
    pick_place = (source[:, :, None] == kernel_spot[None, None, :]).astype(jnp.bfloat16)
    channel = jnp.arange(kernel.shape[-1], dtype=jnp.int32)
    colour = (channel // (SCALE * SCALE))[None, :]
    sub_row = (channel % (SCALE * SCALE) // SCALE)[None, :]
    sub_col = (channel % SCALE)[None, :]
    sub_row_moved = jnp.where(flip_rows == 1, SCALE - 1 - sub_row, sub_row)
    sub_col_moved = jnp.where(flip_cols == 1, SCALE - 1 - sub_col, sub_col)
    anchor_row = jnp.where(transpose_bit == 1, sub_col_moved, sub_row_moved)
    anchor_col = jnp.where(transpose_bit == 1, sub_row_moved, sub_col_moved)
    anchor = colour * SCALE * SCALE + anchor_row * SCALE + anchor_col
    pick_channel = (channel[None, :, None] == anchor[:, None, :]).astype(jnp.bfloat16)
    placed = jnp.einsum(
        "vpq,qcs->vpcs", pick_place, kernel, preferred_element_type=jnp.float32
    ).astype(jnp.bfloat16)
    return jnp.einsum(
        "vpcs,vso->vpco", placed, pick_channel, preferred_element_type=jnp.float32
    ).astype(jnp.bfloat16)


def attend(normed, region, w_qkv, w_proj, bias_grid):
    head_count = bias_grid.shape[1]
    leading, window_count, cells, channels = normed.shape
    head_width = channels // head_count
    projected = jnp.einsum(
        "lnsc,ce->lnse", normed, w_qkv, preferred_element_type=jnp.float32
    ).astype(jnp.bfloat16)
    projected = projected.reshape(leading, window_count, cells, 3, head_count, head_width)
    queries = projected[:, :, :, 0]
    key_part = projected[:, :, :, 1]
    value_part = projected[:, :, :, 2]
    scores = jnp.einsum("lnqhd,lnkhd->lnhqk", queries, key_part, preferred_element_type=jnp.float32)
    scores = scores * head_width ** (-0.5) + bias_grid[:, None]
    matches = region[:, None, :, None] == region[:, None, None, :]
    scores = jnp.where(matches[None], scores, MASKED)
    largest = jnp.max(scores, axis=-1, keepdims=True)
    weights = jnp.exp(scores - largest)
    probabilities = (weights / jnp.sum(weights, axis=-1, keepdims=True)).astype(jnp.bfloat16)
    value_part = jnp.broadcast_to(value_part, (probabilities.shape[0],) + value_part.shape[1:])
    mixed = jnp.einsum(
        "lnhqk,lnkhd->lnqhd", probabilities, value_part, preferred_element_type=jnp.float32
    ).astype(jnp.bfloat16)
    mixed = mixed.reshape(probabilities.shape[0], window_count, cells, channels)
    return jnp.einsum("lnsc,ce->lnse", mixed, w_proj, preferred_element_type=jnp.float32)


def attention_half(tokens, region, w_qkv, w_proj, bias_grid):
    height, breadth = (tokens.shape[1], tokens.shape[2])
    windows = to_windows(tokens)
    region_windows = to_windows(region[None, :, :, None])[0, :, :, 0]
    normed = normalize(windows).astype(jnp.bfloat16)
    branch = attend(normed, region_windows, w_qkv, w_proj, bias_grid)
    result = (windows.astype(jnp.float32) + branch).astype(jnp.bfloat16)
    return from_windows(result, height, breadth)


def feed_forward(tokens, w_up, w_down):
    normed = normalize(tokens).astype(jnp.bfloat16)
    hidden = jnp.einsum("...c,ce->...e", normed, w_up, preferred_element_type=jnp.float32)
    hidden = jax.nn.gelu(hidden, approximate=False).astype(jnp.bfloat16)
    output = tokens.astype(jnp.float32) + jnp.einsum(
        "...e,ec->...c", hidden, w_down, preferred_element_type=jnp.float32
    )
    return output.astype(jnp.bfloat16)


def reconstruct(padded, kernels, height, breadth):
    accumulated = jnp.zeros((padded.shape[0], height, breadth, kernels.shape[-1]), jnp.float32)
    for kernel_spot in range(9):
        spot_row, spot_col = (kernel_spot // 3, kernel_spot % 3)
        window = padded[:, spot_row : spot_row + height, spot_col : spot_col + breadth]
        accumulated = accumulated + jnp.einsum(
            "vrcd,vde->vrce", window, kernels[:, kernel_spot], preferred_element_type=jnp.float32
        )
    return accumulated


def refine(average, region, w_qkv, w_proj, bias_grid):
    normed = normalize(average).astype(jnp.bfloat16)[None]
    return average + attend(normed, region, w_qkv, w_proj, bias_grid)[0]


def local(
    features,
    labels,
    qkv_weight,
    proj_weight,
    up_weight,
    down_weight,
    swin_bias,
    recon_weight,
    refine_qkv,
    refine_proj,
    refine_bias,
):
    height, breadth, channels = features.shape
    variant_codes = lax.axis_index("var") * VAR_DEV + jnp.arange(VAR_DEV, dtype=jnp.int32)
    first_bias = bias_table(swin_bias[0], variant_codes)
    second_bias = bias_table(swin_bias[1], variant_codes)
    region = extended(labels, (("ty", 0), ("tx", 1)), SHIFT)
    block_one = block_on_grid(
        features[None], labels, qkv_weight[0], proj_weight[0], up_weight[0], down_weight[0], first_bias
    )
    shifted = extended(block_one, (("ty", 1), ("tx", 2)), SHIFT)
    block_two = block_on_grid(
        shifted, region, qkv_weight[1], proj_weight[1], up_weight[1], down_weight[1], second_bias
    )
    padded = block_two[:, SHIFT - 1 : SHIFT + height + 1, SHIFT - 1 : SHIFT + breadth + 1]
    row = lax.axis_index("ty") * height - 1 + jnp.arange(height + 2)
    col = lax.axis_index("tx") * breadth - 1 + jnp.arange(breadth + 2)
    inside = ((row >= 0) & (row < lax.axis_size("ty") * height))[:, None] & (
        (col >= 0) & (col < lax.axis_size("tx") * breadth)
    )[None, :]
    padded = jnp.where(inside[None, :, :, None], padded, jnp.zeros_like(padded))
    kernels = variant_kernels(recon_weight, variant_codes)
    summed = jnp.sum(reconstruct(padded, kernels, height, breadth), axis=0)
    region_windows = to_windows(labels[None, :, :, None])[0, :, :, 0]
    refine_grid = bias_table(refine_bias, jnp.zeros((1,), jnp.int32))
    rows, cols, depth = summed.shape
    combined = var_sum(summed.astype(jnp.bfloat16).reshape(rows * cols, depth)).reshape(rows, cols, depth)
    refined = refine(
        to_windows(combined[None])[0] / 8.0, region_windows, refine_qkv, refine_proj, refine_grid
    )
    refined_grid = from_windows(refined[None], height, breadth)[0]
    picture = refined_grid.reshape(height, breadth, 3, SCALE, SCALE).transpose(2, 0, 3, 1, 4)
    return picture.reshape(3, SCALE * height, SCALE * breadth)


def solution(mesh):
    placed = (P("ty", "tx", None), P("ty", "tx"), P(), P(), P(), P(), P(), P(), P(), P(), P())
    return jax.shard_map(
        local, mesh=mesh, in_specs=placed, out_specs=P(None, "ty", "tx"), check_vma=False
    )
```

```python
import functools

import jax
import jax.numpy as jnp
from jax import lax
from jax.experimental import pallas as pl
from jax.experimental.pallas import tpu as pltpu
from jax.sharding import PartitionSpec as P

MESH = pl.DeviceIdType.MESH

WIN = 8
SHIFT = 4
SCALE = 4
VAR_DEV = 2


EPSILON = 1e-05
MASKED = -1e30


def extended(cells, sides, width):
    for axis, dim in sides:
        count = lax.axis_size(axis)
        ends = count - 1
        head = lax.slice_in_dim(cells, 0, width, axis=dim)
        tail = lax.slice_in_dim(cells, cells.shape[dim] - width, cells.shape[dim], axis=dim)
        cells = jnp.concatenate(
            [
                lax.ppermute(tail, axis, [(i, (i + 1) % count) for i in range(ends)]),
                cells,
                lax.ppermute(head, axis, [((i + 1) % count, i) for i in range(ends)]),
            ],
            axis=dim,
        )
    return cells


def var_sum_kernel(count, part_ref, out_ref, held, send_sem, recv_sem, own_sem):
    me = lax.axis_index("var")
    barrier = pltpu.get_barrier_semaphore()
    for step in range(1, count):
        peer = lax.rem(me + step, count)
        pl.semaphore_signal(barrier, inc=1, device_id={"var": peer}, device_id_type=MESH)
    pl.semaphore_wait(barrier, count - 1)
    own = pltpu.make_async_copy(part_ref, held.at[me], own_sem)
    own.start()
    sends = []
    for step in range(1, count):
        peer = lax.rem(me + step, count)
        copy = pltpu.make_async_remote_copy(
            src_ref=part_ref,
            dst_ref=held.at[me],
            send_sem=send_sem.at[step - 1],
            recv_sem=recv_sem.at[me],
            device_id={"var": peer},
            device_id_type=MESH,
        )
        copy.start()
        sends.append(copy)
    own.wait()
    for copy in sends:
        copy.wait_send()
    for step in range(1, count):
        source = lax.rem(me + count - step, count)
        pltpu.make_async_remote_copy(
            src_ref=part_ref,
            dst_ref=held.at[source],
            send_sem=send_sem.at[step - 1],
            recv_sem=recv_sem.at[source],
            device_id={"var": source},
            device_id_type=MESH,
        ).wait_recv()
    total = held[0].astype(jnp.float32)
    for index in range(1, count):
        total = total + held[index].astype(jnp.float32)
    out_ref[...] = total


def var_sum(part):
    count = lax.axis_size("var")
    return pl.pallas_call(
        functools.partial(var_sum_kernel, count),
        out_shape=jax.ShapeDtypeStruct(part.shape, jnp.float32),
        in_specs=[pl.BlockSpec(memory_space=pltpu.VMEM)],
        out_specs=pl.BlockSpec(memory_space=pltpu.VMEM),
        scratch_shapes=[
            pltpu.VMEM((count,) + part.shape, part.dtype),
            pltpu.SemaphoreType.DMA((count - 1,)),
            pltpu.SemaphoreType.DMA((count,)),
            pltpu.SemaphoreType.DMA(()),
        ],
        compiler_params=pltpu.CompilerParams(collective_id=0, has_side_effects=True),
    )(part)


GROUP = 4
LANE = 128


def block_kernel(
    variants, heads, scale, x_ref, labq_ref, labk_ref, bias_ref, wqkv_ref, wp_ref, wup_ref, wdown_ref, out_ref
):
    inputs = x_ref.shape[0]
    tokens = x_ref.shape[2]
    labq = labq_ref[0]
    labk = labk_ref[0]
    slot_q = lax.broadcasted_iota(jnp.int32, (tokens, tokens), 0) // (WIN * WIN)
    slot_k = lax.broadcasted_iota(jnp.int32, (tokens, tokens), 1) // (WIN * WIN)
    match = (labq == labk) & (slot_q == slot_k)
    projected = []
    for index in range(inputs):
        normed = normalize(x_ref[index, 0]).astype(jnp.bfloat16)
        projected.append(
            jnp.dot(normed, wqkv_ref[...], preferred_element_type=jnp.float32).astype(jnp.bfloat16)
        )
    for variant in range(variants):
        source = variant if inputs > 1 else 0
        qkv = projected[source]
        mixed = []
        for head in range(heads):
            base = head * 3 * LANE
            query = qkv[:, base : base + LANE]
            key = qkv[:, base + LANE : base + 2 * LANE]
            value = qkv[:, base + 2 * LANE : base + 3 * LANE]
            scores = lax.dot_general(
                query, key, (((1,), (1,)), ((), ())), preferred_element_type=jnp.float32
            )
            scores = scores * scale
            scores = (scores.reshape(GROUP, WIN * WIN, tokens) + bias_ref[variant, head][None]).reshape(
                tokens, tokens
            )
            scores = jnp.where(match, scores, MASKED)
            largest = jnp.max(scores, axis=-1, keepdims=True)
            weights = jnp.exp(scores - largest)
            probabilities = (weights / jnp.sum(weights, axis=-1, keepdims=True)).astype(jnp.bfloat16)
            mixed.append(
                jnp.dot(probabilities, value, preferred_element_type=jnp.float32).astype(jnp.bfloat16)
            )
        mixed = jnp.concatenate(mixed, axis=-1)
        branch = jnp.dot(mixed, wp_ref[...], preferred_element_type=jnp.float32)
        own = x_ref[source, 0].astype(jnp.float32)
        hidden_in = (own + branch).astype(jnp.bfloat16)
        normed = normalize(hidden_in).astype(jnp.bfloat16)
        hidden = jnp.dot(normed, wup_ref[...], preferred_element_type=jnp.float32)
        hidden = (0.5 * hidden * (1.0 + lax.erf(hidden * (2.0 ** -0.5)))).astype(jnp.bfloat16)
        result = hidden_in.astype(jnp.float32) + jnp.dot(
            hidden, wdown_ref[...], preferred_element_type=jnp.float32
        )
        out_ref[variant, 0] = result.astype(jnp.bfloat16)


def padded_weights(w_qkv, w_proj, heads):
    channels = w_proj.shape[0]
    width = channels // heads
    columns = w_qkv.reshape(channels, 3, heads, width).transpose(0, 2, 1, 3)
    columns = jnp.pad(columns, ((0, 0), (0, 0), (0, 0), (0, LANE - width)))
    rows = jnp.pad(w_proj.reshape(heads, width, channels), ((0, 0), (0, LANE - width), (0, 0)))
    return columns.reshape(channels, heads * 3 * LANE), rows.reshape(heads * LANE, channels)


def swin_block(windows, region, w_qkv, w_proj, w_up, w_down, bias_grid):
    inputs, count, cells, channels = windows.shape
    variants, heads = bias_grid.shape[:2]
    groups = -(-count // GROUP)
    extra = groups * GROUP - count
    windows = jnp.pad(windows, ((0, 0), (0, extra), (0, 0), (0, 0)))
    region = jnp.pad(region, ((0, extra), (0, 0)))
    tokens = GROUP * cells
    x = windows.reshape(inputs, groups, tokens, channels)
    labq = region.reshape(groups, tokens, 1)
    labk = region.reshape(groups, 1, tokens)
    bias = jnp.tile(bias_grid, (1, 1, 1, GROUP))
    wqkv, wp = padded_weights(w_qkv, w_proj, heads)
    scale = (channels // heads) ** (-0.5)
    whole = lambda shape: pl.BlockSpec(shape, lambda g: (0,) * len(shape))
    out = pl.pallas_call(
        functools.partial(block_kernel, variants, heads, scale),
        out_shape=jax.ShapeDtypeStruct((variants, groups, tokens, channels), jnp.bfloat16),
        grid=(groups,),
        in_specs=[
            pl.BlockSpec((inputs, 1, tokens, channels), lambda g: (0, g, 0, 0)),
            pl.BlockSpec((1, tokens, 1), lambda g: (g, 0, 0)),
            pl.BlockSpec((1, 1, tokens), lambda g: (g, 0, 0)),
            whole(bias.shape),
            whole(wqkv.shape),
            whole(wp.shape),
            whole(w_up.shape),
            whole(w_down.shape),
        ],
        out_specs=pl.BlockSpec((variants, 1, tokens, channels), lambda g: (0, g, 0, 0)),
        compiler_params=pltpu.CompilerParams(vmem_limit_bytes=48 * 1024 * 1024),
    )(x, labq, labk, bias, wqkv, wp, w_up, w_down)
    out = out.reshape(variants, groups * GROUP, cells, channels)
    return out[:, :count]


def block_on_grid(tokens, region, w_qkv, w_proj, w_up, w_down, bias_grid):
    height, breadth = tokens.shape[1], tokens.shape[2]
    windows = to_windows(tokens)
    region_windows = to_windows(region[None, :, :, None])[0, :, :, 0]
    out = swin_block(windows, region_windows, w_qkv, w_proj, w_up, w_down, bias_grid)
    return from_windows(out, height, breadth)


def normalize(values):
    values = values.astype(jnp.float32)
    average = jnp.mean(values, axis=-1, keepdims=True)
    centred = values - average
    spread = jnp.mean(centred * centred, axis=-1, keepdims=True)
    return centred * lax.rsqrt(spread + EPSILON)


def to_windows(grid):
    leading, height, breadth, channels = grid.shape
    grid = grid.reshape(leading, height // WIN, WIN, breadth // WIN, WIN, channels)
    grid = grid.transpose(0, 1, 3, 2, 4, 5)
    return grid.reshape(leading, height // WIN * (breadth // WIN), WIN * WIN, channels)


def from_windows(windows, height, breadth):
    leading, window_count, cells, channels = windows.shape
    windows = windows.reshape(leading, height // WIN, breadth // WIN, WIN, WIN, channels)
    windows = windows.transpose(0, 1, 3, 2, 4, 5)
    return windows.reshape(leading, height, breadth, channels)


def bias_table(offset_table, variant_codes):
    position = jnp.arange(WIN * WIN, dtype=jnp.int32)
    row_step = (position // WIN)[:, None] - (position // WIN)[None, :]
    across = (position % WIN)[:, None] - (position % WIN)[None, :]
    transpose_bit = (variant_codes // 4)[:, None, None]
    flip_rows = (variant_codes // 2 % 2)[:, None, None]
    flip_cols = (variant_codes % 2)[:, None, None]
    row_moved = jnp.where(flip_rows == 1, -row_step, row_step)
    col_moved = jnp.where(flip_cols == 1, -across, across)
    leading_step = jnp.where(transpose_bit == 1, col_moved, row_moved)
    trailing_step = jnp.where(transpose_bit == 1, row_moved, col_moved)
    table_index = (leading_step + WIN - 1) * (2 * WIN - 1) + trailing_step + WIN - 1
    slots = jnp.arange((2 * WIN - 1) * (2 * WIN - 1), dtype=jnp.int32)
    one_hot = (table_index[..., None] == slots).astype(jnp.float32)
    return jnp.einsum("vqkt,ht->vhqk", one_hot, offset_table, precision=lax.Precision.HIGHEST)


def variant_kernels(kernel, variant_codes):
    transpose_bit = (variant_codes // 4)[:, None]
    flip_rows = (variant_codes // 2 % 2)[:, None]
    flip_cols = (variant_codes % 2)[:, None]
    kernel_spot = jnp.arange(9, dtype=jnp.int32)
    step_row = (kernel_spot // 3 - 1)[None, :]
    step_col = (kernel_spot % 3 - 1)[None, :]
    row_moved = jnp.where(flip_rows == 1, -step_row, step_row)
    col_moved = jnp.where(flip_cols == 1, -step_col, step_col)
    source_row = jnp.where(transpose_bit == 1, col_moved, row_moved)
    source_col = jnp.where(transpose_bit == 1, row_moved, col_moved)
    source = (source_row + 1) * 3 + source_col + 1
    pick_place = (source[:, :, None] == kernel_spot[None, None, :]).astype(jnp.bfloat16)
    channel = jnp.arange(kernel.shape[-1], dtype=jnp.int32)
    colour = (channel // (SCALE * SCALE))[None, :]
    sub_row = (channel % (SCALE * SCALE) // SCALE)[None, :]
    sub_col = (channel % SCALE)[None, :]
    sub_row_moved = jnp.where(flip_rows == 1, SCALE - 1 - sub_row, sub_row)
    sub_col_moved = jnp.where(flip_cols == 1, SCALE - 1 - sub_col, sub_col)
    anchor_row = jnp.where(transpose_bit == 1, sub_col_moved, sub_row_moved)
    anchor_col = jnp.where(transpose_bit == 1, sub_row_moved, sub_col_moved)
    anchor = colour * SCALE * SCALE + anchor_row * SCALE + anchor_col
    pick_channel = (channel[None, :, None] == anchor[:, None, :]).astype(jnp.bfloat16)
    placed = jnp.einsum(
        "vpq,qcs->vpcs", pick_place, kernel, preferred_element_type=jnp.float32
    ).astype(jnp.bfloat16)
    return jnp.einsum(
        "vpcs,vso->vpco", placed, pick_channel, preferred_element_type=jnp.float32
    ).astype(jnp.bfloat16)


def attend(normed, region, w_qkv, w_proj, bias_grid):
    head_count = bias_grid.shape[1]
    leading, window_count, cells, channels = normed.shape
    head_width = channels // head_count
    projected = jnp.einsum(
        "lnsc,ce->lnse", normed, w_qkv, preferred_element_type=jnp.float32
    ).astype(jnp.bfloat16)
    projected = projected.reshape(leading, window_count, cells, 3, head_count, head_width)
    queries = projected[:, :, :, 0]
    key_part = projected[:, :, :, 1]
    value_part = projected[:, :, :, 2]
    scores = jnp.einsum("lnqhd,lnkhd->lnhqk", queries, key_part, preferred_element_type=jnp.float32)
    scores = scores * head_width ** (-0.5) + bias_grid[:, None]
    matches = region[:, None, :, None] == region[:, None, None, :]
    scores = jnp.where(matches[None], scores, MASKED)
    largest = jnp.max(scores, axis=-1, keepdims=True)
    weights = jnp.exp(scores - largest)
    probabilities = (weights / jnp.sum(weights, axis=-1, keepdims=True)).astype(jnp.bfloat16)
    value_part = jnp.broadcast_to(value_part, (probabilities.shape[0],) + value_part.shape[1:])
    mixed = jnp.einsum(
        "lnhqk,lnkhd->lnqhd", probabilities, value_part, preferred_element_type=jnp.float32
    ).astype(jnp.bfloat16)
    mixed = mixed.reshape(probabilities.shape[0], window_count, cells, channels)
    return jnp.einsum("lnsc,ce->lnse", mixed, w_proj, preferred_element_type=jnp.float32)


def attention_half(tokens, region, w_qkv, w_proj, bias_grid):
    height, breadth = (tokens.shape[1], tokens.shape[2])
    windows = to_windows(tokens)
    region_windows = to_windows(region[None, :, :, None])[0, :, :, 0]
    normed = normalize(windows).astype(jnp.bfloat16)
    branch = attend(normed, region_windows, w_qkv, w_proj, bias_grid)
    result = (windows.astype(jnp.float32) + branch).astype(jnp.bfloat16)
    return from_windows(result, height, breadth)


def feed_forward(tokens, w_up, w_down):
    normed = normalize(tokens).astype(jnp.bfloat16)
    hidden = jnp.einsum("...c,ce->...e", normed, w_up, preferred_element_type=jnp.float32)
    hidden = jax.nn.gelu(hidden, approximate=False).astype(jnp.bfloat16)
    output = tokens.astype(jnp.float32) + jnp.einsum(
        "...e,ec->...c", hidden, w_down, preferred_element_type=jnp.float32
    )
    return output.astype(jnp.bfloat16)


def reconstruct(padded, kernels, height, breadth):
    accumulated = jnp.zeros((padded.shape[0], height, breadth, kernels.shape[-1]), jnp.float32)
    for kernel_spot in range(9):
        spot_row, spot_col = (kernel_spot // 3, kernel_spot % 3)
        window = padded[:, spot_row : spot_row + height, spot_col : spot_col + breadth]
        accumulated = accumulated + jnp.einsum(
            "vrcd,vde->vrce", window, kernels[:, kernel_spot], preferred_element_type=jnp.float32
        )
    return accumulated


def refine(average, region, w_qkv, w_proj, bias_grid):
    normed = normalize(average).astype(jnp.bfloat16)[None]
    return average + attend(normed, region, w_qkv, w_proj, bias_grid)[0]


def local(
    features,
    labels,
    qkv_weight,
    proj_weight,
    up_weight,
    down_weight,
    swin_bias,
    recon_weight,
    refine_qkv,
    refine_proj,
    refine_bias,
):
    height, breadth, channels = features.shape
    variant_codes = lax.axis_index("var") * VAR_DEV + jnp.arange(VAR_DEV, dtype=jnp.int32)
    first_bias = bias_table(swin_bias[0], variant_codes)
    second_bias = bias_table(swin_bias[1], variant_codes)
    region = extended(labels, (("ty", 0), ("tx", 1)), SHIFT)
    block_one = block_on_grid(
        features[None], labels, qkv_weight[0], proj_weight[0], up_weight[0], down_weight[0], first_bias
    )
    shifted = extended(block_one, (("ty", 1), ("tx", 2)), SHIFT)
    block_two = block_on_grid(
        shifted, region, qkv_weight[1], proj_weight[1], up_weight[1], down_weight[1], second_bias
    )
    padded = block_two[:, SHIFT - 1 : SHIFT + height + 1, SHIFT - 1 : SHIFT + breadth + 1]
    row = lax.axis_index("ty") * height - 1 + jnp.arange(height + 2)
    col = lax.axis_index("tx") * breadth - 1 + jnp.arange(breadth + 2)
    inside = ((row >= 0) & (row < lax.axis_size("ty") * height))[:, None] & (
        (col >= 0) & (col < lax.axis_size("tx") * breadth)
    )[None, :]
    padded = jnp.where(inside[None, :, :, None], padded, jnp.zeros_like(padded))
    kernels = variant_kernels(recon_weight, variant_codes)
    summed = jnp.sum(reconstruct(padded, kernels, height, breadth), axis=0)
    region_windows = to_windows(labels[None, :, :, None])[0, :, :, 0]
    refine_grid = bias_table(refine_bias, jnp.zeros((1,), jnp.int32))
    rows, cols, depth = summed.shape
    combined = var_sum(summed.astype(jnp.bfloat16).reshape(rows * cols, depth)).reshape(rows, cols, depth)
    refined = refine(
        to_windows(combined[None])[0] / 8.0, region_windows, refine_qkv, refine_proj, refine_grid
    )
    refined_grid = from_windows(refined[None], height, breadth)[0]
    picture = refined_grid.reshape(height, breadth, 3, SCALE, SCALE).transpose(2, 0, 3, 1, 4)
    return picture.reshape(3, SCALE * height, SCALE * breadth)


def solution(mesh):
    placed = (P("ty", "tx", None), P("ty", "tx"), P(), P(), P(), P(), P(), P(), P(), P(), P())
    return jax.shard_map(
        local, mesh=mesh, in_specs=placed, out_specs=P(None, "ty", "tx"), check_vma=False
    )
```

```python
import functools

import jax
import jax.numpy as jnp
from jax import lax
from jax.experimental import pallas as pl
from jax.experimental.pallas import tpu as pltpu
from jax.sharding import PartitionSpec as P

MESH = pl.DeviceIdType.MESH

WIN = 8
SHIFT = 4
SCALE = 4
VAR_DEV = 2


EPSILON = 1e-05
MASKED = -1e30


def extended(cells, sides, width):
    for axis, dim in sides:
        count = lax.axis_size(axis)
        ends = count - 1
        head = lax.slice_in_dim(cells, 0, width, axis=dim)
        tail = lax.slice_in_dim(cells, cells.shape[dim] - width, cells.shape[dim], axis=dim)
        cells = jnp.concatenate(
            [
                lax.ppermute(tail, axis, [(i, (i + 1) % count) for i in range(ends)]),
                cells,
                lax.ppermute(head, axis, [((i + 1) % count, i) for i in range(ends)]),
            ],
            axis=dim,
        )
    return cells


def var_sum_kernel(count, part_ref, out_ref, held, send_sem, recv_sem, own_sem):
    me = lax.axis_index("var")
    barrier = pltpu.get_barrier_semaphore()
    for step in range(1, count):
        peer = lax.rem(me + step, count)
        pl.semaphore_signal(barrier, inc=1, device_id={"var": peer}, device_id_type=MESH)
    pl.semaphore_wait(barrier, count - 1)
    own = pltpu.make_async_copy(part_ref, held.at[me], own_sem)
    own.start()
    sends = []
    for step in range(1, count):
        peer = lax.rem(me + step, count)
        copy = pltpu.make_async_remote_copy(
            src_ref=part_ref,
            dst_ref=held.at[me],
            send_sem=send_sem.at[step - 1],
            recv_sem=recv_sem.at[me],
            device_id={"var": peer},
            device_id_type=MESH,
        )
        copy.start()
        sends.append(copy)
    own.wait()
    for copy in sends:
        copy.wait_send()
    for step in range(1, count):
        source = lax.rem(me + count - step, count)
        pltpu.make_async_remote_copy(
            src_ref=part_ref,
            dst_ref=held.at[source],
            send_sem=send_sem.at[step - 1],
            recv_sem=recv_sem.at[source],
            device_id={"var": source},
            device_id_type=MESH,
        ).wait_recv()
    total = held[0].astype(jnp.float32)
    for index in range(1, count):
        total = total + held[index].astype(jnp.float32)
    out_ref[...] = total


def var_sum(part):
    count = lax.axis_size("var")
    return pl.pallas_call(
        functools.partial(var_sum_kernel, count),
        out_shape=jax.ShapeDtypeStruct(part.shape, jnp.float32),
        in_specs=[pl.BlockSpec(memory_space=pltpu.VMEM)],
        out_specs=pl.BlockSpec(memory_space=pltpu.VMEM),
        scratch_shapes=[
            pltpu.VMEM((count,) + part.shape, part.dtype),
            pltpu.SemaphoreType.DMA((count - 1,)),
            pltpu.SemaphoreType.DMA((count,)),
            pltpu.SemaphoreType.DMA(()),
        ],
        compiler_params=pltpu.CompilerParams(collective_id=0, has_side_effects=True),
    )(part)


GROUP = 4
LANE = 128


def block_kernel(
    variants, heads, scale, x_ref, labq_ref, labk_ref, bias_ref, wqkv_ref, wp_ref, wup_ref, wdown_ref, out_ref
):
    inputs = x_ref.shape[0]
    tokens = x_ref.shape[2]
    labq = labq_ref[0]
    labk = labk_ref[0]
    slot_q = lax.broadcasted_iota(jnp.int32, (tokens, tokens), 0) // (WIN * WIN)
    slot_k = lax.broadcasted_iota(jnp.int32, (tokens, tokens), 1) // (WIN * WIN)
    match = (labq == labk) & (slot_q == slot_k)
    projected = []
    for index in range(inputs):
        normed = normalize(x_ref[index, 0]).astype(jnp.bfloat16)
        projected.append(
            jnp.dot(normed, wqkv_ref[...], preferred_element_type=jnp.float32).astype(jnp.bfloat16)
        )
    for variant in range(variants):
        source = variant if inputs > 1 else 0
        qkv = projected[source]
        mixed = []
        for head in range(heads):
            base = head * 3 * LANE
            query = qkv[:, base : base + LANE]
            key = qkv[:, base + LANE : base + 2 * LANE]
            value = qkv[:, base + 2 * LANE : base + 3 * LANE]
            scores = lax.dot_general(
                query, key, (((1,), (1,)), ((), ())), preferred_element_type=jnp.float32
            )
            scores = scores * scale
            scores = (scores.reshape(GROUP, WIN * WIN, tokens) + bias_ref[variant, head][None]).reshape(
                tokens, tokens
            )
            scores = jnp.where(match, scores, MASKED)
            largest = jnp.max(scores, axis=-1, keepdims=True)
            weights = jnp.exp(scores - largest)
            probabilities = (weights / jnp.sum(weights, axis=-1, keepdims=True)).astype(jnp.bfloat16)
            mixed.append(
                jnp.dot(probabilities, value, preferred_element_type=jnp.float32).astype(jnp.bfloat16)
            )
        mixed = jnp.concatenate(mixed, axis=-1)
        branch = jnp.dot(mixed, wp_ref[...], preferred_element_type=jnp.float32)
        own = x_ref[source, 0].astype(jnp.float32)
        hidden_in = (own + branch).astype(jnp.bfloat16)
        normed = normalize(hidden_in).astype(jnp.bfloat16)
        hidden = jnp.dot(normed, wup_ref[...], preferred_element_type=jnp.float32)
        hidden = (0.5 * hidden * (1.0 + lax.erf(hidden * (2.0 ** -0.5)))).astype(jnp.bfloat16)
        result = hidden_in.astype(jnp.float32) + jnp.dot(
            hidden, wdown_ref[...], preferred_element_type=jnp.float32
        )
        out_ref[variant, 0] = result.astype(jnp.bfloat16)


def padded_weights(w_qkv, w_proj, heads):
    channels = w_proj.shape[0]
    width = channels // heads
    columns = w_qkv.reshape(channels, 3, heads, width).transpose(0, 2, 1, 3)
    columns = jnp.pad(columns, ((0, 0), (0, 0), (0, 0), (0, LANE - width)))
    rows = jnp.pad(w_proj.reshape(heads, width, channels), ((0, 0), (0, LANE - width), (0, 0)))
    return columns.reshape(channels, heads * 3 * LANE), rows.reshape(heads * LANE, channels)


def swin_block(windows, region, w_qkv, w_proj, w_up, w_down, bias_grid):
    inputs, count, cells, channels = windows.shape
    variants, heads = bias_grid.shape[:2]
    groups = -(-count // GROUP)
    extra = groups * GROUP - count
    windows = jnp.pad(windows, ((0, 0), (0, extra), (0, 0), (0, 0)))
    region = jnp.pad(region, ((0, extra), (0, 0)))
    tokens = GROUP * cells
    x = windows.reshape(inputs, groups, tokens, channels)
    labq = region.reshape(groups, tokens, 1)
    labk = region.reshape(groups, 1, tokens)
    bias = jnp.tile(bias_grid, (1, 1, 1, GROUP))
    wqkv, wp = padded_weights(w_qkv, w_proj, heads)
    scale = (channels // heads) ** (-0.5)
    whole = lambda shape: pl.BlockSpec(shape, lambda g: (0,) * len(shape))
    out = pl.pallas_call(
        functools.partial(block_kernel, variants, heads, scale),
        out_shape=jax.ShapeDtypeStruct((variants, groups, tokens, channels), jnp.bfloat16),
        grid=(groups,),
        in_specs=[
            pl.BlockSpec((inputs, 1, tokens, channels), lambda g: (0, g, 0, 0)),
            pl.BlockSpec((1, tokens, 1), lambda g: (g, 0, 0)),
            pl.BlockSpec((1, 1, tokens), lambda g: (g, 0, 0)),
            whole(bias.shape),
            whole(wqkv.shape),
            whole(wp.shape),
            whole(w_up.shape),
            whole(w_down.shape),
        ],
        out_specs=pl.BlockSpec((variants, 1, tokens, channels), lambda g: (0, g, 0, 0)),
        compiler_params=pltpu.CompilerParams(vmem_limit_bytes=48 * 1024 * 1024),
    )(x, labq, labk, bias, wqkv, wp, w_up, w_down)
    out = out.reshape(variants, groups * GROUP, cells, channels)
    return out[:, :count]


def block_on_grid(tokens, region, w_qkv, w_proj, w_up, w_down, bias_grid):
    height, breadth = tokens.shape[1], tokens.shape[2]
    windows = to_windows(tokens)
    region_windows = to_windows(region[None, :, :, None])[0, :, :, 0]
    out = swin_block(windows, region_windows, w_qkv, w_proj, w_up, w_down, bias_grid)
    return from_windows(out, height, breadth)


def normalize(values):
    values = values.astype(jnp.float32)
    average = jnp.mean(values, axis=-1, keepdims=True)
    centred = values - average
    spread = jnp.mean(centred * centred, axis=-1, keepdims=True)
    return centred * lax.rsqrt(spread + EPSILON)


def to_windows(grid):
    leading, height, breadth, channels = grid.shape
    grid = grid.reshape(leading, height // WIN, WIN, breadth // WIN, WIN, channels)
    grid = grid.transpose(0, 1, 3, 2, 4, 5)
    return grid.reshape(leading, height // WIN * (breadth // WIN), WIN * WIN, channels)


def from_windows(windows, height, breadth):
    leading, window_count, cells, channels = windows.shape
    windows = windows.reshape(leading, height // WIN, breadth // WIN, WIN, WIN, channels)
    windows = windows.transpose(0, 1, 3, 2, 4, 5)
    return windows.reshape(leading, height, breadth, channels)


def bias_table(offset_table, variant_codes):
    position = jnp.arange(WIN * WIN, dtype=jnp.int32)
    row_step = (position // WIN)[:, None] - (position // WIN)[None, :]
    across = (position % WIN)[:, None] - (position % WIN)[None, :]
    transpose_bit = (variant_codes // 4)[:, None, None]
    flip_rows = (variant_codes // 2 % 2)[:, None, None]
    flip_cols = (variant_codes % 2)[:, None, None]
    row_moved = jnp.where(flip_rows == 1, -row_step, row_step)
    col_moved = jnp.where(flip_cols == 1, -across, across)
    leading_step = jnp.where(transpose_bit == 1, col_moved, row_moved)
    trailing_step = jnp.where(transpose_bit == 1, row_moved, col_moved)
    table_index = (leading_step + WIN - 1) * (2 * WIN - 1) + trailing_step + WIN - 1
    slots = jnp.arange((2 * WIN - 1) * (2 * WIN - 1), dtype=jnp.int32)
    one_hot = (table_index[..., None] == slots).astype(jnp.float32)
    return jnp.einsum("vqkt,ht->vhqk", one_hot, offset_table, precision=lax.Precision.HIGHEST)


def variant_kernels(kernel, variant_codes):
    transpose_bit = (variant_codes // 4)[:, None]
    flip_rows = (variant_codes // 2 % 2)[:, None]
    flip_cols = (variant_codes % 2)[:, None]
    kernel_spot = jnp.arange(9, dtype=jnp.int32)
    step_row = (kernel_spot // 3 - 1)[None, :]
    step_col = (kernel_spot % 3 - 1)[None, :]
    row_moved = jnp.where(flip_rows == 1, -step_row, step_row)
    col_moved = jnp.where(flip_cols == 1, -step_col, step_col)
    source_row = jnp.where(transpose_bit == 1, col_moved, row_moved)
    source_col = jnp.where(transpose_bit == 1, row_moved, col_moved)
    source = (source_row + 1) * 3 + source_col + 1
    pick_place = (source[:, :, None] == kernel_spot[None, None, :]).astype(jnp.bfloat16)
    channel = jnp.arange(kernel.shape[-1], dtype=jnp.int32)
    colour = (channel // (SCALE * SCALE))[None, :]
    sub_row = (channel % (SCALE * SCALE) // SCALE)[None, :]
    sub_col = (channel % SCALE)[None, :]
    sub_row_moved = jnp.where(flip_rows == 1, SCALE - 1 - sub_row, sub_row)
    sub_col_moved = jnp.where(flip_cols == 1, SCALE - 1 - sub_col, sub_col)
    anchor_row = jnp.where(transpose_bit == 1, sub_col_moved, sub_row_moved)
    anchor_col = jnp.where(transpose_bit == 1, sub_row_moved, sub_col_moved)
    anchor = colour * SCALE * SCALE + anchor_row * SCALE + anchor_col
    pick_channel = (channel[None, :, None] == anchor[:, None, :]).astype(jnp.bfloat16)
    placed = jnp.einsum(
        "vpq,qcs->vpcs", pick_place, kernel, preferred_element_type=jnp.float32
    ).astype(jnp.bfloat16)
    return jnp.einsum(
        "vpcs,vso->vpco", placed, pick_channel, preferred_element_type=jnp.float32
    ).astype(jnp.bfloat16)


def attend(normed, region, w_qkv, w_proj, bias_grid):
    head_count = bias_grid.shape[1]
    leading, window_count, cells, channels = normed.shape
    head_width = channels // head_count
    projected = jnp.einsum(
        "lnsc,ce->lnse", normed, w_qkv, preferred_element_type=jnp.float32
    ).astype(jnp.bfloat16)
    projected = projected.reshape(leading, window_count, cells, 3, head_count, head_width)
    queries = projected[:, :, :, 0]
    key_part = projected[:, :, :, 1]
    value_part = projected[:, :, :, 2]
    scores = jnp.einsum("lnqhd,lnkhd->lnhqk", queries, key_part, preferred_element_type=jnp.float32)
    scores = scores * head_width ** (-0.5) + bias_grid[:, None]
    matches = region[:, None, :, None] == region[:, None, None, :]
    scores = jnp.where(matches[None], scores, MASKED)
    largest = jnp.max(scores, axis=-1, keepdims=True)
    weights = jnp.exp(scores - largest)
    probabilities = (weights / jnp.sum(weights, axis=-1, keepdims=True)).astype(jnp.bfloat16)
    value_part = jnp.broadcast_to(value_part, (probabilities.shape[0],) + value_part.shape[1:])
    mixed = jnp.einsum(
        "lnhqk,lnkhd->lnqhd", probabilities, value_part, preferred_element_type=jnp.float32
    ).astype(jnp.bfloat16)
    mixed = mixed.reshape(probabilities.shape[0], window_count, cells, channels)
    return jnp.einsum("lnsc,ce->lnse", mixed, w_proj, preferred_element_type=jnp.float32)


def attention_half(tokens, region, w_qkv, w_proj, bias_grid):
    height, breadth = (tokens.shape[1], tokens.shape[2])
    windows = to_windows(tokens)
    region_windows = to_windows(region[None, :, :, None])[0, :, :, 0]
    normed = normalize(windows).astype(jnp.bfloat16)
    branch = attend(normed, region_windows, w_qkv, w_proj, bias_grid)
    result = (windows.astype(jnp.float32) + branch).astype(jnp.bfloat16)
    return from_windows(result, height, breadth)


def feed_forward(tokens, w_up, w_down):
    normed = normalize(tokens).astype(jnp.bfloat16)
    hidden = jnp.einsum("...c,ce->...e", normed, w_up, preferred_element_type=jnp.float32)
    hidden = jax.nn.gelu(hidden, approximate=False).astype(jnp.bfloat16)
    output = tokens.astype(jnp.float32) + jnp.einsum(
        "...e,ec->...c", hidden, w_down, preferred_element_type=jnp.float32
    )
    return output.astype(jnp.bfloat16)


def reconstruct(padded, kernels, height, breadth):
    accumulated = jnp.zeros((padded.shape[0], height, breadth, kernels.shape[-1]), jnp.float32)
    for kernel_spot in range(9):
        spot_row, spot_col = (kernel_spot // 3, kernel_spot % 3)
        window = padded[:, spot_row : spot_row + height, spot_col : spot_col + breadth]
        accumulated = accumulated + jnp.einsum(
            "vrcd,vde->vrce", window, kernels[:, kernel_spot], preferred_element_type=jnp.float32
        )
    return accumulated


def refine(average, region, w_qkv, w_proj, bias_grid):
    normed = normalize(average).astype(jnp.bfloat16)[None]
    return average + attend(normed, region, w_qkv, w_proj, bias_grid)[0]


def local(
    features,
    labels,
    qkv_weight,
    proj_weight,
    up_weight,
    down_weight,
    swin_bias,
    recon_weight,
    refine_qkv,
    refine_proj,
    refine_bias,
):
    height, breadth, channels = features.shape
    variant_codes = lax.axis_index("var") * VAR_DEV + jnp.arange(VAR_DEV, dtype=jnp.int32)
    first_bias = bias_table(swin_bias[0], variant_codes)
    second_bias = bias_table(swin_bias[1], variant_codes)
    region = extended(labels, (("ty", 0), ("tx", 1)), SHIFT)
    block_one = block_on_grid(
        features[None], labels, qkv_weight[0], proj_weight[0], up_weight[0], down_weight[0], first_bias
    )
    shifted = extended(block_one, (("ty", 1), ("tx", 2)), SHIFT)
    block_two = block_on_grid(
        shifted, region, qkv_weight[1], proj_weight[1], up_weight[1], down_weight[1], second_bias
    )
    padded = block_two[:, SHIFT - 1 : SHIFT + height + 1, SHIFT - 1 : SHIFT + breadth + 1]
    row = lax.axis_index("ty") * height - 1 + jnp.arange(height + 2)
    col = lax.axis_index("tx") * breadth - 1 + jnp.arange(breadth + 2)
    inside = ((row >= 0) & (row < lax.axis_size("ty") * height))[:, None] & (
        (col >= 0) & (col < lax.axis_size("tx") * breadth)
    )[None, :]
    padded = jnp.where(inside[None, :, :, None], padded, jnp.zeros_like(padded))
    kernels = variant_kernels(recon_weight, variant_codes)
    summed = jnp.sum(reconstruct(padded, kernels, height, breadth), axis=0)
    region_windows = to_windows(labels[None, :, :, None])[0, :, :, 0]
    refine_grid = bias_table(refine_bias, jnp.zeros((1,), jnp.int32))
    rows, cols, depth = summed.shape
    combined = var_sum(summed.astype(jnp.bfloat16).reshape(rows, cols * depth)).reshape(rows, cols, depth)
    refined = refine(
        to_windows(combined[None])[0] / 8.0, region_windows, refine_qkv, refine_proj, refine_grid
    )
    colours = refined.shape[-1] // (SCALE * SCALE)
    picture = refined.reshape(
        height // WIN, breadth // WIN, WIN, WIN, colours * SCALE, SCALE
    ).transpose(4, 0, 2, 1, 3, 5)
    picture = picture.reshape(colours, SCALE, height, breadth * SCALE).transpose(0, 2, 1, 3)
    return picture.reshape(colours, SCALE * height, SCALE * breadth)


def solution(mesh):
    placed = (P("ty", "tx", None), P("ty", "tx"), P(), P(), P(), P(), P(), P(), P(), P(), P())
    return jax.shard_map(
        local, mesh=mesh, in_specs=placed, out_specs=P(None, "ty", "tx"), check_vma=False
    )
```

```python
import functools

import jax
import jax.numpy as jnp
from jax import lax
from jax.experimental import pallas as pl
from jax.experimental.pallas import tpu as pltpu
from jax.sharding import PartitionSpec as P

MESH = pl.DeviceIdType.MESH

WIN = 8
SHIFT = 4
SCALE = 4
VAR_DEV = 2


EPSILON = 1e-05
MASKED = -1e30


def extended(cells, sides, width):
    for axis, dim in sides:
        count = lax.axis_size(axis)
        ends = count - 1
        head = lax.slice_in_dim(cells, 0, width, axis=dim)
        tail = lax.slice_in_dim(cells, cells.shape[dim] - width, cells.shape[dim], axis=dim)
        cells = jnp.concatenate(
            [
                lax.ppermute(tail, axis, [(i, (i + 1) % count) for i in range(ends)]),
                cells,
                lax.ppermute(head, axis, [((i + 1) % count, i) for i in range(ends)]),
            ],
            axis=dim,
        )
    return cells


def var_sum_kernel(count, part_ref, out_ref, held, send_sem, recv_sem, own_sem):
    me = lax.axis_index("var")
    barrier = pltpu.get_barrier_semaphore()
    for step in range(1, count):
        peer = lax.rem(me + step, count)
        pl.semaphore_signal(barrier, inc=1, device_id={"var": peer}, device_id_type=MESH)
    pl.semaphore_wait(barrier, count - 1)
    own = pltpu.make_async_copy(part_ref, held.at[me], own_sem)
    own.start()
    sends = []
    for step in range(1, count):
        peer = lax.rem(me + step, count)
        copy = pltpu.make_async_remote_copy(
            src_ref=part_ref,
            dst_ref=held.at[me],
            send_sem=send_sem.at[step - 1],
            recv_sem=recv_sem.at[me],
            device_id={"var": peer},
            device_id_type=MESH,
        )
        copy.start()
        sends.append(copy)
    own.wait()
    for copy in sends:
        copy.wait_send()
    for step in range(1, count):
        source = lax.rem(me + count - step, count)
        pltpu.make_async_remote_copy(
            src_ref=part_ref,
            dst_ref=held.at[source],
            send_sem=send_sem.at[step - 1],
            recv_sem=recv_sem.at[source],
            device_id={"var": source},
            device_id_type=MESH,
        ).wait_recv()
    total = held[0].astype(jnp.float32)
    for index in range(1, count):
        total = total + held[index].astype(jnp.float32)
    out_ref[...] = total


def var_sum(part):
    count = lax.axis_size("var")
    return pl.pallas_call(
        functools.partial(var_sum_kernel, count),
        out_shape=jax.ShapeDtypeStruct(part.shape, jnp.float32),
        in_specs=[pl.BlockSpec(memory_space=pltpu.VMEM)],
        out_specs=pl.BlockSpec(memory_space=pltpu.VMEM),
        scratch_shapes=[
            pltpu.VMEM((count,) + part.shape, part.dtype),
            pltpu.SemaphoreType.DMA((count - 1,)),
            pltpu.SemaphoreType.DMA((count,)),
            pltpu.SemaphoreType.DMA(()),
        ],
        compiler_params=pltpu.CompilerParams(collective_id=0, has_side_effects=True),
    )(part)


GROUP = 4
LANE = 128


def block_kernel(
    variants, heads, scale, x_ref, labq_ref, labk_ref, bias_ref, wqkv_ref, wp_ref, wup_ref, wdown_ref, out_ref
):
    inputs = x_ref.shape[0]
    tokens = x_ref.shape[2]
    labq = labq_ref[0]
    labk = labk_ref[0]
    slot_q = lax.broadcasted_iota(jnp.int32, (tokens, tokens), 0) // (WIN * WIN)
    slot_k = lax.broadcasted_iota(jnp.int32, (tokens, tokens), 1) // (WIN * WIN)
    match = (labq == labk) & (slot_q == slot_k)
    projected = []
    for index in range(inputs):
        normed = normalize(x_ref[index, 0]).astype(jnp.bfloat16)
        projected.append(
            jnp.dot(normed, wqkv_ref[...], preferred_element_type=jnp.float32).astype(jnp.bfloat16)
        )
    span = wp_ref.shape[0]
    width = wup_ref.shape[0] // heads
    lane = lax.broadcasted_iota(jnp.int32, (1, span), 1)
    for variant in range(variants):
        source = variant if inputs > 1 else 0
        qkv = projected[source]
        query = qkv[:, :span]
        key = qkv[:, span : 2 * span]
        value = qkv[:, 2 * span :]
        mixed = jnp.zeros((tokens, span), jnp.float32)
        for head in range(heads):
            mine = (lane >= head * width) & (lane < (head + 1) * width)
            scores = lax.dot_general(
                jnp.where(mine, query, jnp.zeros_like(query)),
                key,
                (((1,), (1,)), ((), ())),
                preferred_element_type=jnp.float32,
            )
            scores = scores * scale
            scores = (scores.reshape(GROUP, WIN * WIN, tokens) + bias_ref[variant, head][None]).reshape(
                tokens, tokens
            )
            scores = jnp.where(match, scores, MASKED)
            largest = jnp.max(scores, axis=-1, keepdims=True)
            weights = jnp.exp(scores - largest)
            probabilities = (weights / jnp.sum(weights, axis=-1, keepdims=True)).astype(jnp.bfloat16)
            mixed = mixed + jnp.dot(
                probabilities, jnp.where(mine, value, jnp.zeros_like(value)), preferred_element_type=jnp.float32
            )
        branch = jnp.dot(mixed.astype(jnp.bfloat16), wp_ref[...], preferred_element_type=jnp.float32)
        own = x_ref[source, 0].astype(jnp.float32)
        hidden_in = (own + branch).astype(jnp.bfloat16)
        normed = normalize(hidden_in).astype(jnp.bfloat16)
        hidden = jnp.dot(normed, wup_ref[...], preferred_element_type=jnp.float32)
        hidden = (0.5 * hidden * (1.0 + lax.erf(hidden * (2.0 ** -0.5)))).astype(jnp.bfloat16)
        result = hidden_in.astype(jnp.float32) + jnp.dot(
            hidden, wdown_ref[...], preferred_element_type=jnp.float32
        )
        out_ref[variant, 0] = result.astype(jnp.bfloat16)


def padded_weights(w_qkv, w_proj, heads):
    channels = w_proj.shape[0]
    span = -(-channels // LANE) * LANE
    columns = jnp.pad(w_qkv.reshape(channels, 3, channels), ((0, 0), (0, 0), (0, span - channels)))
    rows = jnp.pad(w_proj, ((0, span - channels), (0, 0)))
    return columns.reshape(channels, 3 * span), rows


def swin_block(windows, region, w_qkv, w_proj, w_up, w_down, bias_grid):
    inputs, count, cells, channels = windows.shape
    variants, heads = bias_grid.shape[:2]
    groups = -(-count // GROUP)
    extra = groups * GROUP - count
    windows = jnp.pad(windows, ((0, 0), (0, extra), (0, 0), (0, 0)))
    region = jnp.pad(region, ((0, extra), (0, 0)))
    tokens = GROUP * cells
    x = windows.reshape(inputs, groups, tokens, channels)
    labq = region.reshape(groups, tokens, 1)
    labk = region.reshape(groups, 1, tokens)
    bias = jnp.tile(bias_grid, (1, 1, 1, GROUP))
    wqkv, wp = padded_weights(w_qkv, w_proj, heads)
    scale = (channels // heads) ** (-0.5)
    whole = lambda shape: pl.BlockSpec(shape, lambda g: (0,) * len(shape))
    out = pl.pallas_call(
        functools.partial(block_kernel, variants, heads, scale),
        out_shape=jax.ShapeDtypeStruct((variants, groups, tokens, channels), jnp.bfloat16),
        grid=(groups,),
        in_specs=[
            pl.BlockSpec((inputs, 1, tokens, channels), lambda g: (0, g, 0, 0)),
            pl.BlockSpec((1, tokens, 1), lambda g: (g, 0, 0)),
            pl.BlockSpec((1, 1, tokens), lambda g: (g, 0, 0)),
            whole(bias.shape),
            whole(wqkv.shape),
            whole(wp.shape),
            whole(w_up.shape),
            whole(w_down.shape),
        ],
        out_specs=pl.BlockSpec((variants, 1, tokens, channels), lambda g: (0, g, 0, 0)),
        compiler_params=pltpu.CompilerParams(vmem_limit_bytes=48 * 1024 * 1024),
    )(x, labq, labk, bias, wqkv, wp, w_up, w_down)
    out = out.reshape(variants, groups * GROUP, cells, channels)
    return out[:, :count]


def block_on_grid(tokens, region, w_qkv, w_proj, w_up, w_down, bias_grid):
    height, breadth = tokens.shape[1], tokens.shape[2]
    windows = to_windows(tokens)
    region_windows = to_windows(region[None, :, :, None])[0, :, :, 0]
    out = swin_block(windows, region_windows, w_qkv, w_proj, w_up, w_down, bias_grid)
    return from_windows(out, height, breadth)


def normalize(values):
    values = values.astype(jnp.float32)
    average = jnp.mean(values, axis=-1, keepdims=True)
    centred = values - average
    spread = jnp.mean(centred * centred, axis=-1, keepdims=True)
    return centred * lax.rsqrt(spread + EPSILON)


def to_windows(grid):
    leading, height, breadth, channels = grid.shape
    grid = grid.reshape(leading, height // WIN, WIN, breadth // WIN, WIN, channels)
    grid = grid.transpose(0, 1, 3, 2, 4, 5)
    return grid.reshape(leading, height // WIN * (breadth // WIN), WIN * WIN, channels)


def from_windows(windows, height, breadth):
    leading, window_count, cells, channels = windows.shape
    windows = windows.reshape(leading, height // WIN, breadth // WIN, WIN, WIN, channels)
    windows = windows.transpose(0, 1, 3, 2, 4, 5)
    return windows.reshape(leading, height, breadth, channels)


def bias_table(offset_table, variant_codes):
    position = jnp.arange(WIN * WIN, dtype=jnp.int32)
    row_step = (position // WIN)[:, None] - (position // WIN)[None, :]
    across = (position % WIN)[:, None] - (position % WIN)[None, :]
    transpose_bit = (variant_codes // 4)[:, None, None]
    flip_rows = (variant_codes // 2 % 2)[:, None, None]
    flip_cols = (variant_codes % 2)[:, None, None]
    row_moved = jnp.where(flip_rows == 1, -row_step, row_step)
    col_moved = jnp.where(flip_cols == 1, -across, across)
    leading_step = jnp.where(transpose_bit == 1, col_moved, row_moved)
    trailing_step = jnp.where(transpose_bit == 1, row_moved, col_moved)
    table_index = (leading_step + WIN - 1) * (2 * WIN - 1) + trailing_step + WIN - 1
    slots = jnp.arange((2 * WIN - 1) * (2 * WIN - 1), dtype=jnp.int32)
    one_hot = (table_index[..., None] == slots).astype(jnp.float32)
    return jnp.einsum("vqkt,ht->vhqk", one_hot, offset_table, precision=lax.Precision.HIGHEST)


def variant_kernels(kernel, variant_codes):
    transpose_bit = (variant_codes // 4)[:, None]
    flip_rows = (variant_codes // 2 % 2)[:, None]
    flip_cols = (variant_codes % 2)[:, None]
    kernel_spot = jnp.arange(9, dtype=jnp.int32)
    step_row = (kernel_spot // 3 - 1)[None, :]
    step_col = (kernel_spot % 3 - 1)[None, :]
    row_moved = jnp.where(flip_rows == 1, -step_row, step_row)
    col_moved = jnp.where(flip_cols == 1, -step_col, step_col)
    source_row = jnp.where(transpose_bit == 1, col_moved, row_moved)
    source_col = jnp.where(transpose_bit == 1, row_moved, col_moved)
    source = (source_row + 1) * 3 + source_col + 1
    pick_place = (source[:, :, None] == kernel_spot[None, None, :]).astype(jnp.bfloat16)
    channel = jnp.arange(kernel.shape[-1], dtype=jnp.int32)
    colour = (channel // (SCALE * SCALE))[None, :]
    sub_row = (channel % (SCALE * SCALE) // SCALE)[None, :]
    sub_col = (channel % SCALE)[None, :]
    sub_row_moved = jnp.where(flip_rows == 1, SCALE - 1 - sub_row, sub_row)
    sub_col_moved = jnp.where(flip_cols == 1, SCALE - 1 - sub_col, sub_col)
    anchor_row = jnp.where(transpose_bit == 1, sub_col_moved, sub_row_moved)
    anchor_col = jnp.where(transpose_bit == 1, sub_row_moved, sub_col_moved)
    anchor = colour * SCALE * SCALE + anchor_row * SCALE + anchor_col
    pick_channel = (channel[None, :, None] == anchor[:, None, :]).astype(jnp.bfloat16)
    placed = jnp.einsum(
        "vpq,qcs->vpcs", pick_place, kernel, preferred_element_type=jnp.float32
    ).astype(jnp.bfloat16)
    return jnp.einsum(
        "vpcs,vso->vpco", placed, pick_channel, preferred_element_type=jnp.float32
    ).astype(jnp.bfloat16)


def attend(normed, region, w_qkv, w_proj, bias_grid):
    head_count = bias_grid.shape[1]
    leading, window_count, cells, channels = normed.shape
    head_width = channels // head_count
    projected = jnp.einsum(
        "lnsc,ce->lnse", normed, w_qkv, preferred_element_type=jnp.float32
    ).astype(jnp.bfloat16)
    projected = projected.reshape(leading, window_count, cells, 3, head_count, head_width)
    queries = projected[:, :, :, 0]
    key_part = projected[:, :, :, 1]
    value_part = projected[:, :, :, 2]
    scores = jnp.einsum("lnqhd,lnkhd->lnhqk", queries, key_part, preferred_element_type=jnp.float32)
    scores = scores * head_width ** (-0.5) + bias_grid[:, None]
    matches = region[:, None, :, None] == region[:, None, None, :]
    scores = jnp.where(matches[None], scores, MASKED)
    largest = jnp.max(scores, axis=-1, keepdims=True)
    weights = jnp.exp(scores - largest)
    probabilities = (weights / jnp.sum(weights, axis=-1, keepdims=True)).astype(jnp.bfloat16)
    value_part = jnp.broadcast_to(value_part, (probabilities.shape[0],) + value_part.shape[1:])
    mixed = jnp.einsum(
        "lnhqk,lnkhd->lnqhd", probabilities, value_part, preferred_element_type=jnp.float32
    ).astype(jnp.bfloat16)
    mixed = mixed.reshape(probabilities.shape[0], window_count, cells, channels)
    return jnp.einsum("lnsc,ce->lnse", mixed, w_proj, preferred_element_type=jnp.float32)


def attention_half(tokens, region, w_qkv, w_proj, bias_grid):
    height, breadth = (tokens.shape[1], tokens.shape[2])
    windows = to_windows(tokens)
    region_windows = to_windows(region[None, :, :, None])[0, :, :, 0]
    normed = normalize(windows).astype(jnp.bfloat16)
    branch = attend(normed, region_windows, w_qkv, w_proj, bias_grid)
    result = (windows.astype(jnp.float32) + branch).astype(jnp.bfloat16)
    return from_windows(result, height, breadth)


def feed_forward(tokens, w_up, w_down):
    normed = normalize(tokens).astype(jnp.bfloat16)
    hidden = jnp.einsum("...c,ce->...e", normed, w_up, preferred_element_type=jnp.float32)
    hidden = jax.nn.gelu(hidden, approximate=False).astype(jnp.bfloat16)
    output = tokens.astype(jnp.float32) + jnp.einsum(
        "...e,ec->...c", hidden, w_down, preferred_element_type=jnp.float32
    )
    return output.astype(jnp.bfloat16)


def reconstruct(padded, kernels, height, breadth):
    accumulated = jnp.zeros((padded.shape[0], height, breadth, kernels.shape[-1]), jnp.float32)
    for kernel_spot in range(9):
        spot_row, spot_col = (kernel_spot // 3, kernel_spot % 3)
        window = padded[:, spot_row : spot_row + height, spot_col : spot_col + breadth]
        accumulated = accumulated + jnp.einsum(
            "vrcd,vde->vrce", window, kernels[:, kernel_spot], preferred_element_type=jnp.float32
        )
    return accumulated


def refine(average, region, w_qkv, w_proj, bias_grid):
    normed = normalize(average).astype(jnp.bfloat16)[None]
    return average + attend(normed, region, w_qkv, w_proj, bias_grid)[0]


def local(
    features,
    labels,
    qkv_weight,
    proj_weight,
    up_weight,
    down_weight,
    swin_bias,
    recon_weight,
    refine_qkv,
    refine_proj,
    refine_bias,
):
    height, breadth, channels = features.shape
    variant_codes = lax.axis_index("var") * VAR_DEV + jnp.arange(VAR_DEV, dtype=jnp.int32)
    first_bias = bias_table(swin_bias[0], variant_codes)
    second_bias = bias_table(swin_bias[1], variant_codes)
    region = extended(labels, (("ty", 0), ("tx", 1)), SHIFT)
    block_one = block_on_grid(
        features[None], labels, qkv_weight[0], proj_weight[0], up_weight[0], down_weight[0], first_bias
    )
    shifted = extended(block_one, (("ty", 1), ("tx", 2)), SHIFT)
    block_two = block_on_grid(
        shifted, region, qkv_weight[1], proj_weight[1], up_weight[1], down_weight[1], second_bias
    )
    padded = block_two[:, SHIFT - 1 : SHIFT + height + 1, SHIFT - 1 : SHIFT + breadth + 1]
    row = lax.axis_index("ty") * height - 1 + jnp.arange(height + 2)
    col = lax.axis_index("tx") * breadth - 1 + jnp.arange(breadth + 2)
    inside = ((row >= 0) & (row < lax.axis_size("ty") * height))[:, None] & (
        (col >= 0) & (col < lax.axis_size("tx") * breadth)
    )[None, :]
    padded = jnp.where(inside[None, :, :, None], padded, jnp.zeros_like(padded))
    kernels = variant_kernels(recon_weight, variant_codes)
    summed = jnp.sum(reconstruct(padded, kernels, height, breadth), axis=0)
    region_windows = to_windows(labels[None, :, :, None])[0, :, :, 0]
    refine_grid = bias_table(refine_bias, jnp.zeros((1,), jnp.int32))
    rows, cols, depth = summed.shape
    combined = var_sum(summed.astype(jnp.bfloat16).reshape(rows, cols * depth)).reshape(rows, cols, depth)
    refined = refine(
        to_windows(combined[None])[0] / 8.0, region_windows, refine_qkv, refine_proj, refine_grid
    )
    colours = refined.shape[-1] // (SCALE * SCALE)
    picture = refined.reshape(
        height // WIN, breadth // WIN, WIN, WIN, colours * SCALE, SCALE
    ).transpose(4, 0, 2, 1, 3, 5)
    picture = picture.reshape(colours, SCALE, height, breadth * SCALE).transpose(0, 2, 1, 3)
    return picture.reshape(colours, SCALE * height, SCALE * breadth)


def solution(mesh):
    placed = (P("ty", "tx", None), P("ty", "tx"), P(), P(), P(), P(), P(), P(), P(), P(), P())
    return jax.shard_map(
        local, mesh=mesh, in_specs=placed, out_specs=P(None, "ty", "tx"), check_vma=False
    )
```

```python
import functools

import jax
import jax.numpy as jnp
from jax import lax
from jax.experimental import pallas as pl
from jax.experimental.pallas import tpu as pltpu
from jax.sharding import PartitionSpec as P

MESH = pl.DeviceIdType.MESH

WIN = 8
SHIFT = 4
SCALE = 4
VAR_DEV = 2


EPSILON = 1e-05
MASKED = -1e30


def extended(cells, sides, width):
    for axis, dim in sides:
        count = lax.axis_size(axis)
        ends = count - 1
        head = lax.slice_in_dim(cells, 0, width, axis=dim)
        tail = lax.slice_in_dim(cells, cells.shape[dim] - width, cells.shape[dim], axis=dim)
        cells = jnp.concatenate(
            [
                lax.ppermute(tail, axis, [(i, (i + 1) % count) for i in range(ends)]),
                cells,
                lax.ppermute(head, axis, [((i + 1) % count, i) for i in range(ends)]),
            ],
            axis=dim,
        )
    return cells


def var_sum_kernel(count, part_ref, out_ref, held, send_sem, recv_sem, own_sem):
    me = lax.axis_index("var")
    barrier = pltpu.get_barrier_semaphore()
    for step in range(1, count):
        peer = lax.rem(me + step, count)
        pl.semaphore_signal(barrier, inc=1, device_id={"var": peer}, device_id_type=MESH)
    pl.semaphore_wait(barrier, count - 1)
    own = pltpu.make_async_copy(part_ref, held.at[me], own_sem)
    own.start()
    sends = []
    for step in range(1, count):
        peer = lax.rem(me + step, count)
        copy = pltpu.make_async_remote_copy(
            src_ref=part_ref,
            dst_ref=held.at[me],
            send_sem=send_sem.at[step - 1],
            recv_sem=recv_sem.at[me],
            device_id={"var": peer},
            device_id_type=MESH,
        )
        copy.start()
        sends.append(copy)
    own.wait()
    for copy in sends:
        copy.wait_send()
    for step in range(1, count):
        source = lax.rem(me + count - step, count)
        pltpu.make_async_remote_copy(
            src_ref=part_ref,
            dst_ref=held.at[source],
            send_sem=send_sem.at[step - 1],
            recv_sem=recv_sem.at[source],
            device_id={"var": source},
            device_id_type=MESH,
        ).wait_recv()
    total = held[0].astype(jnp.float32)
    for index in range(1, count):
        total = total + held[index].astype(jnp.float32)
    out_ref[...] = total


def var_sum(part):
    count = lax.axis_size("var")
    return pl.pallas_call(
        functools.partial(var_sum_kernel, count),
        out_shape=jax.ShapeDtypeStruct(part.shape, jnp.float32),
        in_specs=[pl.BlockSpec(memory_space=pltpu.VMEM)],
        out_specs=pl.BlockSpec(memory_space=pltpu.VMEM),
        scratch_shapes=[
            pltpu.VMEM((count,) + part.shape, part.dtype),
            pltpu.SemaphoreType.DMA((count - 1,)),
            pltpu.SemaphoreType.DMA((count,)),
            pltpu.SemaphoreType.DMA(()),
        ],
        compiler_params=pltpu.CompilerParams(collective_id=0, has_side_effects=True),
    )(part)


GROUP = 4
LANE = 128


def block_kernel(
    variants, heads, scale, x_ref, labq_ref, labk_ref, bias_ref, wqkv_ref, wp_ref, wup_ref, wdown_ref, out_ref
):
    inputs = x_ref.shape[0]
    tokens = x_ref.shape[2]
    labq = labq_ref[0]
    labk = labk_ref[0]
    slot_q = lax.broadcasted_iota(jnp.int32, (tokens, tokens), 0) // (WIN * WIN)
    slot_k = lax.broadcasted_iota(jnp.int32, (tokens, tokens), 1) // (WIN * WIN)
    match = (labq == labk) & (slot_q == slot_k)
    projected = []
    for index in range(inputs):
        normed = normalize(x_ref[index, 0]).astype(jnp.bfloat16)
        projected.append(
            jnp.dot(normed, wqkv_ref[...], preferred_element_type=jnp.float32).astype(jnp.bfloat16)
        )
    span = wp_ref.shape[0]
    width = wup_ref.shape[0] // heads
    lane = lax.broadcasted_iota(jnp.int32, (1, span), 1)
    for variant in range(variants):
        source = variant if inputs > 1 else 0
        qkv = projected[source]
        query = qkv[:, :span]
        key = qkv[:, span : 2 * span]
        value = qkv[:, 2 * span :]
        mixed = jnp.zeros((tokens, span), jnp.float32)
        for head in range(heads):
            mine = (lane >= head * width) & (lane < (head + 1) * width)
            scores = lax.dot_general(
                jnp.where(mine, query, jnp.zeros_like(query)),
                key,
                (((1,), (1,)), ((), ())),
                preferred_element_type=jnp.float32,
            )
            scores = scores * scale
            scores = (scores.reshape(GROUP, WIN * WIN, tokens) + bias_ref[variant, head][None]).reshape(
                tokens, tokens
            )
            scores = jnp.where(match, scores, MASKED)
            largest = jnp.max(scores, axis=-1, keepdims=True)
            weights = jnp.exp(scores - largest)
            probabilities = (weights / jnp.sum(weights, axis=-1, keepdims=True)).astype(jnp.bfloat16)
            mixed = mixed + jnp.dot(
                probabilities, jnp.where(mine, value, jnp.zeros_like(value)), preferred_element_type=jnp.float32
            )
        branch = jnp.dot(mixed.astype(jnp.bfloat16), wp_ref[...], preferred_element_type=jnp.float32)
        own = x_ref[source, 0].astype(jnp.float32)
        hidden_in = (own + branch).astype(jnp.bfloat16)
        normed = normalize(hidden_in).astype(jnp.bfloat16)
        hidden = jnp.dot(normed, wup_ref[...], preferred_element_type=jnp.float32)
        hidden = (0.5 * hidden * (1.0 + lax.erf(hidden * (2.0 ** -0.5)))).astype(jnp.bfloat16)
        result = hidden_in.astype(jnp.float32) + jnp.dot(
            hidden, wdown_ref[...], preferred_element_type=jnp.float32
        )
        out_ref[variant, 0] = result.astype(jnp.bfloat16)


def padded_weights(w_qkv, w_proj, heads):
    channels = w_proj.shape[0]
    span = -(-channels // LANE) * LANE
    columns = jnp.pad(w_qkv.reshape(channels, 3, channels), ((0, 0), (0, 0), (0, span - channels)))
    rows = jnp.pad(w_proj, ((0, span - channels), (0, 0)))
    return columns.reshape(channels, 3 * span), rows


def swin_block(windows, region, w_qkv, w_proj, w_up, w_down, bias_grid):
    inputs, count, cells, channels = windows.shape
    variants, heads = bias_grid.shape[:2]
    groups = -(-count // GROUP)
    extra = groups * GROUP - count
    windows = jnp.pad(windows, ((0, 0), (0, extra), (0, 0), (0, 0)))
    region = jnp.pad(region, ((0, extra), (0, 0)))
    tokens = GROUP * cells
    x = windows.reshape(inputs, groups, tokens, channels)
    labq = region.reshape(groups, tokens, 1)
    labk = region.reshape(groups, 1, tokens)
    bias = jnp.tile(bias_grid, (1, 1, 1, GROUP))
    wqkv, wp = padded_weights(w_qkv, w_proj, heads)
    scale = (channels // heads) ** (-0.5)
    whole = lambda shape: pl.BlockSpec(shape, lambda g: (0,) * len(shape))
    out = pl.pallas_call(
        functools.partial(block_kernel, variants, heads, scale),
        out_shape=jax.ShapeDtypeStruct((variants, groups, tokens, channels), jnp.bfloat16),
        grid=(groups,),
        in_specs=[
            pl.BlockSpec((inputs, 1, tokens, channels), lambda g: (0, g, 0, 0)),
            pl.BlockSpec((1, tokens, 1), lambda g: (g, 0, 0)),
            pl.BlockSpec((1, 1, tokens), lambda g: (g, 0, 0)),
            whole(bias.shape),
            whole(wqkv.shape),
            whole(wp.shape),
            whole(w_up.shape),
            whole(w_down.shape),
        ],
        out_specs=pl.BlockSpec((variants, 1, tokens, channels), lambda g: (0, g, 0, 0)),
        compiler_params=pltpu.CompilerParams(vmem_limit_bytes=48 * 1024 * 1024),
    )(x, labq, labk, bias, wqkv, wp, w_up, w_down)
    out = out.reshape(variants, groups * GROUP, cells, channels)
    return out[:, :count]


def block_on_grid(tokens, region, w_qkv, w_proj, w_up, w_down, bias_grid):
    height, breadth = tokens.shape[1], tokens.shape[2]
    windows = to_windows(tokens)
    region_windows = to_windows(region[None, :, :, None])[0, :, :, 0]
    out = swin_block(windows, region_windows, w_qkv, w_proj, w_up, w_down, bias_grid)
    return from_windows(out, height, breadth)


def normalize(values):
    values = values.astype(jnp.float32)
    average = jnp.mean(values, axis=-1, keepdims=True)
    centred = values - average
    spread = jnp.mean(centred * centred, axis=-1, keepdims=True)
    return centred * lax.rsqrt(spread + EPSILON)


def to_windows(grid):
    leading, height, breadth, channels = grid.shape
    grid = grid.reshape(leading, height // WIN, WIN, breadth // WIN, WIN, channels)
    grid = grid.transpose(0, 1, 3, 2, 4, 5)
    return grid.reshape(leading, height // WIN * (breadth // WIN), WIN * WIN, channels)


def from_windows(windows, height, breadth):
    leading, window_count, cells, channels = windows.shape
    windows = windows.reshape(leading, height // WIN, breadth // WIN, WIN, WIN, channels)
    windows = windows.transpose(0, 1, 3, 2, 4, 5)
    return windows.reshape(leading, height, breadth, channels)


def bias_table(offset_table, variant_codes):
    position = jnp.arange(WIN * WIN, dtype=jnp.int32)
    row_step = (position // WIN)[:, None] - (position // WIN)[None, :]
    across = (position % WIN)[:, None] - (position % WIN)[None, :]
    transpose_bit = (variant_codes // 4)[:, None, None]
    flip_rows = (variant_codes // 2 % 2)[:, None, None]
    flip_cols = (variant_codes % 2)[:, None, None]
    row_moved = jnp.where(flip_rows == 1, -row_step, row_step)
    col_moved = jnp.where(flip_cols == 1, -across, across)
    leading_step = jnp.where(transpose_bit == 1, col_moved, row_moved)
    trailing_step = jnp.where(transpose_bit == 1, row_moved, col_moved)
    table_index = (leading_step + WIN - 1) * (2 * WIN - 1) + trailing_step + WIN - 1
    slots = jnp.arange((2 * WIN - 1) * (2 * WIN - 1), dtype=jnp.int32)
    one_hot = (table_index[..., None] == slots).astype(jnp.float32)
    return jnp.einsum("vqkt,ht->vhqk", one_hot, offset_table, precision=lax.Precision.HIGHEST)


def toeplitz_bias(offset_table, variant_codes):
    side = 2 * WIN - 1
    table = offset_table.reshape(offset_table.shape[0], side, side)
    transpose_bit = (variant_codes // 4)[:, None, None, None]
    flip_rows = (variant_codes // 2 % 2)[:, None, None, None]
    flip_cols = (variant_codes % 2)[:, None, None, None]
    moved = jnp.where(transpose_bit == 1, jnp.swapaxes(table, 1, 2)[None], table[None])
    moved = jnp.where(flip_rows == 1, jnp.flip(moved, 2), moved)
    moved = jnp.where(flip_cols == 1, jnp.flip(moved, 3), moved)
    rows = jnp.stack([moved[:, :, WIN - 1 - k : side - k] for k in range(WIN)], axis=3)
    full = jnp.stack([rows[..., WIN - 1 - k : side - k] for k in range(WIN)], axis=-1)
    full = full.transpose(0, 1, 2, 4, 3, 5)
    return full.reshape(full.shape[0], full.shape[1], WIN * WIN, WIN * WIN)


def variant_kernels(kernel, variant_codes):
    transpose_bit = (variant_codes // 4)[:, None]
    flip_rows = (variant_codes // 2 % 2)[:, None]
    flip_cols = (variant_codes % 2)[:, None]
    kernel_spot = jnp.arange(9, dtype=jnp.int32)
    step_row = (kernel_spot // 3 - 1)[None, :]
    step_col = (kernel_spot % 3 - 1)[None, :]
    row_moved = jnp.where(flip_rows == 1, -step_row, step_row)
    col_moved = jnp.where(flip_cols == 1, -step_col, step_col)
    source_row = jnp.where(transpose_bit == 1, col_moved, row_moved)
    source_col = jnp.where(transpose_bit == 1, row_moved, col_moved)
    source = (source_row + 1) * 3 + source_col + 1
    pick_place = (source[:, :, None] == kernel_spot[None, None, :]).astype(jnp.bfloat16)
    channel = jnp.arange(kernel.shape[-1], dtype=jnp.int32)
    colour = (channel // (SCALE * SCALE))[None, :]
    sub_row = (channel % (SCALE * SCALE) // SCALE)[None, :]
    sub_col = (channel % SCALE)[None, :]
    sub_row_moved = jnp.where(flip_rows == 1, SCALE - 1 - sub_row, sub_row)
    sub_col_moved = jnp.where(flip_cols == 1, SCALE - 1 - sub_col, sub_col)
    anchor_row = jnp.where(transpose_bit == 1, sub_col_moved, sub_row_moved)
    anchor_col = jnp.where(transpose_bit == 1, sub_row_moved, sub_col_moved)
    anchor = colour * SCALE * SCALE + anchor_row * SCALE + anchor_col
    pick_channel = (channel[None, :, None] == anchor[:, None, :]).astype(jnp.bfloat16)
    placed = jnp.einsum(
        "vpq,qcs->vpcs", pick_place, kernel, preferred_element_type=jnp.float32
    ).astype(jnp.bfloat16)
    return jnp.einsum(
        "vpcs,vso->vpco", placed, pick_channel, preferred_element_type=jnp.float32
    ).astype(jnp.bfloat16)


def attend(normed, region, w_qkv, w_proj, bias_grid):
    head_count = bias_grid.shape[1]
    leading, window_count, cells, channels = normed.shape
    head_width = channels // head_count
    projected = jnp.einsum(
        "lnsc,ce->lnse", normed, w_qkv, preferred_element_type=jnp.float32
    ).astype(jnp.bfloat16)
    projected = projected.reshape(leading, window_count, cells, 3, head_count, head_width)
    queries = projected[:, :, :, 0]
    key_part = projected[:, :, :, 1]
    value_part = projected[:, :, :, 2]
    scores = jnp.einsum("lnqhd,lnkhd->lnhqk", queries, key_part, preferred_element_type=jnp.float32)
    scores = scores * head_width ** (-0.5) + bias_grid[:, None]
    matches = region[:, None, :, None] == region[:, None, None, :]
    scores = jnp.where(matches[None], scores, MASKED)
    largest = jnp.max(scores, axis=-1, keepdims=True)
    weights = jnp.exp(scores - largest)
    probabilities = (weights / jnp.sum(weights, axis=-1, keepdims=True)).astype(jnp.bfloat16)
    value_part = jnp.broadcast_to(value_part, (probabilities.shape[0],) + value_part.shape[1:])
    mixed = jnp.einsum(
        "lnhqk,lnkhd->lnqhd", probabilities, value_part, preferred_element_type=jnp.float32
    ).astype(jnp.bfloat16)
    mixed = mixed.reshape(probabilities.shape[0], window_count, cells, channels)
    return jnp.einsum("lnsc,ce->lnse", mixed, w_proj, preferred_element_type=jnp.float32)


def attention_half(tokens, region, w_qkv, w_proj, bias_grid):
    height, breadth = (tokens.shape[1], tokens.shape[2])
    windows = to_windows(tokens)
    region_windows = to_windows(region[None, :, :, None])[0, :, :, 0]
    normed = normalize(windows).astype(jnp.bfloat16)
    branch = attend(normed, region_windows, w_qkv, w_proj, bias_grid)
    result = (windows.astype(jnp.float32) + branch).astype(jnp.bfloat16)
    return from_windows(result, height, breadth)


def feed_forward(tokens, w_up, w_down):
    normed = normalize(tokens).astype(jnp.bfloat16)
    hidden = jnp.einsum("...c,ce->...e", normed, w_up, preferred_element_type=jnp.float32)
    hidden = jax.nn.gelu(hidden, approximate=False).astype(jnp.bfloat16)
    output = tokens.astype(jnp.float32) + jnp.einsum(
        "...e,ec->...c", hidden, w_down, preferred_element_type=jnp.float32
    )
    return output.astype(jnp.bfloat16)


def reconstruct(padded, kernels, height, breadth):
    accumulated = jnp.zeros((padded.shape[0], height, breadth, kernels.shape[-1]), jnp.float32)
    for kernel_spot in range(9):
        spot_row, spot_col = (kernel_spot // 3, kernel_spot % 3)
        window = padded[:, spot_row : spot_row + height, spot_col : spot_col + breadth]
        accumulated = accumulated + jnp.einsum(
            "vrcd,vde->vrce", window, kernels[:, kernel_spot], preferred_element_type=jnp.float32
        )
    return accumulated


def refine(average, region, w_qkv, w_proj, bias_grid):
    normed = normalize(average).astype(jnp.bfloat16)[None]
    return average + attend(normed, region, w_qkv, w_proj, bias_grid)[0]


def local(
    features,
    labels,
    qkv_weight,
    proj_weight,
    up_weight,
    down_weight,
    swin_bias,
    recon_weight,
    refine_qkv,
    refine_proj,
    refine_bias,
):
    height, breadth, channels = features.shape
    variant_codes = lax.axis_index("var") * VAR_DEV + jnp.arange(VAR_DEV, dtype=jnp.int32)
    first_bias = toeplitz_bias(swin_bias[0], variant_codes)
    second_bias = toeplitz_bias(swin_bias[1], variant_codes)
    region = extended(labels, (("ty", 0), ("tx", 1)), SHIFT)
    block_one = block_on_grid(
        features[None], labels, qkv_weight[0], proj_weight[0], up_weight[0], down_weight[0], first_bias
    )
    shifted = extended(block_one, (("ty", 1), ("tx", 2)), SHIFT)
    block_two = block_on_grid(
        shifted, region, qkv_weight[1], proj_weight[1], up_weight[1], down_weight[1], second_bias
    )
    padded = block_two[:, SHIFT - 1 : SHIFT + height + 1, SHIFT - 1 : SHIFT + breadth + 1]
    row = lax.axis_index("ty") * height - 1 + jnp.arange(height + 2)
    col = lax.axis_index("tx") * breadth - 1 + jnp.arange(breadth + 2)
    inside = ((row >= 0) & (row < lax.axis_size("ty") * height))[:, None] & (
        (col >= 0) & (col < lax.axis_size("tx") * breadth)
    )[None, :]
    padded = jnp.where(inside[None, :, :, None], padded, jnp.zeros_like(padded))
    kernels = variant_kernels(recon_weight, variant_codes)
    summed = jnp.sum(reconstruct(padded, kernels, height, breadth), axis=0)
    region_windows = to_windows(labels[None, :, :, None])[0, :, :, 0]
    refine_grid = toeplitz_bias(refine_bias, jnp.zeros((1,), jnp.int32))
    rows, cols, depth = summed.shape
    combined = var_sum(summed.astype(jnp.bfloat16).reshape(rows, cols * depth)).reshape(rows, cols, depth)
    refined = refine(
        to_windows(combined[None])[0] / 8.0, region_windows, refine_qkv, refine_proj, refine_grid
    )
    colours = refined.shape[-1] // (SCALE * SCALE)
    picture = refined.reshape(
        height // WIN, breadth // WIN, WIN, WIN, colours * SCALE, SCALE
    ).transpose(4, 0, 2, 1, 3, 5)
    picture = picture.reshape(colours, SCALE, height, breadth * SCALE).transpose(0, 2, 1, 3)
    return picture.reshape(colours, SCALE * height, SCALE * breadth)


def solution(mesh):
    placed = (P("ty", "tx", None), P("ty", "tx"), P(), P(), P(), P(), P(), P(), P(), P(), P())
    return jax.shard_map(
        local, mesh=mesh, in_specs=placed, out_specs=P(None, "ty", "tx"), check_vma=False
    )
```

```python
import functools

import jax
import jax.numpy as jnp
from jax import lax
from jax.experimental import pallas as pl
from jax.experimental.pallas import tpu as pltpu
from jax.sharding import PartitionSpec as P

MESH = pl.DeviceIdType.MESH

WIN = 8
SHIFT = 4
SCALE = 4
VAR_DEV = 2


EPSILON = 1e-05
MASKED = -1e30


def extended(cells, sides, width):
    for axis, dim in sides:
        count = lax.axis_size(axis)
        ends = count - 1
        head = lax.slice_in_dim(cells, 0, width, axis=dim)
        tail = lax.slice_in_dim(cells, cells.shape[dim] - width, cells.shape[dim], axis=dim)
        cells = jnp.concatenate(
            [
                lax.ppermute(tail, axis, [(i, (i + 1) % count) for i in range(ends)]),
                cells,
                lax.ppermute(head, axis, [((i + 1) % count, i) for i in range(ends)]),
            ],
            axis=dim,
        )
    return cells


def var_sum_kernel(count, part_ref, out_ref, held, send_sem, recv_sem, own_sem):
    me = lax.axis_index("var")
    barrier = pltpu.get_barrier_semaphore()
    for step in range(1, count):
        peer = lax.rem(me + step, count)
        pl.semaphore_signal(barrier, inc=1, device_id={"var": peer}, device_id_type=MESH)
    pl.semaphore_wait(barrier, count - 1)
    own = pltpu.make_async_copy(part_ref, held.at[me], own_sem)
    own.start()
    sends = []
    for step in range(1, count):
        peer = lax.rem(me + step, count)
        copy = pltpu.make_async_remote_copy(
            src_ref=part_ref,
            dst_ref=held.at[me],
            send_sem=send_sem.at[step - 1],
            recv_sem=recv_sem.at[me],
            device_id={"var": peer},
            device_id_type=MESH,
        )
        copy.start()
        sends.append(copy)
    own.wait()
    for copy in sends:
        copy.wait_send()
    for step in range(1, count):
        source = lax.rem(me + count - step, count)
        pltpu.make_async_remote_copy(
            src_ref=part_ref,
            dst_ref=held.at[source],
            send_sem=send_sem.at[step - 1],
            recv_sem=recv_sem.at[source],
            device_id={"var": source},
            device_id_type=MESH,
        ).wait_recv()
    total = held[0].astype(jnp.float32)
    for index in range(1, count):
        total = total + held[index].astype(jnp.float32)
    out_ref[...] = total


def var_sum(part):
    count = lax.axis_size("var")
    return pl.pallas_call(
        functools.partial(var_sum_kernel, count),
        out_shape=jax.ShapeDtypeStruct(part.shape, jnp.float32),
        in_specs=[pl.BlockSpec(memory_space=pltpu.VMEM)],
        out_specs=pl.BlockSpec(memory_space=pltpu.VMEM),
        scratch_shapes=[
            pltpu.VMEM((count,) + part.shape, part.dtype),
            pltpu.SemaphoreType.DMA((count - 1,)),
            pltpu.SemaphoreType.DMA((count,)),
            pltpu.SemaphoreType.DMA(()),
        ],
        compiler_params=pltpu.CompilerParams(collective_id=0, has_side_effects=True),
    )(part)


GROUP = 4
LANE = 128


def block_kernel(
    variants, heads, scale, x_ref, labq_ref, labk_ref, bias_ref, wqkv_ref, wp_ref, wup_ref, wdown_ref, out_ref
):
    inputs = x_ref.shape[0]
    tokens = x_ref.shape[2]
    labq = labq_ref[0]
    labk = labk_ref[0]
    slot_q = lax.broadcasted_iota(jnp.int32, (tokens, tokens), 0) // (WIN * WIN)
    slot_k = lax.broadcasted_iota(jnp.int32, (tokens, tokens), 1) // (WIN * WIN)
    match = (labq == labk) & (slot_q == slot_k)
    projected = []
    for index in range(inputs):
        normed = normalize(x_ref[index, 0]).astype(jnp.bfloat16)
        projected.append(
            jnp.dot(normed, wqkv_ref[...], preferred_element_type=jnp.float32).astype(jnp.bfloat16)
        )
    span = wp_ref.shape[0]
    width = wup_ref.shape[0] // heads
    lane = lax.broadcasted_iota(jnp.int32, (1, span), 1)
    for variant in range(variants):
        source = variant if inputs > 1 else 0
        qkv = projected[source]
        query = qkv[:, :span]
        key = qkv[:, span : 2 * span]
        value = qkv[:, 2 * span :]
        mixed = jnp.zeros((tokens, span), jnp.float32)
        for head in range(heads):
            mine = (lane >= head * width) & (lane < (head + 1) * width)
            scores = lax.dot_general(
                jnp.where(mine, query, jnp.zeros_like(query)),
                key,
                (((1,), (1,)), ((), ())),
                preferred_element_type=jnp.float32,
            )
            scores = scores * scale
            scores = (scores.reshape(GROUP, WIN * WIN, tokens) + bias_ref[variant, head][None]).reshape(
                tokens, tokens
            )
            scores = jnp.where(match, scores, MASKED)
            largest = jnp.max(scores, axis=-1, keepdims=True)
            weights = jnp.exp(scores - largest)
            probabilities = (weights / jnp.sum(weights, axis=-1, keepdims=True)).astype(jnp.bfloat16)
            mixed = mixed + jnp.dot(
                probabilities, jnp.where(mine, value, jnp.zeros_like(value)), preferred_element_type=jnp.float32
            )
        branch = jnp.dot(mixed.astype(jnp.bfloat16), wp_ref[...], preferred_element_type=jnp.float32)
        own = x_ref[source, 0].astype(jnp.float32)
        hidden_in = (own + branch).astype(jnp.bfloat16)
        normed = normalize(hidden_in).astype(jnp.bfloat16)
        hidden = jnp.dot(normed, wup_ref[...], preferred_element_type=jnp.float32)
        hidden = (0.5 * hidden * (1.0 + lax.erf(hidden * (2.0 ** -0.5)))).astype(jnp.bfloat16)
        result = hidden_in.astype(jnp.float32) + jnp.dot(
            hidden, wdown_ref[...], preferred_element_type=jnp.float32
        )
        out_ref[variant, 0] = result.astype(jnp.bfloat16)


def padded_weights(w_qkv, w_proj, heads):
    channels = w_proj.shape[0]
    span = -(-channels // LANE) * LANE
    columns = jnp.pad(w_qkv.reshape(channels, 3, channels), ((0, 0), (0, 0), (0, span - channels)))
    rows = jnp.pad(w_proj, ((0, span - channels), (0, 0)))
    return columns.reshape(channels, 3 * span), rows


def swin_block(windows, region, w_qkv, w_proj, w_up, w_down, bias_grid):
    inputs, count, cells, channels = windows.shape
    variants, heads = bias_grid.shape[:2]
    groups = -(-count // GROUP)
    extra = groups * GROUP - count
    windows = jnp.pad(windows, ((0, 0), (0, extra), (0, 0), (0, 0)))
    region = jnp.pad(region, ((0, extra), (0, 0)))
    tokens = GROUP * cells
    x = windows.reshape(inputs, groups, tokens, channels)
    labq = region.reshape(groups, tokens, 1)
    labk = region.reshape(groups, 1, tokens)
    bias = jnp.tile(bias_grid, (1, 1, 1, GROUP))
    wqkv, wp = padded_weights(w_qkv, w_proj, heads)
    scale = (channels // heads) ** (-0.5)
    whole = lambda shape: pl.BlockSpec(shape, lambda g: (0,) * len(shape))
    out = pl.pallas_call(
        functools.partial(block_kernel, variants, heads, scale),
        out_shape=jax.ShapeDtypeStruct((variants, groups, tokens, channels), jnp.bfloat16),
        grid=(groups,),
        in_specs=[
            pl.BlockSpec((inputs, 1, tokens, channels), lambda g: (0, g, 0, 0)),
            pl.BlockSpec((1, tokens, 1), lambda g: (g, 0, 0)),
            pl.BlockSpec((1, 1, tokens), lambda g: (g, 0, 0)),
            whole(bias.shape),
            whole(wqkv.shape),
            whole(wp.shape),
            whole(w_up.shape),
            whole(w_down.shape),
        ],
        out_specs=pl.BlockSpec((variants, 1, tokens, channels), lambda g: (0, g, 0, 0)),
        compiler_params=pltpu.CompilerParams(vmem_limit_bytes=48 * 1024 * 1024),
    )(x, labq, labk, bias, wqkv, wp, w_up, w_down)
    out = out.reshape(variants, groups * GROUP, cells, channels)
    return out[:, :count]


def block_on_grid(tokens, region, w_qkv, w_proj, w_up, w_down, bias_grid):
    height, breadth = tokens.shape[1], tokens.shape[2]
    windows = to_windows(tokens)
    region_windows = to_windows(region[None, :, :, None])[0, :, :, 0]
    out = swin_block(windows, region_windows, w_qkv, w_proj, w_up, w_down, bias_grid)
    return from_windows(out, height, breadth)


def normalize(values):
    values = values.astype(jnp.float32)
    average = jnp.mean(values, axis=-1, keepdims=True)
    centred = values - average
    spread = jnp.mean(centred * centred, axis=-1, keepdims=True)
    return centred * lax.rsqrt(spread + EPSILON)


def to_windows(grid):
    leading, height, breadth, channels = grid.shape
    grid = grid.reshape(leading, height // WIN, WIN, breadth // WIN, WIN, channels)
    grid = grid.transpose(0, 1, 3, 2, 4, 5)
    return grid.reshape(leading, height // WIN * (breadth // WIN), WIN * WIN, channels)


def from_windows(windows, height, breadth):
    leading, window_count, cells, channels = windows.shape
    windows = windows.reshape(leading, height // WIN, breadth // WIN, WIN, WIN, channels)
    windows = windows.transpose(0, 1, 3, 2, 4, 5)
    return windows.reshape(leading, height, breadth, channels)


def bias_table(offset_table, variant_codes):
    position = jnp.arange(WIN * WIN, dtype=jnp.int32)
    row_step = (position // WIN)[:, None] - (position // WIN)[None, :]
    across = (position % WIN)[:, None] - (position % WIN)[None, :]
    transpose_bit = (variant_codes // 4)[:, None, None]
    flip_rows = (variant_codes // 2 % 2)[:, None, None]
    flip_cols = (variant_codes % 2)[:, None, None]
    row_moved = jnp.where(flip_rows == 1, -row_step, row_step)
    col_moved = jnp.where(flip_cols == 1, -across, across)
    leading_step = jnp.where(transpose_bit == 1, col_moved, row_moved)
    trailing_step = jnp.where(transpose_bit == 1, row_moved, col_moved)
    table_index = (leading_step + WIN - 1) * (2 * WIN - 1) + trailing_step + WIN - 1
    slots = jnp.arange((2 * WIN - 1) * (2 * WIN - 1), dtype=jnp.int32)
    one_hot = (table_index[..., None] == slots).astype(jnp.bfloat16)
    high = lax.reduce_precision(offset_table, exponent_bits=8, mantissa_bits=7)
    rest = offset_table - high
    middle = lax.reduce_precision(rest, exponent_bits=8, mantissa_bits=7)
    low = rest - middle
    parts = jnp.concatenate([high, middle, low], axis=0).astype(jnp.bfloat16)
    picked = jnp.einsum("vqkt,ht->vhqk", one_hot, parts, preferred_element_type=jnp.float32)
    heads = offset_table.shape[0]
    return (picked[:, :heads] + picked[:, heads : 2 * heads]) + picked[:, 2 * heads :]


def variant_kernels(kernel, variant_codes):
    transpose_bit = (variant_codes // 4)[:, None]
    flip_rows = (variant_codes // 2 % 2)[:, None]
    flip_cols = (variant_codes % 2)[:, None]
    kernel_spot = jnp.arange(9, dtype=jnp.int32)
    step_row = (kernel_spot // 3 - 1)[None, :]
    step_col = (kernel_spot % 3 - 1)[None, :]
    row_moved = jnp.where(flip_rows == 1, -step_row, step_row)
    col_moved = jnp.where(flip_cols == 1, -step_col, step_col)
    source_row = jnp.where(transpose_bit == 1, col_moved, row_moved)
    source_col = jnp.where(transpose_bit == 1, row_moved, col_moved)
    source = (source_row + 1) * 3 + source_col + 1
    pick_place = (source[:, :, None] == kernel_spot[None, None, :]).astype(jnp.bfloat16)
    channel = jnp.arange(kernel.shape[-1], dtype=jnp.int32)
    colour = (channel // (SCALE * SCALE))[None, :]
    sub_row = (channel % (SCALE * SCALE) // SCALE)[None, :]
    sub_col = (channel % SCALE)[None, :]
    sub_row_moved = jnp.where(flip_rows == 1, SCALE - 1 - sub_row, sub_row)
    sub_col_moved = jnp.where(flip_cols == 1, SCALE - 1 - sub_col, sub_col)
    anchor_row = jnp.where(transpose_bit == 1, sub_col_moved, sub_row_moved)
    anchor_col = jnp.where(transpose_bit == 1, sub_row_moved, sub_col_moved)
    anchor = colour * SCALE * SCALE + anchor_row * SCALE + anchor_col
    pick_channel = (channel[None, :, None] == anchor[:, None, :]).astype(jnp.bfloat16)
    placed = jnp.einsum(
        "vpq,qcs->vpcs", pick_place, kernel, preferred_element_type=jnp.float32
    ).astype(jnp.bfloat16)
    return jnp.einsum(
        "vpcs,vso->vpco", placed, pick_channel, preferred_element_type=jnp.float32
    ).astype(jnp.bfloat16)


def attend(normed, region, w_qkv, w_proj, bias_grid):
    head_count = bias_grid.shape[1]
    leading, window_count, cells, channels = normed.shape
    head_width = channels // head_count
    projected = jnp.einsum(
        "lnsc,ce->lnse", normed, w_qkv, preferred_element_type=jnp.float32
    ).astype(jnp.bfloat16)
    projected = projected.reshape(leading, window_count, cells, 3, head_count, head_width)
    queries = projected[:, :, :, 0]
    key_part = projected[:, :, :, 1]
    value_part = projected[:, :, :, 2]
    scores = jnp.einsum("lnqhd,lnkhd->lnhqk", queries, key_part, preferred_element_type=jnp.float32)
    scores = scores * head_width ** (-0.5) + bias_grid[:, None]
    matches = region[:, None, :, None] == region[:, None, None, :]
    scores = jnp.where(matches[None], scores, MASKED)
    largest = jnp.max(scores, axis=-1, keepdims=True)
    weights = jnp.exp(scores - largest)
    probabilities = (weights / jnp.sum(weights, axis=-1, keepdims=True)).astype(jnp.bfloat16)
    value_part = jnp.broadcast_to(value_part, (probabilities.shape[0],) + value_part.shape[1:])
    mixed = jnp.einsum(
        "lnhqk,lnkhd->lnqhd", probabilities, value_part, preferred_element_type=jnp.float32
    ).astype(jnp.bfloat16)
    mixed = mixed.reshape(probabilities.shape[0], window_count, cells, channels)
    return jnp.einsum("lnsc,ce->lnse", mixed, w_proj, preferred_element_type=jnp.float32)


def attention_half(tokens, region, w_qkv, w_proj, bias_grid):
    height, breadth = (tokens.shape[1], tokens.shape[2])
    windows = to_windows(tokens)
    region_windows = to_windows(region[None, :, :, None])[0, :, :, 0]
    normed = normalize(windows).astype(jnp.bfloat16)
    branch = attend(normed, region_windows, w_qkv, w_proj, bias_grid)
    result = (windows.astype(jnp.float32) + branch).astype(jnp.bfloat16)
    return from_windows(result, height, breadth)


def feed_forward(tokens, w_up, w_down):
    normed = normalize(tokens).astype(jnp.bfloat16)
    hidden = jnp.einsum("...c,ce->...e", normed, w_up, preferred_element_type=jnp.float32)
    hidden = jax.nn.gelu(hidden, approximate=False).astype(jnp.bfloat16)
    output = tokens.astype(jnp.float32) + jnp.einsum(
        "...e,ec->...c", hidden, w_down, preferred_element_type=jnp.float32
    )
    return output.astype(jnp.bfloat16)


def reconstruct(padded, kernels, height, breadth):
    accumulated = jnp.zeros((padded.shape[0], height, breadth, kernels.shape[-1]), jnp.float32)
    for kernel_spot in range(9):
        spot_row, spot_col = (kernel_spot // 3, kernel_spot % 3)
        window = padded[:, spot_row : spot_row + height, spot_col : spot_col + breadth]
        accumulated = accumulated + jnp.einsum(
            "vrcd,vde->vrce", window, kernels[:, kernel_spot], preferred_element_type=jnp.float32
        )
    return accumulated


def refine(average, region, w_qkv, w_proj, bias_grid):
    normed = normalize(average).astype(jnp.bfloat16)[None]
    return average + attend(normed, region, w_qkv, w_proj, bias_grid)[0]


def local(
    features,
    labels,
    qkv_weight,
    proj_weight,
    up_weight,
    down_weight,
    swin_bias,
    recon_weight,
    refine_qkv,
    refine_proj,
    refine_bias,
):
    height, breadth, channels = features.shape
    variant_codes = lax.axis_index("var") * VAR_DEV + jnp.arange(VAR_DEV, dtype=jnp.int32)
    first_bias = bias_table(swin_bias[0], variant_codes)
    second_bias = bias_table(swin_bias[1], variant_codes)
    region = extended(labels, (("ty", 0), ("tx", 1)), SHIFT)
    block_one = block_on_grid(
        features[None], labels, qkv_weight[0], proj_weight[0], up_weight[0], down_weight[0], first_bias
    )
    shifted = extended(block_one, (("ty", 1), ("tx", 2)), SHIFT)
    block_two = block_on_grid(
        shifted, region, qkv_weight[1], proj_weight[1], up_weight[1], down_weight[1], second_bias
    )
    padded = block_two[:, SHIFT - 1 : SHIFT + height + 1, SHIFT - 1 : SHIFT + breadth + 1]
    row = lax.axis_index("ty") * height - 1 + jnp.arange(height + 2)
    col = lax.axis_index("tx") * breadth - 1 + jnp.arange(breadth + 2)
    inside = ((row >= 0) & (row < lax.axis_size("ty") * height))[:, None] & (
        (col >= 0) & (col < lax.axis_size("tx") * breadth)
    )[None, :]
    padded = jnp.where(inside[None, :, :, None], padded, jnp.zeros_like(padded))
    kernels = variant_kernels(recon_weight, variant_codes)
    summed = jnp.sum(reconstruct(padded, kernels, height, breadth), axis=0)
    region_windows = to_windows(labels[None, :, :, None])[0, :, :, 0]
    refine_grid = bias_table(refine_bias, jnp.zeros((1,), jnp.int32))
    rows, cols, depth = summed.shape
    combined = var_sum(summed.astype(jnp.bfloat16).reshape(rows, cols * depth)).reshape(rows, cols, depth)
    refined = refine(
        to_windows(combined[None])[0] / 8.0, region_windows, refine_qkv, refine_proj, refine_grid
    )
    refined = lax.optimization_barrier(refined)
    colours = refined.shape[-1] // (SCALE * SCALE)
    picture = refined.reshape(
        height // WIN, breadth // WIN, WIN, WIN, colours * SCALE, SCALE
    ).transpose(4, 0, 2, 1, 3, 5)
    picture = picture.reshape(colours, SCALE, height, breadth * SCALE).transpose(0, 2, 1, 3)
    return picture.reshape(colours, SCALE * height, SCALE * breadth)


def solution(mesh):
    placed = (P("ty", "tx", None), P("ty", "tx"), P(), P(), P(), P(), P(), P(), P(), P(), P())
    return jax.shard_map(
        local, mesh=mesh, in_specs=placed, out_specs=P(None, "ty", "tx"), check_vma=False
    )
```

```python
import functools

import jax
import jax.numpy as jnp
from jax import lax
from jax.experimental import pallas as pl
from jax.experimental.pallas import tpu as pltpu
from jax.sharding import PartitionSpec as P

MESH = pl.DeviceIdType.MESH

WIN = 8
SHIFT = 4
SCALE = 4
VAR_DEV = 2


EPSILON = 1e-05
MASKED = -1e30


def extended(cells, sides, width):
    for axis, dim in sides:
        count = lax.axis_size(axis)
        ends = count - 1
        head = lax.slice_in_dim(cells, 0, width, axis=dim)
        tail = lax.slice_in_dim(cells, cells.shape[dim] - width, cells.shape[dim], axis=dim)
        cells = jnp.concatenate(
            [
                lax.ppermute(tail, axis, [(i, (i + 1) % count) for i in range(ends)]),
                cells,
                lax.ppermute(head, axis, [((i + 1) % count, i) for i in range(ends)]),
            ],
            axis=dim,
        )
    return cells


def var_sum_kernel(count, part_ref, out_ref, held, send_sem, recv_sem, own_sem):
    me = lax.axis_index("var")
    barrier = pltpu.get_barrier_semaphore()
    for step in range(1, count):
        peer = lax.rem(me + step, count)
        pl.semaphore_signal(barrier, inc=1, device_id={"var": peer}, device_id_type=MESH)
    pl.semaphore_wait(barrier, count - 1)
    own = pltpu.make_async_copy(part_ref, held.at[me], own_sem)
    own.start()
    sends = []
    for step in range(1, count):
        peer = lax.rem(me + step, count)
        copy = pltpu.make_async_remote_copy(
            src_ref=part_ref,
            dst_ref=held.at[me],
            send_sem=send_sem.at[step - 1],
            recv_sem=recv_sem.at[me],
            device_id={"var": peer},
            device_id_type=MESH,
        )
        copy.start()
        sends.append(copy)
    own.wait()
    for copy in sends:
        copy.wait_send()
    for step in range(1, count):
        source = lax.rem(me + count - step, count)
        pltpu.make_async_remote_copy(
            src_ref=part_ref,
            dst_ref=held.at[source],
            send_sem=send_sem.at[step - 1],
            recv_sem=recv_sem.at[source],
            device_id={"var": source},
            device_id_type=MESH,
        ).wait_recv()
    total = held[0].astype(jnp.float32)
    for index in range(1, count):
        total = total + held[index].astype(jnp.float32)
    out_ref[...] = total


def var_sum(part):
    count = lax.axis_size("var")
    return pl.pallas_call(
        functools.partial(var_sum_kernel, count),
        out_shape=jax.ShapeDtypeStruct(part.shape, jnp.float32),
        in_specs=[pl.BlockSpec(memory_space=pltpu.VMEM)],
        out_specs=pl.BlockSpec(memory_space=pltpu.VMEM),
        scratch_shapes=[
            pltpu.VMEM((count,) + part.shape, part.dtype),
            pltpu.SemaphoreType.DMA((count - 1,)),
            pltpu.SemaphoreType.DMA((count,)),
            pltpu.SemaphoreType.DMA(()),
        ],
        compiler_params=pltpu.CompilerParams(collective_id=0, has_side_effects=True),
    )(part)


GROUP = 4
LANE = 128


def block_kernel(
    variants, heads, scale, x_ref, labq_ref, labk_ref, bias_ref, wqkv_ref, wp_ref, wup_ref, wdown_ref, out_ref
):
    inputs = x_ref.shape[0]
    tokens = x_ref.shape[2]
    labq = labq_ref[0]
    labk = labk_ref[0]
    slot_q = lax.broadcasted_iota(jnp.int32, (tokens, tokens), 0) // (WIN * WIN)
    slot_k = lax.broadcasted_iota(jnp.int32, (tokens, tokens), 1) // (WIN * WIN)
    match = (labq == labk) & (slot_q == slot_k)
    projected = []
    for index in range(inputs):
        normed = normalize(x_ref[index, 0]).astype(jnp.bfloat16)
        projected.append(
            jnp.dot(normed, wqkv_ref[...], preferred_element_type=jnp.float32).astype(jnp.bfloat16)
        )
    span = wp_ref.shape[0]
    width = wup_ref.shape[0] // heads
    lane = lax.broadcasted_iota(jnp.int32, (1, span), 1)
    for variant in range(variants):
        source = variant if inputs > 1 else 0
        qkv = projected[source]
        query = qkv[:, :span]
        key = qkv[:, span : 2 * span]
        value = qkv[:, 2 * span :]
        mixed = jnp.zeros((tokens, span), jnp.float32)
        for head in range(heads):
            mine = (lane >= head * width) & (lane < (head + 1) * width)
            scores = lax.dot_general(
                jnp.where(mine, query, jnp.zeros_like(query)),
                key,
                (((1,), (1,)), ((), ())),
                preferred_element_type=jnp.float32,
            )
            scores = scores * scale
            scores = (scores.reshape(GROUP, WIN * WIN, tokens) + bias_ref[variant, head][None]).reshape(
                tokens, tokens
            )
            scores = jnp.where(match, scores, MASKED)
            largest = jnp.max(scores, axis=-1, keepdims=True)
            weights = jnp.exp(scores - largest)
            probabilities = (weights / jnp.sum(weights, axis=-1, keepdims=True)).astype(jnp.bfloat16)
            mixed = mixed + jnp.dot(
                probabilities, jnp.where(mine, value, jnp.zeros_like(value)), preferred_element_type=jnp.float32
            )
        branch = jnp.dot(mixed.astype(jnp.bfloat16), wp_ref[...], preferred_element_type=jnp.float32)
        own = x_ref[source, 0].astype(jnp.float32)
        hidden_in = (own + branch).astype(jnp.bfloat16)
        normed = normalize(hidden_in).astype(jnp.bfloat16)
        hidden = jnp.dot(normed, wup_ref[...], preferred_element_type=jnp.float32)
        hidden = (0.5 * hidden * (1.0 + lax.erf(hidden * (2.0 ** -0.5)))).astype(jnp.bfloat16)
        result = hidden_in.astype(jnp.float32) + jnp.dot(
            hidden, wdown_ref[...], preferred_element_type=jnp.float32
        )
        out_ref[variant, 0] = result.astype(jnp.bfloat16)


def padded_weights(w_qkv, w_proj, heads):
    channels = w_proj.shape[0]
    span = -(-channels // LANE) * LANE
    columns = jnp.pad(w_qkv.reshape(channels, 3, channels), ((0, 0), (0, 0), (0, span - channels)))
    rows = jnp.pad(w_proj, ((0, span - channels), (0, 0)))
    return columns.reshape(channels, 3 * span), rows


def swin_block(windows, region, w_qkv, w_proj, w_up, w_down, bias_grid):
    inputs, count, cells, channels = windows.shape
    variants, heads = bias_grid.shape[:2]
    groups = -(-count // GROUP)
    extra = groups * GROUP - count
    windows = jnp.pad(windows, ((0, 0), (0, extra), (0, 0), (0, 0)))
    region = jnp.pad(region, ((0, extra), (0, 0)))
    tokens = GROUP * cells
    x = windows.reshape(inputs, groups, tokens, channels)
    labq = region.reshape(groups, tokens, 1)
    labk = region.reshape(groups, 1, tokens)
    bias = jnp.tile(bias_grid, (1, 1, 1, GROUP))
    wqkv, wp = padded_weights(w_qkv, w_proj, heads)
    scale = (channels // heads) ** (-0.5)
    whole = lambda shape: pl.BlockSpec(shape, lambda g: (0,) * len(shape))
    out = pl.pallas_call(
        functools.partial(block_kernel, variants, heads, scale),
        out_shape=jax.ShapeDtypeStruct((variants, groups, tokens, channels), jnp.bfloat16),
        grid=(groups,),
        in_specs=[
            pl.BlockSpec((inputs, 1, tokens, channels), lambda g: (0, g, 0, 0)),
            pl.BlockSpec((1, tokens, 1), lambda g: (g, 0, 0)),
            pl.BlockSpec((1, 1, tokens), lambda g: (g, 0, 0)),
            whole(bias.shape),
            whole(wqkv.shape),
            whole(wp.shape),
            whole(w_up.shape),
            whole(w_down.shape),
        ],
        out_specs=pl.BlockSpec((variants, 1, tokens, channels), lambda g: (0, g, 0, 0)),
        compiler_params=pltpu.CompilerParams(vmem_limit_bytes=48 * 1024 * 1024),
    )(x, labq, labk, bias, wqkv, wp, w_up, w_down)
    out = out.reshape(variants, groups * GROUP, cells, channels)
    return out[:, :count]


def block_on_grid(tokens, region, w_qkv, w_proj, w_up, w_down, bias_grid):
    height, breadth = tokens.shape[1], tokens.shape[2]
    windows = to_windows(tokens)
    region_windows = to_windows(region[None, :, :, None])[0, :, :, 0]
    out = swin_block(windows, region_windows, w_qkv, w_proj, w_up, w_down, bias_grid)
    return from_windows(out, height, breadth)


def normalize(values):
    values = values.astype(jnp.float32)
    average = jnp.mean(values, axis=-1, keepdims=True)
    centred = values - average
    spread = jnp.mean(centred * centred, axis=-1, keepdims=True)
    return centred * lax.rsqrt(spread + EPSILON)


def to_windows(grid):
    leading, height, breadth, channels = grid.shape
    grid = grid.reshape(leading, height // WIN, WIN, breadth // WIN, WIN, channels)
    grid = grid.transpose(0, 1, 3, 2, 4, 5)
    return grid.reshape(leading, height // WIN * (breadth // WIN), WIN * WIN, channels)


def from_windows(windows, height, breadth):
    leading, window_count, cells, channels = windows.shape
    windows = windows.reshape(leading, height // WIN, breadth // WIN, WIN, WIN, channels)
    windows = windows.transpose(0, 1, 3, 2, 4, 5)
    return windows.reshape(leading, height, breadth, channels)


def bias_table(offset_table, variant_codes):
    position = jnp.arange(WIN * WIN, dtype=jnp.int32)
    row_step = (position // WIN)[:, None] - (position // WIN)[None, :]
    across = (position % WIN)[:, None] - (position % WIN)[None, :]
    transpose_bit = (variant_codes // 4)[:, None, None]
    flip_rows = (variant_codes // 2 % 2)[:, None, None]
    flip_cols = (variant_codes % 2)[:, None, None]
    row_moved = jnp.where(flip_rows == 1, -row_step, row_step)
    col_moved = jnp.where(flip_cols == 1, -across, across)
    leading_step = jnp.where(transpose_bit == 1, col_moved, row_moved)
    trailing_step = jnp.where(transpose_bit == 1, row_moved, col_moved)
    table_index = (leading_step + WIN - 1) * (2 * WIN - 1) + trailing_step + WIN - 1
    slots = jnp.arange((2 * WIN - 1) * (2 * WIN - 1), dtype=jnp.int32)
    one_hot = (table_index[..., None] == slots).astype(jnp.bfloat16)
    high = lax.reduce_precision(offset_table, exponent_bits=8, mantissa_bits=7)
    rest = offset_table - high
    middle = lax.reduce_precision(rest, exponent_bits=8, mantissa_bits=7)
    low = rest - middle
    parts = jnp.concatenate([high, middle, low], axis=0).astype(jnp.bfloat16)
    picked = jnp.einsum("vqkt,ht->vhqk", one_hot, parts, preferred_element_type=jnp.float32)
    heads = offset_table.shape[0]
    return (picked[:, :heads] + picked[:, heads : 2 * heads]) + picked[:, 2 * heads :]


def variant_kernels(kernel, variant_codes):
    transpose_bit = (variant_codes // 4)[:, None]
    flip_rows = (variant_codes // 2 % 2)[:, None]
    flip_cols = (variant_codes % 2)[:, None]
    kernel_spot = jnp.arange(9, dtype=jnp.int32)
    step_row = (kernel_spot // 3 - 1)[None, :]
    step_col = (kernel_spot % 3 - 1)[None, :]
    row_moved = jnp.where(flip_rows == 1, -step_row, step_row)
    col_moved = jnp.where(flip_cols == 1, -step_col, step_col)
    source_row = jnp.where(transpose_bit == 1, col_moved, row_moved)
    source_col = jnp.where(transpose_bit == 1, row_moved, col_moved)
    source = (source_row + 1) * 3 + source_col + 1
    pick_place = (source[:, :, None] == kernel_spot[None, None, :]).astype(jnp.bfloat16)
    channel = jnp.arange(kernel.shape[-1], dtype=jnp.int32)
    colour = (channel // (SCALE * SCALE))[None, :]
    sub_row = (channel % (SCALE * SCALE) // SCALE)[None, :]
    sub_col = (channel % SCALE)[None, :]
    sub_row_moved = jnp.where(flip_rows == 1, SCALE - 1 - sub_row, sub_row)
    sub_col_moved = jnp.where(flip_cols == 1, SCALE - 1 - sub_col, sub_col)
    anchor_row = jnp.where(transpose_bit == 1, sub_col_moved, sub_row_moved)
    anchor_col = jnp.where(transpose_bit == 1, sub_row_moved, sub_col_moved)
    anchor = colour * SCALE * SCALE + anchor_row * SCALE + anchor_col
    pick_channel = (channel[None, :, None] == anchor[:, None, :]).astype(jnp.bfloat16)
    placed = jnp.einsum(
        "vpq,qcs->vpcs", pick_place, kernel, preferred_element_type=jnp.float32
    ).astype(jnp.bfloat16)
    return jnp.einsum(
        "vpcs,vso->vpco", placed, pick_channel, preferred_element_type=jnp.float32
    ).astype(jnp.bfloat16)


def attend(normed, region, w_qkv, w_proj, bias_grid):
    head_count = bias_grid.shape[1]
    leading, window_count, cells, channels = normed.shape
    head_width = channels // head_count
    projected = jnp.einsum(
        "lnsc,ce->lnse", normed, w_qkv, preferred_element_type=jnp.float32
    ).astype(jnp.bfloat16)
    projected = projected.reshape(leading, window_count, cells, 3, head_count, head_width)
    queries = projected[:, :, :, 0]
    key_part = projected[:, :, :, 1]
    value_part = projected[:, :, :, 2]
    scores = jnp.einsum("lnqhd,lnkhd->lnhqk", queries, key_part, preferred_element_type=jnp.float32)
    scores = scores * head_width ** (-0.5) + bias_grid[:, None]
    matches = region[:, None, :, None] == region[:, None, None, :]
    scores = jnp.where(matches[None], scores, MASKED)
    largest = jnp.max(scores, axis=-1, keepdims=True)
    weights = jnp.exp(scores - largest)
    probabilities = (weights / jnp.sum(weights, axis=-1, keepdims=True)).astype(jnp.bfloat16)
    value_part = jnp.broadcast_to(value_part, (probabilities.shape[0],) + value_part.shape[1:])
    mixed = jnp.einsum(
        "lnhqk,lnkhd->lnqhd", probabilities, value_part, preferred_element_type=jnp.float32
    ).astype(jnp.bfloat16)
    mixed = mixed.reshape(probabilities.shape[0], window_count, cells, channels)
    return jnp.einsum("lnsc,ce->lnse", mixed, w_proj, preferred_element_type=jnp.float32)


def attention_half(tokens, region, w_qkv, w_proj, bias_grid):
    height, breadth = (tokens.shape[1], tokens.shape[2])
    windows = to_windows(tokens)
    region_windows = to_windows(region[None, :, :, None])[0, :, :, 0]
    normed = normalize(windows).astype(jnp.bfloat16)
    branch = attend(normed, region_windows, w_qkv, w_proj, bias_grid)
    result = (windows.astype(jnp.float32) + branch).astype(jnp.bfloat16)
    return from_windows(result, height, breadth)


def feed_forward(tokens, w_up, w_down):
    normed = normalize(tokens).astype(jnp.bfloat16)
    hidden = jnp.einsum("...c,ce->...e", normed, w_up, preferred_element_type=jnp.float32)
    hidden = jax.nn.gelu(hidden, approximate=False).astype(jnp.bfloat16)
    output = tokens.astype(jnp.float32) + jnp.einsum(
        "...e,ec->...c", hidden, w_down, preferred_element_type=jnp.float32
    )
    return output.astype(jnp.bfloat16)


def reconstruct(padded, kernels, height, breadth):
    accumulated = jnp.zeros((padded.shape[0], height, breadth, kernels.shape[-1]), jnp.float32)
    for kernel_spot in range(9):
        spot_row, spot_col = (kernel_spot // 3, kernel_spot % 3)
        window = padded[:, spot_row : spot_row + height, spot_col : spot_col + breadth]
        accumulated = accumulated + jnp.einsum(
            "vrcd,vde->vrce", window, kernels[:, kernel_spot], preferred_element_type=jnp.float32
        )
    return accumulated


def refine(average, region, w_qkv, w_proj, bias_grid):
    normed = normalize(average).astype(jnp.bfloat16)[None]
    return average + attend(normed, region, w_qkv, w_proj, bias_grid)[0]


def local(
    features,
    labels,
    qkv_weight,
    proj_weight,
    up_weight,
    down_weight,
    swin_bias,
    recon_weight,
    refine_qkv,
    refine_proj,
    refine_bias,
):
    height, breadth, channels = features.shape
    variant_codes = lax.axis_index("var") * VAR_DEV + jnp.arange(VAR_DEV, dtype=jnp.int32)
    first_bias = bias_table(swin_bias[0], variant_codes)
    second_bias = bias_table(swin_bias[1], variant_codes)
    block_one = block_on_grid(
        features[None], labels, qkv_weight[0], proj_weight[0], up_weight[0], down_weight[0], first_bias
    )
    tagged = jnp.broadcast_to(labels.astype(jnp.bfloat16)[None, :, :, None], block_one.shape[:3] + (1,))
    carried = extended(jnp.concatenate([block_one, tagged], axis=-1), (("ty", 1), ("tx", 2)), SHIFT)
    shifted = carried[..., :channels]
    region = carried[0, :, :, channels].astype(jnp.int32)
    block_two = block_on_grid(
        shifted, region, qkv_weight[1], proj_weight[1], up_weight[1], down_weight[1], second_bias
    )
    padded = block_two[:, SHIFT - 1 : SHIFT + height + 1, SHIFT - 1 : SHIFT + breadth + 1]
    row = lax.axis_index("ty") * height - 1 + jnp.arange(height + 2)
    col = lax.axis_index("tx") * breadth - 1 + jnp.arange(breadth + 2)
    inside = ((row >= 0) & (row < lax.axis_size("ty") * height))[:, None] & (
        (col >= 0) & (col < lax.axis_size("tx") * breadth)
    )[None, :]
    padded = jnp.where(inside[None, :, :, None], padded, jnp.zeros_like(padded))
    kernels = variant_kernels(recon_weight, variant_codes)
    summed = jnp.sum(reconstruct(padded, kernels, height, breadth), axis=0)
    region_windows = to_windows(labels[None, :, :, None])[0, :, :, 0]
    refine_grid = bias_table(refine_bias, jnp.zeros((1,), jnp.int32))
    rows, cols, depth = summed.shape
    combined = var_sum(summed.astype(jnp.bfloat16).reshape(rows, cols * depth)).reshape(rows, cols, depth)
    refined = refine(
        to_windows(combined[None])[0] / 8.0, region_windows, refine_qkv, refine_proj, refine_grid
    )
    refined = lax.optimization_barrier(refined)
    colours = refined.shape[-1] // (SCALE * SCALE)
    picture = refined.reshape(
        height // WIN, breadth // WIN, WIN, WIN, colours * SCALE, SCALE
    ).transpose(4, 0, 2, 1, 3, 5)
    picture = picture.reshape(colours, SCALE, height, breadth * SCALE).transpose(0, 2, 1, 3)
    return picture.reshape(colours, SCALE * height, SCALE * breadth)


def solution(mesh):
    placed = (P("ty", "tx", None), P("ty", "tx"), P(), P(), P(), P(), P(), P(), P(), P(), P())
    return jax.shard_map(
        local, mesh=mesh, in_specs=placed, out_specs=P(None, "ty", "tx"), check_vma=False
    )
```

```python
import functools

import jax
import jax.numpy as jnp
from jax import lax
from jax.experimental import pallas as pl
from jax.experimental.pallas import tpu as pltpu
from jax.sharding import PartitionSpec as P

MESH = pl.DeviceIdType.MESH

WIN = 8
SHIFT = 4
SCALE = 4
VAR_DEV = 2


EPSILON = 1e-05
MASKED = -1e30


def extended(cells, sides, width):
    for axis, dim in sides:
        count = lax.axis_size(axis)
        ends = count - 1
        head = lax.slice_in_dim(cells, 0, width, axis=dim)
        tail = lax.slice_in_dim(cells, cells.shape[dim] - width, cells.shape[dim], axis=dim)
        cells = jnp.concatenate(
            [
                lax.ppermute(tail, axis, [(i, (i + 1) % count) for i in range(ends)]),
                cells,
                lax.ppermute(head, axis, [((i + 1) % count, i) for i in range(ends)]),
            ],
            axis=dim,
        )
    return cells


def var_sum_kernel(count, part_ref, out_ref, held, send_sem, recv_sem, own_sem):
    me = lax.axis_index("var")
    barrier = pltpu.get_barrier_semaphore()
    for step in range(1, count):
        peer = lax.rem(me + step, count)
        pl.semaphore_signal(barrier, inc=1, device_id={"var": peer}, device_id_type=MESH)
    pl.semaphore_wait(barrier, count - 1)
    own = pltpu.make_async_copy(part_ref, held.at[me], own_sem)
    own.start()
    sends = []
    for step in range(1, count):
        peer = lax.rem(me + step, count)
        copy = pltpu.make_async_remote_copy(
            src_ref=part_ref,
            dst_ref=held.at[me],
            send_sem=send_sem.at[step - 1],
            recv_sem=recv_sem.at[me],
            device_id={"var": peer},
            device_id_type=MESH,
        )
        copy.start()
        sends.append(copy)
    own.wait()
    for copy in sends:
        copy.wait_send()
    for step in range(1, count):
        source = lax.rem(me + count - step, count)
        pltpu.make_async_remote_copy(
            src_ref=part_ref,
            dst_ref=held.at[source],
            send_sem=send_sem.at[step - 1],
            recv_sem=recv_sem.at[source],
            device_id={"var": source},
            device_id_type=MESH,
        ).wait_recv()
    total = held[0].astype(jnp.float32)
    for index in range(1, count):
        total = total + held[index].astype(jnp.float32)
    out_ref[...] = total


def var_sum(part):
    count = lax.axis_size("var")
    return pl.pallas_call(
        functools.partial(var_sum_kernel, count),
        out_shape=jax.ShapeDtypeStruct(part.shape, jnp.float32),
        in_specs=[pl.BlockSpec(memory_space=pltpu.VMEM)],
        out_specs=pl.BlockSpec(memory_space=pltpu.VMEM),
        scratch_shapes=[
            pltpu.VMEM((count,) + part.shape, part.dtype),
            pltpu.SemaphoreType.DMA((count - 1,)),
            pltpu.SemaphoreType.DMA((count,)),
            pltpu.SemaphoreType.DMA(()),
        ],
        compiler_params=pltpu.CompilerParams(collective_id=0, has_side_effects=True),
    )(part)


GROUP = 4
LANE = 128


def block_kernel(
    variants, heads, scale, x_ref, labq_ref, labk_ref, bias_ref, wqkv_ref, wp_ref, wup_ref, wdown_ref, out_ref
):
    inputs = x_ref.shape[0]
    tokens = x_ref.shape[2]
    labq = labq_ref[0]
    labk = labk_ref[0]
    slot_q = lax.broadcasted_iota(jnp.int32, (tokens, tokens), 0) // (WIN * WIN)
    slot_k = lax.broadcasted_iota(jnp.int32, (tokens, tokens), 1) // (WIN * WIN)
    match = (labq == labk) & (slot_q == slot_k)
    projected = []
    for index in range(inputs):
        normed = normalize(x_ref[index, 0]).astype(jnp.bfloat16)
        projected.append(
            jnp.dot(normed, wqkv_ref[...], preferred_element_type=jnp.float32).astype(jnp.bfloat16)
        )
    span = wp_ref.shape[0]
    width = wup_ref.shape[0] // heads
    lane = lax.broadcasted_iota(jnp.int32, (1, span), 1)
    for variant in range(variants):
        source = variant if inputs > 1 else 0
        qkv = projected[source]
        query = qkv[:, :span]
        key = qkv[:, span : 2 * span]
        value = qkv[:, 2 * span :]
        mixed = jnp.zeros((tokens, span), jnp.float32)
        for head in range(heads):
            mine = (lane >= head * width) & (lane < (head + 1) * width)
            scores = lax.dot_general(
                jnp.where(mine, query, jnp.zeros_like(query)),
                key,
                (((1,), (1,)), ((), ())),
                preferred_element_type=jnp.float32,
            )
            scores = scores * scale
            scores = (scores.reshape(GROUP, WIN * WIN, tokens) + bias_ref[variant, head][None]).reshape(
                tokens, tokens
            )
            scores = jnp.where(match, scores, MASKED)
            largest = jnp.max(scores, axis=-1, keepdims=True)
            weights = jnp.exp(scores - largest)
            probabilities = (weights / jnp.sum(weights, axis=-1, keepdims=True)).astype(jnp.bfloat16)
            mixed = mixed + jnp.dot(
                probabilities, jnp.where(mine, value, jnp.zeros_like(value)), preferred_element_type=jnp.float32
            )
        branch = jnp.dot(mixed.astype(jnp.bfloat16), wp_ref[...], preferred_element_type=jnp.float32)
        own = x_ref[source, 0].astype(jnp.float32)
        hidden_in = (own + branch).astype(jnp.bfloat16)
        normed = normalize(hidden_in).astype(jnp.bfloat16)
        hidden = jnp.dot(normed, wup_ref[...], preferred_element_type=jnp.float32)
        hidden = (0.5 * hidden * (1.0 + lax.erf(hidden * (2.0 ** -0.5)))).astype(jnp.bfloat16)
        result = hidden_in.astype(jnp.float32) + jnp.dot(
            hidden, wdown_ref[...], preferred_element_type=jnp.float32
        )
        out_ref[variant, 0] = result.astype(jnp.bfloat16)


def padded_weights(w_qkv, w_proj, heads):
    channels = w_proj.shape[0]
    span = -(-channels // LANE) * LANE
    columns = jnp.pad(w_qkv.reshape(channels, 3, channels), ((0, 0), (0, 0), (0, span - channels)))
    rows = jnp.pad(w_proj, ((0, span - channels), (0, 0)))
    return columns.reshape(channels, 3 * span), rows


def swin_block(windows, region, layer, w_qkv, w_proj, w_up, w_down, bias_grid):
    inputs, count, cells, channels = windows.shape
    variants, heads = bias_grid.shape[:2]
    groups = -(-count // GROUP)
    extra = groups * GROUP - count
    windows = jnp.pad(windows, ((0, 0), (0, extra), (0, 0), (0, 0)))
    region = jnp.pad(region, ((0, extra), (0, 0)))
    tokens = GROUP * cells
    x = windows.reshape(inputs, groups, tokens, channels)
    labq = region.reshape(groups, tokens, 1)
    labk = region.reshape(groups, 1, tokens)
    bias = jnp.tile(bias_grid, (1, 1, 1, GROUP))
    scale = (channels // heads) ** (-0.5)
    whole = lambda shape: pl.BlockSpec(shape, lambda g: (0,) * len(shape))
    out = pl.pallas_call(
        functools.partial(block_kernel, variants, heads, scale),
        out_shape=jax.ShapeDtypeStruct((variants, groups, tokens, channels), jnp.bfloat16),
        grid=(groups,),
        in_specs=[
            pl.BlockSpec((inputs, 1, tokens, channels), lambda g: (0, g, 0, 0)),
            pl.BlockSpec((1, tokens, 1), lambda g: (g, 0, 0)),
            pl.BlockSpec((1, 1, tokens), lambda g: (g, 0, 0)),
            whole(bias.shape),
            pl.BlockSpec((None,) + w_qkv.shape[1:], lambda g: (layer, 0, 0)),
            pl.BlockSpec((None,) + w_proj.shape[1:], lambda g: (layer, 0, 0)),
            pl.BlockSpec((None,) + w_up.shape[1:], lambda g: (layer, 0, 0)),
            pl.BlockSpec((None,) + w_down.shape[1:], lambda g: (layer, 0, 0)),
        ],
        out_specs=pl.BlockSpec((variants, 1, tokens, channels), lambda g: (0, g, 0, 0)),
        compiler_params=pltpu.CompilerParams(vmem_limit_bytes=48 * 1024 * 1024),
    )(x, labq, labk, bias, w_qkv, w_proj, w_up, w_down)
    out = out.reshape(variants, groups * GROUP, cells, channels)
    return out[:, :count]


def block_on_grid(tokens, region, layer, w_qkv, w_proj, w_up, w_down, bias_grid):
    height, breadth = tokens.shape[1], tokens.shape[2]
    windows = to_windows(tokens)
    region_windows = to_windows(region[None, :, :, None])[0, :, :, 0]
    out = swin_block(windows, region_windows, layer, w_qkv, w_proj, w_up, w_down, bias_grid)
    return from_windows(out, height, breadth)


def normalize(values):
    values = values.astype(jnp.float32)
    average = jnp.mean(values, axis=-1, keepdims=True)
    centred = values - average
    spread = jnp.mean(centred * centred, axis=-1, keepdims=True)
    return centred * lax.rsqrt(spread + EPSILON)


def to_windows(grid):
    leading, height, breadth, channels = grid.shape
    grid = grid.reshape(leading, height // WIN, WIN, breadth // WIN, WIN, channels)
    grid = grid.transpose(0, 1, 3, 2, 4, 5)
    return grid.reshape(leading, height // WIN * (breadth // WIN), WIN * WIN, channels)


def from_windows(windows, height, breadth):
    leading, window_count, cells, channels = windows.shape
    windows = windows.reshape(leading, height // WIN, breadth // WIN, WIN, WIN, channels)
    windows = windows.transpose(0, 1, 3, 2, 4, 5)
    return windows.reshape(leading, height, breadth, channels)


def bias_table(offset_table, variant_codes):
    position = jnp.arange(WIN * WIN, dtype=jnp.int32)
    row_step = (position // WIN)[:, None] - (position // WIN)[None, :]
    across = (position % WIN)[:, None] - (position % WIN)[None, :]
    transpose_bit = (variant_codes // 4)[:, None, None]
    flip_rows = (variant_codes // 2 % 2)[:, None, None]
    flip_cols = (variant_codes % 2)[:, None, None]
    row_moved = jnp.where(flip_rows == 1, -row_step, row_step)
    col_moved = jnp.where(flip_cols == 1, -across, across)
    leading_step = jnp.where(transpose_bit == 1, col_moved, row_moved)
    trailing_step = jnp.where(transpose_bit == 1, row_moved, col_moved)
    table_index = (leading_step + WIN - 1) * (2 * WIN - 1) + trailing_step + WIN - 1
    slots = jnp.arange((2 * WIN - 1) * (2 * WIN - 1), dtype=jnp.int32)
    one_hot = (table_index[..., None] == slots).astype(jnp.bfloat16)
    high = lax.reduce_precision(offset_table, exponent_bits=8, mantissa_bits=7)
    rest = offset_table - high
    middle = lax.reduce_precision(rest, exponent_bits=8, mantissa_bits=7)
    low = rest - middle
    parts = jnp.concatenate([high, middle, low], axis=0).astype(jnp.bfloat16)
    picked = jnp.einsum("vqkt,ht->vhqk", one_hot, parts, preferred_element_type=jnp.float32)
    heads = offset_table.shape[0]
    return (picked[:, :heads] + picked[:, heads : 2 * heads]) + picked[:, 2 * heads :]


def variant_kernels(kernel, variant_codes):
    transpose_bit = (variant_codes // 4)[:, None]
    flip_rows = (variant_codes // 2 % 2)[:, None]
    flip_cols = (variant_codes % 2)[:, None]
    kernel_spot = jnp.arange(9, dtype=jnp.int32)
    step_row = (kernel_spot // 3 - 1)[None, :]
    step_col = (kernel_spot % 3 - 1)[None, :]
    row_moved = jnp.where(flip_rows == 1, -step_row, step_row)
    col_moved = jnp.where(flip_cols == 1, -step_col, step_col)
    source_row = jnp.where(transpose_bit == 1, col_moved, row_moved)
    source_col = jnp.where(transpose_bit == 1, row_moved, col_moved)
    source = (source_row + 1) * 3 + source_col + 1
    pick_place = (source[:, :, None] == kernel_spot[None, None, :]).astype(jnp.bfloat16)
    channel = jnp.arange(kernel.shape[-1], dtype=jnp.int32)
    colour = (channel // (SCALE * SCALE))[None, :]
    sub_row = (channel % (SCALE * SCALE) // SCALE)[None, :]
    sub_col = (channel % SCALE)[None, :]
    sub_row_moved = jnp.where(flip_rows == 1, SCALE - 1 - sub_row, sub_row)
    sub_col_moved = jnp.where(flip_cols == 1, SCALE - 1 - sub_col, sub_col)
    anchor_row = jnp.where(transpose_bit == 1, sub_col_moved, sub_row_moved)
    anchor_col = jnp.where(transpose_bit == 1, sub_row_moved, sub_col_moved)
    anchor = colour * SCALE * SCALE + anchor_row * SCALE + anchor_col
    pick_channel = (channel[None, :, None] == anchor[:, None, :]).astype(jnp.bfloat16)
    placed = jnp.einsum(
        "vpq,qcs->vpcs", pick_place, kernel, preferred_element_type=jnp.float32
    ).astype(jnp.bfloat16)
    return jnp.einsum(
        "vpcs,vso->vpco", placed, pick_channel, preferred_element_type=jnp.float32
    ).astype(jnp.bfloat16)


def attend(normed, region, w_qkv, w_proj, bias_grid):
    head_count = bias_grid.shape[1]
    leading, window_count, cells, channels = normed.shape
    head_width = channels // head_count
    projected = jnp.einsum(
        "lnsc,ce->lnse", normed, w_qkv, preferred_element_type=jnp.float32
    ).astype(jnp.bfloat16)
    projected = projected.reshape(leading, window_count, cells, 3, head_count, head_width)
    queries = projected[:, :, :, 0]
    key_part = projected[:, :, :, 1]
    value_part = projected[:, :, :, 2]
    scores = jnp.einsum("lnqhd,lnkhd->lnhqk", queries, key_part, preferred_element_type=jnp.float32)
    scores = scores * head_width ** (-0.5) + bias_grid[:, None]
    matches = region[:, None, :, None] == region[:, None, None, :]
    scores = jnp.where(matches[None], scores, MASKED)
    largest = jnp.max(scores, axis=-1, keepdims=True)
    weights = jnp.exp(scores - largest)
    probabilities = (weights / jnp.sum(weights, axis=-1, keepdims=True)).astype(jnp.bfloat16)
    value_part = jnp.broadcast_to(value_part, (probabilities.shape[0],) + value_part.shape[1:])
    mixed = jnp.einsum(
        "lnhqk,lnkhd->lnqhd", probabilities, value_part, preferred_element_type=jnp.float32
    ).astype(jnp.bfloat16)
    mixed = mixed.reshape(probabilities.shape[0], window_count, cells, channels)
    return jnp.einsum("lnsc,ce->lnse", mixed, w_proj, preferred_element_type=jnp.float32)


def attention_half(tokens, region, w_qkv, w_proj, bias_grid):
    height, breadth = (tokens.shape[1], tokens.shape[2])
    windows = to_windows(tokens)
    region_windows = to_windows(region[None, :, :, None])[0, :, :, 0]
    normed = normalize(windows).astype(jnp.bfloat16)
    branch = attend(normed, region_windows, w_qkv, w_proj, bias_grid)
    result = (windows.astype(jnp.float32) + branch).astype(jnp.bfloat16)
    return from_windows(result, height, breadth)


def feed_forward(tokens, w_up, w_down):
    normed = normalize(tokens).astype(jnp.bfloat16)
    hidden = jnp.einsum("...c,ce->...e", normed, w_up, preferred_element_type=jnp.float32)
    hidden = jax.nn.gelu(hidden, approximate=False).astype(jnp.bfloat16)
    output = tokens.astype(jnp.float32) + jnp.einsum(
        "...e,ec->...c", hidden, w_down, preferred_element_type=jnp.float32
    )
    return output.astype(jnp.bfloat16)


def reconstruct(padded, kernels, height, breadth):
    accumulated = jnp.zeros((padded.shape[0], height, breadth, kernels.shape[-1]), jnp.float32)
    for kernel_spot in range(9):
        spot_row, spot_col = (kernel_spot // 3, kernel_spot % 3)
        window = padded[:, spot_row : spot_row + height, spot_col : spot_col + breadth]
        accumulated = accumulated + jnp.einsum(
            "vrcd,vde->vrce", window, kernels[:, kernel_spot], preferred_element_type=jnp.float32
        )
    return accumulated


def refine(average, region, w_qkv, w_proj, bias_grid):
    normed = normalize(average).astype(jnp.bfloat16)[None]
    return average + attend(normed, region, w_qkv, w_proj, bias_grid)[0]


def local(
    features,
    labels,
    qkv_weight,
    proj_weight,
    up_weight,
    down_weight,
    swin_bias,
    recon_weight,
    refine_qkv,
    refine_proj,
    refine_bias,
):
    height, breadth, channels = features.shape
    variant_codes = lax.axis_index("var") * VAR_DEV + jnp.arange(VAR_DEV, dtype=jnp.int32)
    first_bias = bias_table(swin_bias[0], variant_codes)
    second_bias = bias_table(swin_bias[1], variant_codes)
    block_one = block_on_grid(
        features[None], labels, 0, qkv_weight, proj_weight, up_weight, down_weight, first_bias
    )
    tagged = jnp.broadcast_to(labels.astype(jnp.bfloat16)[None, :, :, None], block_one.shape[:3] + (1,))
    carried = extended(jnp.concatenate([block_one, tagged], axis=-1), (("ty", 1), ("tx", 2)), SHIFT)
    shifted = carried[..., :channels]
    region = carried[0, :, :, channels].astype(jnp.int32)
    block_two = block_on_grid(
        shifted, region, 1, qkv_weight, proj_weight, up_weight, down_weight, second_bias
    )
    padded = block_two[:, SHIFT - 1 : SHIFT + height + 1, SHIFT - 1 : SHIFT + breadth + 1]
    row = lax.axis_index("ty") * height - 1 + jnp.arange(height + 2)
    col = lax.axis_index("tx") * breadth - 1 + jnp.arange(breadth + 2)
    inside = ((row >= 0) & (row < lax.axis_size("ty") * height))[:, None] & (
        (col >= 0) & (col < lax.axis_size("tx") * breadth)
    )[None, :]
    padded = jnp.where(inside[None, :, :, None], padded, jnp.zeros_like(padded))
    kernels = variant_kernels(recon_weight, variant_codes)
    summed = jnp.sum(reconstruct(padded, kernels, height, breadth), axis=0)
    region_windows = to_windows(labels[None, :, :, None])[0, :, :, 0]
    refine_grid = bias_table(refine_bias, jnp.zeros((1,), jnp.int32))
    rows, cols, depth = summed.shape
    combined = var_sum(summed.astype(jnp.bfloat16).reshape(rows, cols * depth)).reshape(rows, cols, depth)
    refined = refine(
        to_windows(combined[None])[0] / 8.0, region_windows, refine_qkv, refine_proj, refine_grid
    )
    refined = lax.optimization_barrier(refined)
    colours = refined.shape[-1] // (SCALE * SCALE)
    picture = refined.reshape(
        height // WIN, breadth // WIN, WIN, WIN, colours * SCALE, SCALE
    ).transpose(4, 0, 2, 1, 3, 5)
    picture = picture.reshape(colours, SCALE, height, breadth * SCALE).transpose(0, 2, 1, 3)
    return picture.reshape(colours, SCALE * height, SCALE * breadth)


def solution(mesh):
    placed = (P("ty", "tx", None), P("ty", "tx"), P(), P(), P(), P(), P(), P(), P(), P(), P())
    return jax.shard_map(
        local, mesh=mesh, in_specs=placed, out_specs=P(None, "ty", "tx"), check_vma=False
    )
```

```python
import functools

import jax
import jax.numpy as jnp
from jax import lax
from jax.experimental import pallas as pl
from jax.experimental.pallas import tpu as pltpu
from jax.sharding import PartitionSpec as P

MESH = pl.DeviceIdType.MESH

WIN = 8
SHIFT = 4
SCALE = 4
VAR_DEV = 2


EPSILON = 1e-05
MASKED = -1e30


def extended(cells, sides, width):
    for axis, dim in sides:
        count = lax.axis_size(axis)
        ends = count - 1
        head = lax.slice_in_dim(cells, 0, width, axis=dim)
        tail = lax.slice_in_dim(cells, cells.shape[dim] - width, cells.shape[dim], axis=dim)
        cells = jnp.concatenate(
            [
                lax.ppermute(tail, axis, [(i, (i + 1) % count) for i in range(ends)]),
                cells,
                lax.ppermute(head, axis, [((i + 1) % count, i) for i in range(ends)]),
            ],
            axis=dim,
        )
    return cells


def var_sum_kernel(count, part_ref, out_ref, held, send_sem, recv_sem, own_sem):
    me = lax.axis_index("var")
    barrier = pltpu.get_barrier_semaphore()
    for step in range(1, count):
        peer = lax.rem(me + step, count)
        pl.semaphore_signal(barrier, inc=1, device_id={"var": peer}, device_id_type=MESH)
    pl.semaphore_wait(barrier, count - 1)
    own = pltpu.make_async_copy(part_ref, held.at[me], own_sem)
    own.start()
    sends = []
    for step in range(1, count):
        peer = lax.rem(me + step, count)
        copy = pltpu.make_async_remote_copy(
            src_ref=part_ref,
            dst_ref=held.at[me],
            send_sem=send_sem.at[step - 1],
            recv_sem=recv_sem.at[me],
            device_id={"var": peer},
            device_id_type=MESH,
        )
        copy.start()
        sends.append(copy)
    own.wait()
    for copy in sends:
        copy.wait_send()
    for step in range(1, count):
        source = lax.rem(me + count - step, count)
        pltpu.make_async_remote_copy(
            src_ref=part_ref,
            dst_ref=held.at[source],
            send_sem=send_sem.at[step - 1],
            recv_sem=recv_sem.at[source],
            device_id={"var": source},
            device_id_type=MESH,
        ).wait_recv()
    total = held[0].astype(jnp.float32)
    for index in range(1, count):
        total = total + held[index].astype(jnp.float32)
    out_ref[...] = total


def var_sum(part):
    count = lax.axis_size("var")
    return pl.pallas_call(
        functools.partial(var_sum_kernel, count),
        out_shape=jax.ShapeDtypeStruct(part.shape, jnp.float32),
        in_specs=[pl.BlockSpec(memory_space=pltpu.VMEM)],
        out_specs=pl.BlockSpec(memory_space=pltpu.VMEM),
        scratch_shapes=[
            pltpu.VMEM((count,) + part.shape, part.dtype),
            pltpu.SemaphoreType.DMA((count - 1,)),
            pltpu.SemaphoreType.DMA((count,)),
            pltpu.SemaphoreType.DMA(()),
        ],
        compiler_params=pltpu.CompilerParams(collective_id=0, has_side_effects=True),
    )(part)


GROUP = 4
LANE = 128


def block_kernel(
    variants, heads, scale, x_ref, labq_ref, labk_ref, bias_ref, wqkv_ref, wp_ref, wup_ref, wdown_ref, out_ref
):
    inputs = x_ref.shape[0]
    tokens = x_ref.shape[2]
    labq = labq_ref[0]
    labk = labk_ref[0]
    slot_q = lax.broadcasted_iota(jnp.int32, (tokens, tokens), 0) // (WIN * WIN)
    slot_k = lax.broadcasted_iota(jnp.int32, (tokens, tokens), 1) // (WIN * WIN)
    match = (labq == labk) & (slot_q == slot_k)
    projected = []
    for index in range(inputs):
        normed = normalize(x_ref[index, 0]).astype(jnp.bfloat16)
        projected.append(
            jnp.dot(normed, wqkv_ref[...], preferred_element_type=jnp.float32).astype(jnp.bfloat16)
        )
    span = wp_ref.shape[0]
    width = wup_ref.shape[0] // heads
    lane = lax.broadcasted_iota(jnp.int32, (1, span), 1)
    for variant in range(variants):
        source = variant if inputs > 1 else 0
        qkv = projected[source]
        query = qkv[:, :span]
        key = qkv[:, span : 2 * span]
        value = qkv[:, 2 * span :]
        mixed = jnp.zeros((tokens, span), jnp.float32)
        for head in range(heads):
            mine = (lane >= head * width) & (lane < (head + 1) * width)
            scores = lax.dot_general(
                jnp.where(mine, query, jnp.zeros_like(query)),
                key,
                (((1,), (1,)), ((), ())),
                preferred_element_type=jnp.float32,
            )
            scores = scores * scale
            table = bias_ref[variant, head]
            table = jnp.concatenate([table] * GROUP, axis=1)
            scores = (scores.reshape(GROUP, WIN * WIN, tokens) + table[None]).reshape(tokens, tokens)
            scores = jnp.where(match, scores, MASKED)
            largest = jnp.max(scores, axis=-1, keepdims=True)
            weights = jnp.exp(scores - largest)
            probabilities = (weights / jnp.sum(weights, axis=-1, keepdims=True)).astype(jnp.bfloat16)
            mixed = mixed + jnp.dot(
                probabilities, jnp.where(mine, value, jnp.zeros_like(value)), preferred_element_type=jnp.float32
            )
        branch = jnp.dot(mixed.astype(jnp.bfloat16), wp_ref[...], preferred_element_type=jnp.float32)
        own = x_ref[source, 0].astype(jnp.float32)
        hidden_in = (own + branch).astype(jnp.bfloat16)
        normed = normalize(hidden_in).astype(jnp.bfloat16)
        hidden = jnp.dot(normed, wup_ref[...], preferred_element_type=jnp.float32)
        hidden = (0.5 * hidden * (1.0 + lax.erf(hidden * (2.0 ** -0.5)))).astype(jnp.bfloat16)
        result = hidden_in.astype(jnp.float32) + jnp.dot(
            hidden, wdown_ref[...], preferred_element_type=jnp.float32
        )
        out_ref[variant, 0] = result.astype(jnp.bfloat16)


def padded_weights(w_qkv, w_proj, heads):
    channels = w_proj.shape[0]
    span = -(-channels // LANE) * LANE
    columns = jnp.pad(w_qkv.reshape(channels, 3, channels), ((0, 0), (0, 0), (0, span - channels)))
    rows = jnp.pad(w_proj, ((0, span - channels), (0, 0)))
    return columns.reshape(channels, 3 * span), rows


def swin_block(windows, region, layer, w_qkv, w_proj, w_up, w_down, bias_grid):
    inputs, count, cells, channels = windows.shape
    variants, heads = bias_grid.shape[:2]
    groups = -(-count // GROUP)
    extra = groups * GROUP - count
    windows = jnp.pad(windows, ((0, 0), (0, extra), (0, 0), (0, 0)))
    region = jnp.pad(region, ((0, extra), (0, 0)))
    tokens = GROUP * cells
    x = windows.reshape(inputs, groups, tokens, channels)
    labq = region.reshape(groups, tokens, 1)
    labk = region.reshape(groups, 1, tokens)
    bias = bias_grid
    scale = (channels // heads) ** (-0.5)
    whole = lambda shape: pl.BlockSpec(shape, lambda g: (0,) * len(shape))
    out = pl.pallas_call(
        functools.partial(block_kernel, variants, heads, scale),
        out_shape=jax.ShapeDtypeStruct((variants, groups, tokens, channels), jnp.bfloat16),
        grid=(groups,),
        in_specs=[
            pl.BlockSpec((inputs, 1, tokens, channels), lambda g: (0, g, 0, 0)),
            pl.BlockSpec((1, tokens, 1), lambda g: (g, 0, 0)),
            pl.BlockSpec((1, 1, tokens), lambda g: (g, 0, 0)),
            whole(bias.shape),
            pl.BlockSpec((None,) + w_qkv.shape[1:], lambda g: (layer, 0, 0)),
            pl.BlockSpec((None,) + w_proj.shape[1:], lambda g: (layer, 0, 0)),
            pl.BlockSpec((None,) + w_up.shape[1:], lambda g: (layer, 0, 0)),
            pl.BlockSpec((None,) + w_down.shape[1:], lambda g: (layer, 0, 0)),
        ],
        out_specs=pl.BlockSpec((variants, 1, tokens, channels), lambda g: (0, g, 0, 0)),
        compiler_params=pltpu.CompilerParams(vmem_limit_bytes=48 * 1024 * 1024),
    )(x, labq, labk, bias, w_qkv, w_proj, w_up, w_down)
    out = out.reshape(variants, groups * GROUP, cells, channels)
    return out[:, :count]


def block_on_grid(tokens, region, layer, w_qkv, w_proj, w_up, w_down, bias_grid):
    height, breadth = tokens.shape[1], tokens.shape[2]
    windows = to_windows(tokens)
    region_windows = to_windows(region[None, :, :, None])[0, :, :, 0]
    out = swin_block(windows, region_windows, layer, w_qkv, w_proj, w_up, w_down, bias_grid)
    return from_windows(out, height, breadth)


def normalize(values):
    values = values.astype(jnp.float32)
    average = jnp.mean(values, axis=-1, keepdims=True)
    centred = values - average
    spread = jnp.mean(centred * centred, axis=-1, keepdims=True)
    return centred * lax.rsqrt(spread + EPSILON)


def to_windows(grid):
    leading, height, breadth, channels = grid.shape
    grid = grid.reshape(leading, height // WIN, WIN, breadth // WIN, WIN, channels)
    grid = grid.transpose(0, 1, 3, 2, 4, 5)
    return grid.reshape(leading, height // WIN * (breadth // WIN), WIN * WIN, channels)


def from_windows(windows, height, breadth):
    leading, window_count, cells, channels = windows.shape
    windows = windows.reshape(leading, height // WIN, breadth // WIN, WIN, WIN, channels)
    windows = windows.transpose(0, 1, 3, 2, 4, 5)
    return windows.reshape(leading, height, breadth, channels)


def bias_table(offset_table, variant_codes):
    position = jnp.arange(WIN * WIN, dtype=jnp.int32)
    row_step = (position // WIN)[:, None] - (position // WIN)[None, :]
    across = (position % WIN)[:, None] - (position % WIN)[None, :]
    transpose_bit = (variant_codes // 4)[:, None, None]
    flip_rows = (variant_codes // 2 % 2)[:, None, None]
    flip_cols = (variant_codes % 2)[:, None, None]
    row_moved = jnp.where(flip_rows == 1, -row_step, row_step)
    col_moved = jnp.where(flip_cols == 1, -across, across)
    leading_step = jnp.where(transpose_bit == 1, col_moved, row_moved)
    trailing_step = jnp.where(transpose_bit == 1, row_moved, col_moved)
    table_index = (leading_step + WIN - 1) * (2 * WIN - 1) + trailing_step + WIN - 1
    slots = jnp.arange((2 * WIN - 1) * (2 * WIN - 1), dtype=jnp.int32)
    one_hot = (table_index[..., None] == slots).astype(jnp.bfloat16)
    high = lax.reduce_precision(offset_table, exponent_bits=8, mantissa_bits=7)
    rest = offset_table - high
    middle = lax.reduce_precision(rest, exponent_bits=8, mantissa_bits=7)
    low = rest - middle
    parts = jnp.concatenate([high, middle, low], axis=0).astype(jnp.bfloat16)
    picked = jnp.einsum("vqkt,ht->vhqk", one_hot, parts, preferred_element_type=jnp.float32)
    heads = offset_table.shape[0]
    return (picked[:, :heads] + picked[:, heads : 2 * heads]) + picked[:, 2 * heads :]


def variant_kernels(kernel, variant_codes):
    transpose_bit = (variant_codes // 4)[:, None]
    flip_rows = (variant_codes // 2 % 2)[:, None]
    flip_cols = (variant_codes % 2)[:, None]
    kernel_spot = jnp.arange(9, dtype=jnp.int32)
    step_row = (kernel_spot // 3 - 1)[None, :]
    step_col = (kernel_spot % 3 - 1)[None, :]
    row_moved = jnp.where(flip_rows == 1, -step_row, step_row)
    col_moved = jnp.where(flip_cols == 1, -step_col, step_col)
    source_row = jnp.where(transpose_bit == 1, col_moved, row_moved)
    source_col = jnp.where(transpose_bit == 1, row_moved, col_moved)
    source = (source_row + 1) * 3 + source_col + 1
    pick_place = (source[:, :, None] == kernel_spot[None, None, :]).astype(jnp.bfloat16)
    channel = jnp.arange(kernel.shape[-1], dtype=jnp.int32)
    colour = (channel // (SCALE * SCALE))[None, :]
    sub_row = (channel % (SCALE * SCALE) // SCALE)[None, :]
    sub_col = (channel % SCALE)[None, :]
    sub_row_moved = jnp.where(flip_rows == 1, SCALE - 1 - sub_row, sub_row)
    sub_col_moved = jnp.where(flip_cols == 1, SCALE - 1 - sub_col, sub_col)
    anchor_row = jnp.where(transpose_bit == 1, sub_col_moved, sub_row_moved)
    anchor_col = jnp.where(transpose_bit == 1, sub_row_moved, sub_col_moved)
    anchor = colour * SCALE * SCALE + anchor_row * SCALE + anchor_col
    pick_channel = (channel[None, :, None] == anchor[:, None, :]).astype(jnp.bfloat16)
    placed = jnp.einsum(
        "vpq,qcs->vpcs", pick_place, kernel, preferred_element_type=jnp.float32
    ).astype(jnp.bfloat16)
    return jnp.einsum(
        "vpcs,vso->vpco", placed, pick_channel, preferred_element_type=jnp.float32
    ).astype(jnp.bfloat16)


def attend(normed, region, w_qkv, w_proj, bias_grid):
    head_count = bias_grid.shape[1]
    leading, window_count, cells, channels = normed.shape
    head_width = channels // head_count
    projected = jnp.einsum(
        "lnsc,ce->lnse", normed, w_qkv, preferred_element_type=jnp.float32
    ).astype(jnp.bfloat16)
    projected = projected.reshape(leading, window_count, cells, 3, head_count, head_width)
    queries = projected[:, :, :, 0]
    key_part = projected[:, :, :, 1]
    value_part = projected[:, :, :, 2]
    scores = jnp.einsum("lnqhd,lnkhd->lnhqk", queries, key_part, preferred_element_type=jnp.float32)
    scores = scores * head_width ** (-0.5) + bias_grid[:, None]
    matches = region[:, None, :, None] == region[:, None, None, :]
    scores = jnp.where(matches[None], scores, MASKED)
    largest = jnp.max(scores, axis=-1, keepdims=True)
    weights = jnp.exp(scores - largest)
    probabilities = (weights / jnp.sum(weights, axis=-1, keepdims=True)).astype(jnp.bfloat16)
    value_part = jnp.broadcast_to(value_part, (probabilities.shape[0],) + value_part.shape[1:])
    mixed = jnp.einsum(
        "lnhqk,lnkhd->lnqhd", probabilities, value_part, preferred_element_type=jnp.float32
    ).astype(jnp.bfloat16)
    mixed = mixed.reshape(probabilities.shape[0], window_count, cells, channels)
    return jnp.einsum("lnsc,ce->lnse", mixed, w_proj, preferred_element_type=jnp.float32)


def attention_half(tokens, region, w_qkv, w_proj, bias_grid):
    height, breadth = (tokens.shape[1], tokens.shape[2])
    windows = to_windows(tokens)
    region_windows = to_windows(region[None, :, :, None])[0, :, :, 0]
    normed = normalize(windows).astype(jnp.bfloat16)
    branch = attend(normed, region_windows, w_qkv, w_proj, bias_grid)
    result = (windows.astype(jnp.float32) + branch).astype(jnp.bfloat16)
    return from_windows(result, height, breadth)


def feed_forward(tokens, w_up, w_down):
    normed = normalize(tokens).astype(jnp.bfloat16)
    hidden = jnp.einsum("...c,ce->...e", normed, w_up, preferred_element_type=jnp.float32)
    hidden = jax.nn.gelu(hidden, approximate=False).astype(jnp.bfloat16)
    output = tokens.astype(jnp.float32) + jnp.einsum(
        "...e,ec->...c", hidden, w_down, preferred_element_type=jnp.float32
    )
    return output.astype(jnp.bfloat16)


def reconstruct(padded, kernels, height, breadth):
    accumulated = jnp.zeros((padded.shape[0], height, breadth, kernels.shape[-1]), jnp.float32)
    for kernel_spot in range(9):
        spot_row, spot_col = (kernel_spot // 3, kernel_spot % 3)
        window = padded[:, spot_row : spot_row + height, spot_col : spot_col + breadth]
        accumulated = accumulated + jnp.einsum(
            "vrcd,vde->vrce", window, kernels[:, kernel_spot], preferred_element_type=jnp.float32
        )
    return accumulated


def refine(average, region, w_qkv, w_proj, bias_grid):
    normed = normalize(average).astype(jnp.bfloat16)[None]
    return average + attend(normed, region, w_qkv, w_proj, bias_grid)[0]


def local(
    features,
    labels,
    qkv_weight,
    proj_weight,
    up_weight,
    down_weight,
    swin_bias,
    recon_weight,
    refine_qkv,
    refine_proj,
    refine_bias,
):
    height, breadth, channels = features.shape
    variant_codes = lax.axis_index("var") * VAR_DEV + jnp.arange(VAR_DEV, dtype=jnp.int32)
    first_bias = bias_table(swin_bias[0], variant_codes)
    second_bias = bias_table(swin_bias[1], variant_codes)
    block_one = block_on_grid(
        features[None], labels, 0, qkv_weight, proj_weight, up_weight, down_weight, first_bias
    )
    tagged = jnp.broadcast_to(labels.astype(jnp.bfloat16)[None, :, :, None], block_one.shape[:3] + (1,))
    carried = extended(jnp.concatenate([block_one, tagged], axis=-1), (("ty", 1), ("tx", 2)), SHIFT)
    shifted = carried[..., :channels]
    region = carried[0, :, :, channels].astype(jnp.int32)
    block_two = block_on_grid(
        shifted, region, 1, qkv_weight, proj_weight, up_weight, down_weight, second_bias
    )
    padded = block_two[:, SHIFT - 1 : SHIFT + height + 1, SHIFT - 1 : SHIFT + breadth + 1]
    row = lax.axis_index("ty") * height - 1 + jnp.arange(height + 2)
    col = lax.axis_index("tx") * breadth - 1 + jnp.arange(breadth + 2)
    inside = ((row >= 0) & (row < lax.axis_size("ty") * height))[:, None] & (
        (col >= 0) & (col < lax.axis_size("tx") * breadth)
    )[None, :]
    padded = jnp.where(inside[None, :, :, None], padded, jnp.zeros_like(padded))
    kernels = variant_kernels(recon_weight, variant_codes)
    summed = jnp.sum(reconstruct(padded, kernels, height, breadth), axis=0)
    region_windows = to_windows(labels[None, :, :, None])[0, :, :, 0]
    refine_grid = bias_table(refine_bias, jnp.zeros((1,), jnp.int32))
    rows, cols, depth = summed.shape
    combined = var_sum(summed.astype(jnp.bfloat16).reshape(rows, cols * depth)).reshape(rows, cols, depth)
    refined = refine(
        to_windows(combined[None])[0] / 8.0, region_windows, refine_qkv, refine_proj, refine_grid
    )
    refined = lax.optimization_barrier(refined)
    colours = refined.shape[-1] // (SCALE * SCALE)
    picture = refined.reshape(
        height // WIN, breadth // WIN, WIN, WIN, colours * SCALE, SCALE
    ).transpose(4, 0, 2, 1, 3, 5)
    picture = picture.reshape(colours, SCALE, height, breadth * SCALE).transpose(0, 2, 1, 3)
    return picture.reshape(colours, SCALE * height, SCALE * breadth)


def solution(mesh):
    placed = (P("ty", "tx", None), P("ty", "tx"), P(), P(), P(), P(), P(), P(), P(), P(), P())
    return jax.shard_map(
        local, mesh=mesh, in_specs=placed, out_specs=P(None, "ty", "tx"), check_vma=False
    )
```

```python
import functools

import jax
import jax.numpy as jnp
from jax import lax
from jax.experimental import pallas as pl
from jax.experimental.pallas import tpu as pltpu
from jax.sharding import PartitionSpec as P

MESH = pl.DeviceIdType.MESH

WIN = 8
SHIFT = 4
SCALE = 4
VAR_DEV = 2


EPSILON = 1e-05
MASKED = -1e30


def extended(cells, sides, width):
    for axis, dim in sides:
        count = lax.axis_size(axis)
        ends = count - 1
        head = lax.slice_in_dim(cells, 0, width, axis=dim)
        tail = lax.slice_in_dim(cells, cells.shape[dim] - width, cells.shape[dim], axis=dim)
        cells = jnp.concatenate(
            [
                lax.ppermute(tail, axis, [(i, (i + 1) % count) for i in range(ends)]),
                cells,
                lax.ppermute(head, axis, [((i + 1) % count, i) for i in range(ends)]),
            ],
            axis=dim,
        )
    return cells


def var_sum_kernel(count, part_ref, out_ref, held, send_sem, recv_sem, own_sem):
    me = lax.axis_index("var")
    barrier = pltpu.get_barrier_semaphore()
    for step in range(1, count):
        peer = lax.rem(me + step, count)
        pl.semaphore_signal(barrier, inc=1, device_id={"var": peer}, device_id_type=MESH)
    pl.semaphore_wait(barrier, count - 1)
    own = pltpu.make_async_copy(part_ref, held.at[me], own_sem)
    own.start()
    sends = []
    for step in range(1, count):
        peer = lax.rem(me + step, count)
        copy = pltpu.make_async_remote_copy(
            src_ref=part_ref,
            dst_ref=held.at[me],
            send_sem=send_sem.at[step - 1],
            recv_sem=recv_sem.at[me],
            device_id={"var": peer},
            device_id_type=MESH,
        )
        copy.start()
        sends.append(copy)
    own.wait()
    for copy in sends:
        copy.wait_send()
    for step in range(1, count):
        source = lax.rem(me + count - step, count)
        pltpu.make_async_remote_copy(
            src_ref=part_ref,
            dst_ref=held.at[source],
            send_sem=send_sem.at[step - 1],
            recv_sem=recv_sem.at[source],
            device_id={"var": source},
            device_id_type=MESH,
        ).wait_recv()
    total = held[0].astype(jnp.float32)
    for index in range(1, count):
        total = total + held[index].astype(jnp.float32)
    out_ref[...] = total


def var_sum(part):
    count = lax.axis_size("var")
    return pl.pallas_call(
        functools.partial(var_sum_kernel, count),
        out_shape=jax.ShapeDtypeStruct(part.shape, jnp.float32),
        in_specs=[pl.BlockSpec(memory_space=pltpu.VMEM)],
        out_specs=pl.BlockSpec(memory_space=pltpu.VMEM),
        scratch_shapes=[
            pltpu.VMEM((count,) + part.shape, part.dtype),
            pltpu.SemaphoreType.DMA((count - 1,)),
            pltpu.SemaphoreType.DMA((count,)),
            pltpu.SemaphoreType.DMA(()),
        ],
        compiler_params=pltpu.CompilerParams(collective_id=0, has_side_effects=True),
    )(part)


GROUP = 4
LANE = 128


def block_kernel(
    variants, heads, scale, x_ref, labq_ref, labk_ref, bias_ref, wqkv_ref, wp_ref, wup_ref, wdown_ref, out_ref, wide_ref
):
    @pl.when(pl.program_id(0) == 0)
    def _():
        for variant in range(variants):
            for head in range(heads):
                wide_ref[variant, head] = jnp.concatenate([bias_ref[variant, head]] * GROUP, axis=1)

    inputs = x_ref.shape[0]
    tokens = x_ref.shape[2]
    labq = labq_ref[0]
    labk = labk_ref[0]
    slot_q = lax.broadcasted_iota(jnp.int32, (tokens, tokens), 0) // (WIN * WIN)
    slot_k = lax.broadcasted_iota(jnp.int32, (tokens, tokens), 1) // (WIN * WIN)
    match = (labq == labk) & (slot_q == slot_k)
    projected = []
    for index in range(inputs):
        normed = normalize(x_ref[index, 0]).astype(jnp.bfloat16)
        projected.append(
            jnp.dot(normed, wqkv_ref[...], preferred_element_type=jnp.float32).astype(jnp.bfloat16)
        )
    span = wp_ref.shape[0]
    width = wup_ref.shape[0] // heads
    lane = lax.broadcasted_iota(jnp.int32, (1, span), 1)
    for variant in range(variants):
        source = variant if inputs > 1 else 0
        qkv = projected[source]
        query = qkv[:, :span]
        key = qkv[:, span : 2 * span]
        value = qkv[:, 2 * span :]
        mixed = jnp.zeros((tokens, span), jnp.float32)
        for head in range(heads):
            mine = (lane >= head * width) & (lane < (head + 1) * width)
            scores = lax.dot_general(
                jnp.where(mine, query, jnp.zeros_like(query)),
                key,
                (((1,), (1,)), ((), ())),
                preferred_element_type=jnp.float32,
            )
            scores = scores * scale
            scores = (scores.reshape(GROUP, WIN * WIN, tokens) + wide_ref[variant, head][None]).reshape(
                tokens, tokens
            )
            scores = jnp.where(match, scores, MASKED)
            largest = jnp.max(scores, axis=-1, keepdims=True)
            weights = jnp.exp(scores - largest)
            probabilities = (weights / jnp.sum(weights, axis=-1, keepdims=True)).astype(jnp.bfloat16)
            mixed = mixed + jnp.dot(
                probabilities, jnp.where(mine, value, jnp.zeros_like(value)), preferred_element_type=jnp.float32
            )
        branch = jnp.dot(mixed.astype(jnp.bfloat16), wp_ref[...], preferred_element_type=jnp.float32)
        own = x_ref[source, 0].astype(jnp.float32)
        hidden_in = (own + branch).astype(jnp.bfloat16)
        normed = normalize(hidden_in).astype(jnp.bfloat16)
        hidden = jnp.dot(normed, wup_ref[...], preferred_element_type=jnp.float32)
        hidden = (0.5 * hidden * (1.0 + lax.erf(hidden * (2.0 ** -0.5)))).astype(jnp.bfloat16)
        result = hidden_in.astype(jnp.float32) + jnp.dot(
            hidden, wdown_ref[...], preferred_element_type=jnp.float32
        )
        out_ref[variant, 0] = result.astype(jnp.bfloat16)


def padded_weights(w_qkv, w_proj, heads):
    channels = w_proj.shape[0]
    span = -(-channels // LANE) * LANE
    columns = jnp.pad(w_qkv.reshape(channels, 3, channels), ((0, 0), (0, 0), (0, span - channels)))
    rows = jnp.pad(w_proj, ((0, span - channels), (0, 0)))
    return columns.reshape(channels, 3 * span), rows


def swin_block(windows, region, layer, w_qkv, w_proj, w_up, w_down, bias_grid):
    inputs, count, cells, channels = windows.shape
    variants, heads = bias_grid.shape[:2]
    groups = -(-count // GROUP)
    extra = groups * GROUP - count
    windows = jnp.pad(windows, ((0, 0), (0, extra), (0, 0), (0, 0)))
    region = jnp.pad(region, ((0, extra), (0, 0)))
    tokens = GROUP * cells
    x = windows.reshape(inputs, groups, tokens, channels)
    labq = region.reshape(groups, tokens, 1)
    labk = region.reshape(groups, 1, tokens)
    bias = bias_grid
    scale = (channels // heads) ** (-0.5)
    whole = lambda shape: pl.BlockSpec(shape, lambda g: (0,) * len(shape))
    out = pl.pallas_call(
        functools.partial(block_kernel, variants, heads, scale),
        out_shape=jax.ShapeDtypeStruct((variants, groups, tokens, channels), jnp.bfloat16),
        grid=(groups,),
        in_specs=[
            pl.BlockSpec((inputs, 1, tokens, channels), lambda g: (0, g, 0, 0)),
            pl.BlockSpec((1, tokens, 1), lambda g: (g, 0, 0)),
            pl.BlockSpec((1, 1, tokens), lambda g: (g, 0, 0)),
            whole(bias.shape),
            pl.BlockSpec((None,) + w_qkv.shape[1:], lambda g: (layer, 0, 0)),
            pl.BlockSpec((None,) + w_proj.shape[1:], lambda g: (layer, 0, 0)),
            pl.BlockSpec((None,) + w_up.shape[1:], lambda g: (layer, 0, 0)),
            pl.BlockSpec((None,) + w_down.shape[1:], lambda g: (layer, 0, 0)),
        ],
        out_specs=pl.BlockSpec((variants, 1, tokens, channels), lambda g: (0, g, 0, 0)),
        scratch_shapes=[pltpu.VMEM((variants, heads, cells, tokens), jnp.float32)],
        compiler_params=pltpu.CompilerParams(vmem_limit_bytes=48 * 1024 * 1024),
    )(x, labq, labk, bias, w_qkv, w_proj, w_up, w_down)
    out = out.reshape(variants, groups * GROUP, cells, channels)
    return out[:, :count]


def block_on_grid(tokens, region, layer, w_qkv, w_proj, w_up, w_down, bias_grid):
    height, breadth = tokens.shape[1], tokens.shape[2]
    windows = to_windows(tokens)
    region_windows = to_windows(region[None, :, :, None])[0, :, :, 0]
    out = swin_block(windows, region_windows, layer, w_qkv, w_proj, w_up, w_down, bias_grid)
    return from_windows(out, height, breadth)


def normalize(values):
    values = values.astype(jnp.float32)
    average = jnp.mean(values, axis=-1, keepdims=True)
    centred = values - average
    spread = jnp.mean(centred * centred, axis=-1, keepdims=True)
    return centred * lax.rsqrt(spread + EPSILON)


def to_windows(grid):
    leading, height, breadth, channels = grid.shape
    grid = grid.reshape(leading, height // WIN, WIN, breadth // WIN, WIN, channels)
    grid = grid.transpose(0, 1, 3, 2, 4, 5)
    return grid.reshape(leading, height // WIN * (breadth // WIN), WIN * WIN, channels)


def from_windows(windows, height, breadth):
    leading, window_count, cells, channels = windows.shape
    windows = windows.reshape(leading, height // WIN, breadth // WIN, WIN, WIN, channels)
    windows = windows.transpose(0, 1, 3, 2, 4, 5)
    return windows.reshape(leading, height, breadth, channels)


def bias_table(offset_table, variant_codes):
    position = jnp.arange(WIN * WIN, dtype=jnp.int32)
    row_step = (position // WIN)[:, None] - (position // WIN)[None, :]
    across = (position % WIN)[:, None] - (position % WIN)[None, :]
    transpose_bit = (variant_codes // 4)[:, None, None]
    flip_rows = (variant_codes // 2 % 2)[:, None, None]
    flip_cols = (variant_codes % 2)[:, None, None]
    row_moved = jnp.where(flip_rows == 1, -row_step, row_step)
    col_moved = jnp.where(flip_cols == 1, -across, across)
    leading_step = jnp.where(transpose_bit == 1, col_moved, row_moved)
    trailing_step = jnp.where(transpose_bit == 1, row_moved, col_moved)
    table_index = (leading_step + WIN - 1) * (2 * WIN - 1) + trailing_step + WIN - 1
    slots = jnp.arange((2 * WIN - 1) * (2 * WIN - 1), dtype=jnp.int32)
    one_hot = (table_index[..., None] == slots).astype(jnp.bfloat16)
    high = lax.reduce_precision(offset_table, exponent_bits=8, mantissa_bits=7)
    rest = offset_table - high
    middle = lax.reduce_precision(rest, exponent_bits=8, mantissa_bits=7)
    low = rest - middle
    parts = jnp.concatenate([high, middle, low], axis=0).astype(jnp.bfloat16)
    picked = jnp.einsum("vqkt,ht->vhqk", one_hot, parts, preferred_element_type=jnp.float32)
    heads = offset_table.shape[0]
    return (picked[:, :heads] + picked[:, heads : 2 * heads]) + picked[:, 2 * heads :]


def variant_kernels(kernel, variant_codes):
    transpose_bit = (variant_codes // 4)[:, None]
    flip_rows = (variant_codes // 2 % 2)[:, None]
    flip_cols = (variant_codes % 2)[:, None]
    kernel_spot = jnp.arange(9, dtype=jnp.int32)
    step_row = (kernel_spot // 3 - 1)[None, :]
    step_col = (kernel_spot % 3 - 1)[None, :]
    row_moved = jnp.where(flip_rows == 1, -step_row, step_row)
    col_moved = jnp.where(flip_cols == 1, -step_col, step_col)
    source_row = jnp.where(transpose_bit == 1, col_moved, row_moved)
    source_col = jnp.where(transpose_bit == 1, row_moved, col_moved)
    source = (source_row + 1) * 3 + source_col + 1
    pick_place = (source[:, :, None] == kernel_spot[None, None, :]).astype(jnp.bfloat16)
    channel = jnp.arange(kernel.shape[-1], dtype=jnp.int32)
    colour = (channel // (SCALE * SCALE))[None, :]
    sub_row = (channel % (SCALE * SCALE) // SCALE)[None, :]
    sub_col = (channel % SCALE)[None, :]
    sub_row_moved = jnp.where(flip_rows == 1, SCALE - 1 - sub_row, sub_row)
    sub_col_moved = jnp.where(flip_cols == 1, SCALE - 1 - sub_col, sub_col)
    anchor_row = jnp.where(transpose_bit == 1, sub_col_moved, sub_row_moved)
    anchor_col = jnp.where(transpose_bit == 1, sub_row_moved, sub_col_moved)
    anchor = colour * SCALE * SCALE + anchor_row * SCALE + anchor_col
    pick_channel = (channel[None, :, None] == anchor[:, None, :]).astype(jnp.bfloat16)
    placed = jnp.einsum(
        "vpq,qcs->vpcs", pick_place, kernel, preferred_element_type=jnp.float32
    ).astype(jnp.bfloat16)
    return jnp.einsum(
        "vpcs,vso->vpco", placed, pick_channel, preferred_element_type=jnp.float32
    ).astype(jnp.bfloat16)


def attend(normed, region, w_qkv, w_proj, bias_grid):
    head_count = bias_grid.shape[1]
    leading, window_count, cells, channels = normed.shape
    head_width = channels // head_count
    projected = jnp.einsum(
        "lnsc,ce->lnse", normed, w_qkv, preferred_element_type=jnp.float32
    ).astype(jnp.bfloat16)
    projected = projected.reshape(leading, window_count, cells, 3, head_count, head_width)
    queries = projected[:, :, :, 0]
    key_part = projected[:, :, :, 1]
    value_part = projected[:, :, :, 2]
    scores = jnp.einsum("lnqhd,lnkhd->lnhqk", queries, key_part, preferred_element_type=jnp.float32)
    scores = scores * head_width ** (-0.5) + bias_grid[:, None]
    matches = region[:, None, :, None] == region[:, None, None, :]
    scores = jnp.where(matches[None], scores, MASKED)
    largest = jnp.max(scores, axis=-1, keepdims=True)
    weights = jnp.exp(scores - largest)
    probabilities = (weights / jnp.sum(weights, axis=-1, keepdims=True)).astype(jnp.bfloat16)
    value_part = jnp.broadcast_to(value_part, (probabilities.shape[0],) + value_part.shape[1:])
    mixed = jnp.einsum(
        "lnhqk,lnkhd->lnqhd", probabilities, value_part, preferred_element_type=jnp.float32
    ).astype(jnp.bfloat16)
    mixed = mixed.reshape(probabilities.shape[0], window_count, cells, channels)
    return jnp.einsum("lnsc,ce->lnse", mixed, w_proj, preferred_element_type=jnp.float32)


def attention_half(tokens, region, w_qkv, w_proj, bias_grid):
    height, breadth = (tokens.shape[1], tokens.shape[2])
    windows = to_windows(tokens)
    region_windows = to_windows(region[None, :, :, None])[0, :, :, 0]
    normed = normalize(windows).astype(jnp.bfloat16)
    branch = attend(normed, region_windows, w_qkv, w_proj, bias_grid)
    result = (windows.astype(jnp.float32) + branch).astype(jnp.bfloat16)
    return from_windows(result, height, breadth)


def feed_forward(tokens, w_up, w_down):
    normed = normalize(tokens).astype(jnp.bfloat16)
    hidden = jnp.einsum("...c,ce->...e", normed, w_up, preferred_element_type=jnp.float32)
    hidden = jax.nn.gelu(hidden, approximate=False).astype(jnp.bfloat16)
    output = tokens.astype(jnp.float32) + jnp.einsum(
        "...e,ec->...c", hidden, w_down, preferred_element_type=jnp.float32
    )
    return output.astype(jnp.bfloat16)


def reconstruct(padded, kernels, height, breadth):
    accumulated = jnp.zeros((padded.shape[0], height, breadth, kernels.shape[-1]), jnp.float32)
    for kernel_spot in range(9):
        spot_row, spot_col = (kernel_spot // 3, kernel_spot % 3)
        window = padded[:, spot_row : spot_row + height, spot_col : spot_col + breadth]
        accumulated = accumulated + jnp.einsum(
            "vrcd,vde->vrce", window, kernels[:, kernel_spot], preferred_element_type=jnp.float32
        )
    return accumulated


def refine(average, region, w_qkv, w_proj, bias_grid):
    normed = normalize(average).astype(jnp.bfloat16)[None]
    return average + attend(normed, region, w_qkv, w_proj, bias_grid)[0]


def local(
    features,
    labels,
    qkv_weight,
    proj_weight,
    up_weight,
    down_weight,
    swin_bias,
    recon_weight,
    refine_qkv,
    refine_proj,
    refine_bias,
):
    height, breadth, channels = features.shape
    variant_codes = lax.axis_index("var") * VAR_DEV + jnp.arange(VAR_DEV, dtype=jnp.int32)
    first_bias = bias_table(swin_bias[0], variant_codes)
    second_bias = bias_table(swin_bias[1], variant_codes)
    block_one = block_on_grid(
        features[None], labels, 0, qkv_weight, proj_weight, up_weight, down_weight, first_bias
    )
    tagged = jnp.broadcast_to(labels.astype(jnp.bfloat16)[None, :, :, None], block_one.shape[:3] + (1,))
    carried = extended(jnp.concatenate([block_one, tagged], axis=-1), (("ty", 1), ("tx", 2)), SHIFT)
    shifted = carried[..., :channels]
    region = carried[0, :, :, channels].astype(jnp.int32)
    block_two = block_on_grid(
        shifted, region, 1, qkv_weight, proj_weight, up_weight, down_weight, second_bias
    )
    padded = block_two[:, SHIFT - 1 : SHIFT + height + 1, SHIFT - 1 : SHIFT + breadth + 1]
    row = lax.axis_index("ty") * height - 1 + jnp.arange(height + 2)
    col = lax.axis_index("tx") * breadth - 1 + jnp.arange(breadth + 2)
    inside = ((row >= 0) & (row < lax.axis_size("ty") * height))[:, None] & (
        (col >= 0) & (col < lax.axis_size("tx") * breadth)
    )[None, :]
    padded = jnp.where(inside[None, :, :, None], padded, jnp.zeros_like(padded))
    kernels = variant_kernels(recon_weight, variant_codes)
    summed = jnp.sum(reconstruct(padded, kernels, height, breadth), axis=0)
    region_windows = to_windows(labels[None, :, :, None])[0, :, :, 0]
    refine_grid = bias_table(refine_bias, jnp.zeros((1,), jnp.int32))
    rows, cols, depth = summed.shape
    combined = var_sum(summed.astype(jnp.bfloat16).reshape(rows, cols * depth)).reshape(rows, cols, depth)
    refined = refine(
        to_windows(combined[None])[0] / 8.0, region_windows, refine_qkv, refine_proj, refine_grid
    )
    refined = lax.optimization_barrier(refined)
    colours = refined.shape[-1] // (SCALE * SCALE)
    picture = refined.reshape(
        height // WIN, breadth // WIN, WIN, WIN, colours * SCALE, SCALE
    ).transpose(4, 0, 2, 1, 3, 5)
    picture = picture.reshape(colours, SCALE, height, breadth * SCALE).transpose(0, 2, 1, 3)
    return picture.reshape(colours, SCALE * height, SCALE * breadth)


def solution(mesh):
    placed = (P("ty", "tx", None), P("ty", "tx"), P(), P(), P(), P(), P(), P(), P(), P(), P())
    return jax.shard_map(
        local, mesh=mesh, in_specs=placed, out_specs=P(None, "ty", "tx"), check_vma=False
    )
```

```python
import functools

import jax
import jax.numpy as jnp
from jax import lax
from jax.experimental import pallas as pl
from jax.experimental.pallas import tpu as pltpu
from jax.sharding import PartitionSpec as P

MESH = pl.DeviceIdType.MESH

WIN = 8
SHIFT = 4
SCALE = 4
VAR_DEV = 2


EPSILON = 1e-05
MASKED = -1e30


def extended(cells, sides, width):
    for axis, dim in sides:
        count = lax.axis_size(axis)
        ends = count - 1
        head = lax.slice_in_dim(cells, 0, width, axis=dim)
        tail = lax.slice_in_dim(cells, cells.shape[dim] - width, cells.shape[dim], axis=dim)
        cells = jnp.concatenate(
            [
                lax.ppermute(tail, axis, [(i, (i + 1) % count) for i in range(ends)]),
                cells,
                lax.ppermute(head, axis, [((i + 1) % count, i) for i in range(ends)]),
            ],
            axis=dim,
        )
    return cells


def var_sum_kernel(count, part_ref, out_ref, held, send_sem, recv_sem, own_sem):
    me = lax.axis_index("var")
    barrier = pltpu.get_barrier_semaphore()
    for step in range(1, count):
        peer = lax.rem(me + step, count)
        pl.semaphore_signal(barrier, inc=1, device_id={"var": peer}, device_id_type=MESH)
    pl.semaphore_wait(barrier, count - 1)
    own = pltpu.make_async_copy(part_ref, held.at[me], own_sem)
    own.start()
    sends = []
    for step in range(1, count):
        peer = lax.rem(me + step, count)
        copy = pltpu.make_async_remote_copy(
            src_ref=part_ref,
            dst_ref=held.at[me],
            send_sem=send_sem.at[step - 1],
            recv_sem=recv_sem.at[me],
            device_id={"var": peer},
            device_id_type=MESH,
        )
        copy.start()
        sends.append(copy)
    own.wait()
    for copy in sends:
        copy.wait_send()
    for step in range(1, count):
        source = lax.rem(me + count - step, count)
        pltpu.make_async_remote_copy(
            src_ref=part_ref,
            dst_ref=held.at[source],
            send_sem=send_sem.at[step - 1],
            recv_sem=recv_sem.at[source],
            device_id={"var": source},
            device_id_type=MESH,
        ).wait_recv()
    total = held[0].astype(jnp.float32)
    for index in range(1, count):
        total = total + held[index].astype(jnp.float32)
    out_ref[...] = total


def var_sum(part):
    count = lax.axis_size("var")
    return pl.pallas_call(
        functools.partial(var_sum_kernel, count),
        out_shape=jax.ShapeDtypeStruct(part.shape, jnp.float32),
        in_specs=[pl.BlockSpec(memory_space=pltpu.VMEM)],
        out_specs=pl.BlockSpec(memory_space=pltpu.VMEM),
        scratch_shapes=[
            pltpu.VMEM((count,) + part.shape, part.dtype),
            pltpu.SemaphoreType.DMA((count - 1,)),
            pltpu.SemaphoreType.DMA((count,)),
            pltpu.SemaphoreType.DMA(()),
        ],
        compiler_params=pltpu.CompilerParams(collective_id=0, has_side_effects=True),
    )(part)


GROUP = 4
LANE = 128


def block_kernel(
    variants, heads, scale, x_ref, labq_ref, labk_ref, bias_ref, wqkv_ref, wp_ref, wup_ref, wdown_ref, out_ref, wide_ref
):
    @pl.when(pl.program_id(0) == 0)
    def _():
        for variant in range(variants):
            for head in range(heads):
                wide_ref[variant, head] = jnp.concatenate([bias_ref[variant, head]] * GROUP, axis=1)

    inputs = x_ref.shape[0]
    tokens = x_ref.shape[2]
    labq = labq_ref[0]
    labk = labk_ref[0]
    slot_q = lax.broadcasted_iota(jnp.int32, (tokens, tokens), 0) // (WIN * WIN)
    slot_k = lax.broadcasted_iota(jnp.int32, (tokens, tokens), 1) // (WIN * WIN)
    match = (labq == labk) & (slot_q == slot_k)
    projected = []
    for index in range(inputs):
        normed = normalize(x_ref[index, 0]).astype(jnp.bfloat16)
        projected.append(
            jnp.dot(normed, wqkv_ref[...], preferred_element_type=jnp.float32).astype(jnp.bfloat16)
        )
    span = wp_ref.shape[0]
    width = wup_ref.shape[0] // heads
    lane = lax.broadcasted_iota(jnp.int32, (1, span), 1)
    for variant in range(variants):
        source = variant if inputs > 1 else 0
        qkv = projected[source]
        query = qkv[:, :span]
        key = qkv[:, span : 2 * span]
        value = qkv[:, 2 * span :]
        mixed = jnp.zeros((tokens, span), jnp.float32)
        for head in range(heads):
            mine = (lane >= head * width) & (lane < (head + 1) * width)
            scores = lax.dot_general(
                jnp.where(mine, query, jnp.zeros_like(query)),
                key,
                (((1,), (1,)), ((), ())),
                preferred_element_type=jnp.float32,
            )
            scores = scores * scale
            scores = (scores.reshape(GROUP, WIN * WIN, tokens) + wide_ref[variant, head][None]).reshape(
                tokens, tokens
            )
            scores = jnp.where(match, scores, MASKED)
            largest = jnp.max(scores, axis=-1, keepdims=True)
            weights = jnp.exp(scores - largest)
            probabilities = (weights / jnp.sum(weights, axis=-1, keepdims=True)).astype(jnp.bfloat16)
            mixed = mixed + jnp.dot(
                probabilities, jnp.where(mine, value, jnp.zeros_like(value)), preferred_element_type=jnp.float32
            )
        branch = jnp.dot(mixed.astype(jnp.bfloat16), wp_ref[...], preferred_element_type=jnp.float32)
        own = x_ref[source, 0].astype(jnp.float32)
        hidden_in = (own + branch).astype(jnp.bfloat16)
        normed = normalize(hidden_in).astype(jnp.bfloat16)
        hidden = jnp.dot(normed, wup_ref[...], preferred_element_type=jnp.float32)
        hidden = (0.5 * hidden * (1.0 + lax.erf(hidden * (2.0 ** -0.5)))).astype(jnp.bfloat16)
        result = hidden_in.astype(jnp.float32) + jnp.dot(
            hidden, wdown_ref[...], preferred_element_type=jnp.float32
        )
        out_ref[variant, 0] = result.astype(jnp.bfloat16)


def padded_weights(w_qkv, w_proj, heads):
    channels = w_proj.shape[0]
    span = -(-channels // LANE) * LANE
    columns = jnp.pad(w_qkv.reshape(channels, 3, channels), ((0, 0), (0, 0), (0, span - channels)))
    rows = jnp.pad(w_proj, ((0, span - channels), (0, 0)))
    return columns.reshape(channels, 3 * span), rows


def swin_block(windows, region, layer, w_qkv, w_proj, w_up, w_down, bias_grid):
    inputs, count, cells, channels = windows.shape
    variants, heads = bias_grid.shape[:2]
    groups = -(-count // GROUP)
    extra = groups * GROUP - count
    windows = jnp.pad(windows, ((0, 0), (0, extra), (0, 0), (0, 0)))
    region = jnp.pad(region, ((0, extra), (0, 0)))
    tokens = GROUP * cells
    x = windows.reshape(inputs, groups, tokens, channels)
    labq = region.reshape(groups, tokens, 1)
    labk = region.reshape(groups, 1, tokens)
    bias = bias_grid
    scale = (channels // heads) ** (-0.5)
    whole = lambda shape: pl.BlockSpec(shape, lambda g: (0,) * len(shape))
    out = pl.pallas_call(
        functools.partial(block_kernel, variants, heads, scale),
        out_shape=jax.ShapeDtypeStruct((variants, groups, tokens, channels), jnp.bfloat16),
        grid=(groups,),
        in_specs=[
            pl.BlockSpec((inputs, 1, tokens, channels), lambda g: (0, g, 0, 0)),
            pl.BlockSpec((1, tokens, 1), lambda g: (g, 0, 0)),
            pl.BlockSpec((1, 1, tokens), lambda g: (g, 0, 0)),
            whole(bias.shape),
            pl.BlockSpec((None,) + w_qkv.shape[1:], lambda g: (layer, 0, 0)),
            pl.BlockSpec((None,) + w_proj.shape[1:], lambda g: (layer, 0, 0)),
            pl.BlockSpec((None,) + w_up.shape[1:], lambda g: (layer, 0, 0)),
            pl.BlockSpec((None,) + w_down.shape[1:], lambda g: (layer, 0, 0)),
        ],
        out_specs=pl.BlockSpec((variants, 1, tokens, channels), lambda g: (0, g, 0, 0)),
        scratch_shapes=[pltpu.VMEM((variants, heads, cells, tokens), jnp.float32)],
        compiler_params=pltpu.CompilerParams(vmem_limit_bytes=48 * 1024 * 1024),
    )(x, labq, labk, bias, w_qkv, w_proj, w_up, w_down)
    out = out.reshape(variants, groups * GROUP, cells, channels)
    return out[:, :count]


def block_on_grid(tokens, region, layer, w_qkv, w_proj, w_up, w_down, bias_grid):
    height, breadth = tokens.shape[1], tokens.shape[2]
    windows = to_windows(tokens)
    region_windows = to_windows(region[None, :, :, None])[0, :, :, 0]
    out = swin_block(windows, region_windows, layer, w_qkv, w_proj, w_up, w_down, bias_grid)
    return from_windows(out, height, breadth)


def normalize(values):
    values = values.astype(jnp.float32)
    average = jnp.mean(values, axis=-1, keepdims=True)
    centred = values - average
    spread = jnp.mean(centred * centred, axis=-1, keepdims=True)
    return centred * lax.rsqrt(spread + EPSILON)


def to_windows(grid):
    leading, height, breadth, channels = grid.shape
    grid = grid.reshape(leading, height // WIN, WIN, breadth // WIN, WIN, channels)
    grid = grid.transpose(0, 1, 3, 2, 4, 5)
    return grid.reshape(leading, height // WIN * (breadth // WIN), WIN * WIN, channels)


def from_windows(windows, height, breadth):
    leading, window_count, cells, channels = windows.shape
    windows = windows.reshape(leading, height // WIN, breadth // WIN, WIN, WIN, channels)
    windows = windows.transpose(0, 1, 3, 2, 4, 5)
    return windows.reshape(leading, height, breadth, channels)


def bias_table(offset_table, variant_codes):
    position = jnp.arange(WIN * WIN, dtype=jnp.int32)
    row_step = (position // WIN)[:, None] - (position // WIN)[None, :]
    across = (position % WIN)[:, None] - (position % WIN)[None, :]
    transpose_bit = (variant_codes // 4)[:, None, None]
    flip_rows = (variant_codes // 2 % 2)[:, None, None]
    flip_cols = (variant_codes % 2)[:, None, None]
    row_moved = jnp.where(flip_rows == 1, -row_step, row_step)
    col_moved = jnp.where(flip_cols == 1, -across, across)
    leading_step = jnp.where(transpose_bit == 1, col_moved, row_moved)
    trailing_step = jnp.where(transpose_bit == 1, row_moved, col_moved)
    table_index = (leading_step + WIN - 1) * (2 * WIN - 1) + trailing_step + WIN - 1
    slots = jnp.arange((2 * WIN - 1) * (2 * WIN - 1), dtype=jnp.int32)
    one_hot = (table_index[..., None] == slots).astype(jnp.bfloat16)
    high = lax.reduce_precision(offset_table, exponent_bits=8, mantissa_bits=7)
    rest = offset_table - high
    middle = lax.reduce_precision(rest, exponent_bits=8, mantissa_bits=7)
    low = rest - middle
    parts = jnp.concatenate([high, middle, low], axis=0).astype(jnp.bfloat16)
    picked = jnp.einsum("vqkt,ht->vhqk", one_hot, parts, preferred_element_type=jnp.float32)
    heads = offset_table.shape[0]
    return (picked[:, :heads] + picked[:, heads : 2 * heads]) + picked[:, 2 * heads :]


def variant_kernels(kernel, variant_codes):
    transpose_bit = (variant_codes // 4)[:, None]
    flip_rows = (variant_codes // 2 % 2)[:, None]
    flip_cols = (variant_codes % 2)[:, None]
    kernel_spot = jnp.arange(9, dtype=jnp.int32)
    step_row = (kernel_spot // 3 - 1)[None, :]
    step_col = (kernel_spot % 3 - 1)[None, :]
    row_moved = jnp.where(flip_rows == 1, -step_row, step_row)
    col_moved = jnp.where(flip_cols == 1, -step_col, step_col)
    source_row = jnp.where(transpose_bit == 1, col_moved, row_moved)
    source_col = jnp.where(transpose_bit == 1, row_moved, col_moved)
    source = (source_row + 1) * 3 + source_col + 1
    pick_place = (source[:, :, None] == kernel_spot[None, None, :]).astype(jnp.bfloat16)
    channel = jnp.arange(kernel.shape[-1], dtype=jnp.int32)
    colour = (channel // (SCALE * SCALE))[None, :]
    sub_row = (channel % (SCALE * SCALE) // SCALE)[None, :]
    sub_col = (channel % SCALE)[None, :]
    sub_row_moved = jnp.where(flip_rows == 1, SCALE - 1 - sub_row, sub_row)
    sub_col_moved = jnp.where(flip_cols == 1, SCALE - 1 - sub_col, sub_col)
    anchor_row = jnp.where(transpose_bit == 1, sub_col_moved, sub_row_moved)
    anchor_col = jnp.where(transpose_bit == 1, sub_row_moved, sub_col_moved)
    anchor = colour * SCALE * SCALE + anchor_row * SCALE + anchor_col
    pick_channel = (channel[None, :, None] == anchor[:, None, :]).astype(jnp.bfloat16)
    placed = jnp.einsum(
        "vpq,qcs->vpcs", pick_place, kernel, preferred_element_type=jnp.float32
    ).astype(jnp.bfloat16)
    return jnp.einsum(
        "vpcs,vso->vpco", placed, pick_channel, preferred_element_type=jnp.float32
    ).astype(jnp.bfloat16)


def attend(normed, region, w_qkv, w_proj, bias_grid):
    head_count = bias_grid.shape[1]
    leading, window_count, cells, channels = normed.shape
    head_width = channels // head_count
    projected = jnp.einsum(
        "lnsc,ce->lnse", normed, w_qkv, preferred_element_type=jnp.float32
    ).astype(jnp.bfloat16)
    projected = projected.reshape(leading, window_count, cells, 3, head_count, head_width)
    queries = projected[:, :, :, 0]
    key_part = projected[:, :, :, 1]
    value_part = projected[:, :, :, 2]
    scores = jnp.einsum("lnqhd,lnkhd->lnhqk", queries, key_part, preferred_element_type=jnp.float32)
    scores = scores * head_width ** (-0.5) + bias_grid[:, None]
    matches = region[:, None, :, None] == region[:, None, None, :]
    scores = jnp.where(matches[None], scores, MASKED)
    largest = jnp.max(scores, axis=-1, keepdims=True)
    weights = jnp.exp(scores - largest)
    probabilities = (weights / jnp.sum(weights, axis=-1, keepdims=True)).astype(jnp.bfloat16)
    value_part = jnp.broadcast_to(value_part, (probabilities.shape[0],) + value_part.shape[1:])
    mixed = jnp.einsum(
        "lnhqk,lnkhd->lnqhd", probabilities, value_part, preferred_element_type=jnp.float32
    ).astype(jnp.bfloat16)
    mixed = mixed.reshape(probabilities.shape[0], window_count, cells, channels)
    return jnp.einsum("lnsc,ce->lnse", mixed, w_proj, preferred_element_type=jnp.float32)


def attention_half(tokens, region, w_qkv, w_proj, bias_grid):
    height, breadth = (tokens.shape[1], tokens.shape[2])
    windows = to_windows(tokens)
    region_windows = to_windows(region[None, :, :, None])[0, :, :, 0]
    normed = normalize(windows).astype(jnp.bfloat16)
    branch = attend(normed, region_windows, w_qkv, w_proj, bias_grid)
    result = (windows.astype(jnp.float32) + branch).astype(jnp.bfloat16)
    return from_windows(result, height, breadth)


def feed_forward(tokens, w_up, w_down):
    normed = normalize(tokens).astype(jnp.bfloat16)
    hidden = jnp.einsum("...c,ce->...e", normed, w_up, preferred_element_type=jnp.float32)
    hidden = jax.nn.gelu(hidden, approximate=False).astype(jnp.bfloat16)
    output = tokens.astype(jnp.float32) + jnp.einsum(
        "...e,ec->...c", hidden, w_down, preferred_element_type=jnp.float32
    )
    return output.astype(jnp.bfloat16)


def reconstruct(padded, kernels, height, breadth):
    accumulated = jnp.zeros((padded.shape[0], height, breadth, kernels.shape[-1]), jnp.float32)
    for kernel_spot in range(9):
        spot_row, spot_col = (kernel_spot // 3, kernel_spot % 3)
        window = padded[:, spot_row : spot_row + height, spot_col : spot_col + breadth]
        accumulated = accumulated + jnp.einsum(
            "vrcd,vde->vrce", window, kernels[:, kernel_spot], preferred_element_type=jnp.float32
        )
    return accumulated


def refine(average, region, w_qkv, w_proj, bias_grid):
    normed = normalize(average).astype(jnp.bfloat16)[None]
    return average + attend(normed, region, w_qkv, w_proj, bias_grid)[0]


def local(
    features,
    labels,
    qkv_weight,
    proj_weight,
    up_weight,
    down_weight,
    swin_bias,
    recon_weight,
    refine_qkv,
    refine_proj,
    refine_bias,
):
    height, breadth, channels = features.shape
    variant_codes = lax.axis_index("var") * VAR_DEV + jnp.arange(VAR_DEV, dtype=jnp.int32)
    first_bias = bias_table(swin_bias[0], variant_codes)
    second_bias = bias_table(swin_bias[1], variant_codes)
    block_one = block_on_grid(
        features[None], labels, 0, qkv_weight, proj_weight, up_weight, down_weight, first_bias
    )
    tagged = jnp.broadcast_to(labels.astype(jnp.bfloat16)[None, :, :, None], block_one.shape[:3] + (1,))
    carried = extended(jnp.concatenate([block_one, tagged], axis=-1), (("tx", 2), ("ty", 1)), SHIFT)
    shifted = carried[..., :channels]
    region = carried[0, :, :, channels].astype(jnp.int32)
    block_two = block_on_grid(
        shifted, region, 1, qkv_weight, proj_weight, up_weight, down_weight, second_bias
    )
    padded = block_two[:, SHIFT - 1 : SHIFT + height + 1, SHIFT - 1 : SHIFT + breadth + 1]
    row = lax.axis_index("ty") * height - 1 + jnp.arange(height + 2)
    col = lax.axis_index("tx") * breadth - 1 + jnp.arange(breadth + 2)
    inside = ((row >= 0) & (row < lax.axis_size("ty") * height))[:, None] & (
        (col >= 0) & (col < lax.axis_size("tx") * breadth)
    )[None, :]
    padded = jnp.where(inside[None, :, :, None], padded, jnp.zeros_like(padded))
    kernels = variant_kernels(recon_weight, variant_codes)
    summed = jnp.sum(reconstruct(padded, kernels, height, breadth), axis=0)
    region_windows = to_windows(labels[None, :, :, None])[0, :, :, 0]
    refine_grid = bias_table(refine_bias, jnp.zeros((1,), jnp.int32))
    rows, cols, depth = summed.shape
    combined = var_sum(summed.astype(jnp.bfloat16).reshape(rows, cols * depth)).reshape(rows, cols, depth)
    refined = refine(
        to_windows(combined[None])[0] / 8.0, region_windows, refine_qkv, refine_proj, refine_grid
    )
    refined = lax.optimization_barrier(refined)
    colours = refined.shape[-1] // (SCALE * SCALE)
    picture = refined.reshape(
        height // WIN, breadth // WIN, WIN, WIN, colours * SCALE, SCALE
    ).transpose(4, 0, 2, 1, 3, 5)
    picture = picture.reshape(colours, SCALE, height, breadth * SCALE).transpose(0, 2, 1, 3)
    return picture.reshape(colours, SCALE * height, SCALE * breadth)


def solution(mesh):
    placed = (P("ty", "tx", None), P("ty", "tx"), P(), P(), P(), P(), P(), P(), P(), P(), P())
    return jax.shard_map(
        local, mesh=mesh, in_specs=placed, out_specs=P(None, "ty", "tx"), check_vma=False
    )
```

```python
import functools

import jax
import jax.numpy as jnp
from jax import lax
from jax.experimental import pallas as pl
from jax.experimental.pallas import tpu as pltpu
from jax.sharding import PartitionSpec as P

MESH = pl.DeviceIdType.MESH

WIN = 8
SHIFT = 4
SCALE = 4
VAR_DEV = 2


EPSILON = 1e-05
MASKED = -1e30


def extended(cells, sides, width):
    for axis, dim in sides:
        count = lax.axis_size(axis)
        ends = count - 1
        head = lax.slice_in_dim(cells, 0, width, axis=dim)
        tail = lax.slice_in_dim(cells, cells.shape[dim] - width, cells.shape[dim], axis=dim)
        cells = jnp.concatenate(
            [
                lax.ppermute(tail, axis, [(i, (i + 1) % count) for i in range(ends)]),
                cells,
                lax.ppermute(head, axis, [((i + 1) % count, i) for i in range(ends)]),
            ],
            axis=dim,
        )
    return cells


def var_sum_kernel(count, part_ref, out_ref, held, send_sem, recv_sem, own_sem):
    me = lax.axis_index("var")
    barrier = pltpu.get_barrier_semaphore()
    for step in range(1, count):
        peer = lax.rem(me + step, count)
        pl.semaphore_signal(barrier, inc=1, device_id={"var": peer}, device_id_type=MESH)
    pl.semaphore_wait(barrier, count - 1)
    own = pltpu.make_async_copy(part_ref, held.at[me], own_sem)
    own.start()
    sends = []
    for step in range(1, count):
        peer = lax.rem(me + step, count)
        copy = pltpu.make_async_remote_copy(
            src_ref=part_ref,
            dst_ref=held.at[me],
            send_sem=send_sem.at[step - 1],
            recv_sem=recv_sem.at[me],
            device_id={"var": peer},
            device_id_type=MESH,
        )
        copy.start()
        sends.append(copy)
    own.wait()
    for copy in sends:
        copy.wait_send()
    for step in range(1, count):
        source = lax.rem(me + count - step, count)
        pltpu.make_async_remote_copy(
            src_ref=part_ref,
            dst_ref=held.at[source],
            send_sem=send_sem.at[step - 1],
            recv_sem=recv_sem.at[source],
            device_id={"var": source},
            device_id_type=MESH,
        ).wait_recv()
    total = held[0].astype(jnp.float32)
    for index in range(1, count):
        total = total + held[index].astype(jnp.float32)
    out_ref[...] = total


def var_sum(part):
    count = lax.axis_size("var")
    return pl.pallas_call(
        functools.partial(var_sum_kernel, count),
        out_shape=jax.ShapeDtypeStruct(part.shape, jnp.float32),
        in_specs=[pl.BlockSpec(memory_space=pltpu.VMEM)],
        out_specs=pl.BlockSpec(memory_space=pltpu.VMEM),
        scratch_shapes=[
            pltpu.VMEM((count,) + part.shape, part.dtype),
            pltpu.SemaphoreType.DMA((count - 1,)),
            pltpu.SemaphoreType.DMA((count,)),
            pltpu.SemaphoreType.DMA(()),
        ],
        compiler_params=pltpu.CompilerParams(collective_id=0, has_side_effects=True),
    )(part)


GROUP = 4
LANE = 128


def block_kernel(
    variants, heads, scale, x_ref, labq_ref, labk_ref, bias_ref, wqkv_ref, wp_ref, wup_ref, wdown_ref, out_ref, wide_ref
):
    @pl.when(pl.program_id(0) == 0)
    def _():
        for variant in range(variants):
            for head in range(heads):
                wide_ref[variant, head] = jnp.concatenate([bias_ref[variant, head]] * (wide_ref.shape[-1] // (WIN * WIN)), axis=1)

    inputs = x_ref.shape[0]
    tokens = x_ref.shape[2]
    labq = labq_ref[0]
    labk = labk_ref[0]
    slot_q = lax.broadcasted_iota(jnp.int32, (tokens, tokens), 0) // (WIN * WIN)
    slot_k = lax.broadcasted_iota(jnp.int32, (tokens, tokens), 1) // (WIN * WIN)
    match = (labq == labk) & (slot_q == slot_k)
    projected = []
    for index in range(inputs):
        normed = normalize(x_ref[index, 0]).astype(jnp.bfloat16)
        projected.append(
            jnp.dot(normed, wqkv_ref[...], preferred_element_type=jnp.float32).astype(jnp.bfloat16)
        )
    span = wp_ref.shape[0]
    width = wup_ref.shape[0] // heads
    lane = lax.broadcasted_iota(jnp.int32, (1, span), 1)
    for variant in range(variants):
        source = variant if inputs > 1 else 0
        qkv = projected[source]
        query = qkv[:, :span]
        key = qkv[:, span : 2 * span]
        value = qkv[:, 2 * span :]
        mixed = jnp.zeros((tokens, span), jnp.float32)
        for head in range(heads):
            mine = (lane >= head * width) & (lane < (head + 1) * width)
            scores = lax.dot_general(
                jnp.where(mine, query, jnp.zeros_like(query)),
                key,
                (((1,), (1,)), ((), ())),
                preferred_element_type=jnp.float32,
            )
            scores = scores * scale
            scores = (scores.reshape(tokens // (WIN * WIN), WIN * WIN, tokens) + wide_ref[variant, head][None]).reshape(
                tokens, tokens
            )
            scores = jnp.where(match, scores, MASKED)
            largest = jnp.max(scores, axis=-1, keepdims=True)
            weights = jnp.exp(scores - largest)
            probabilities = (weights / jnp.sum(weights, axis=-1, keepdims=True)).astype(jnp.bfloat16)
            mixed = mixed + jnp.dot(
                probabilities, jnp.where(mine, value, jnp.zeros_like(value)), preferred_element_type=jnp.float32
            )
        branch = jnp.dot(mixed.astype(jnp.bfloat16), wp_ref[...], preferred_element_type=jnp.float32)
        own = x_ref[source, 0].astype(jnp.float32)
        hidden_in = (own + branch).astype(jnp.bfloat16)
        normed = normalize(hidden_in).astype(jnp.bfloat16)
        hidden = jnp.dot(normed, wup_ref[...], preferred_element_type=jnp.float32)
        hidden = (0.5 * hidden * (1.0 + lax.erf(hidden * (2.0 ** -0.5)))).astype(jnp.bfloat16)
        result = hidden_in.astype(jnp.float32) + jnp.dot(
            hidden, wdown_ref[...], preferred_element_type=jnp.float32
        )
        out_ref[variant, 0] = result.astype(jnp.bfloat16)


def padded_weights(w_qkv, w_proj, heads):
    channels = w_proj.shape[0]
    span = -(-channels // LANE) * LANE
    columns = jnp.pad(w_qkv.reshape(channels, 3, channels), ((0, 0), (0, 0), (0, span - channels)))
    rows = jnp.pad(w_proj, ((0, span - channels), (0, 0)))
    return columns.reshape(channels, 3 * span), rows


def swin_block(windows, region, layer, w_qkv, w_proj, w_up, w_down, bias_grid):
    inputs, count, cells, channels = windows.shape
    variants, heads = bias_grid.shape[:2]
    size = 5 if count % GROUP and count % 5 == 0 else GROUP
    groups = -(-count // size)
    extra = groups * size - count
    windows = jnp.pad(windows, ((0, 0), (0, extra), (0, 0), (0, 0)))
    region = jnp.pad(region, ((0, extra), (0, 0)))
    tokens = size * cells
    x = windows.reshape(inputs, groups, tokens, channels)
    labq = region.reshape(groups, tokens, 1)
    labk = region.reshape(groups, 1, tokens)
    bias = bias_grid
    scale = (channels // heads) ** (-0.5)
    whole = lambda shape: pl.BlockSpec(shape, lambda g: (0,) * len(shape))
    out = pl.pallas_call(
        functools.partial(block_kernel, variants, heads, scale),
        out_shape=jax.ShapeDtypeStruct((variants, groups, tokens, channels), jnp.bfloat16),
        grid=(groups,),
        in_specs=[
            pl.BlockSpec((inputs, 1, tokens, channels), lambda g: (0, g, 0, 0)),
            pl.BlockSpec((1, tokens, 1), lambda g: (g, 0, 0)),
            pl.BlockSpec((1, 1, tokens), lambda g: (g, 0, 0)),
            whole(bias.shape),
            pl.BlockSpec((None,) + w_qkv.shape[1:], lambda g: (layer, 0, 0)),
            pl.BlockSpec((None,) + w_proj.shape[1:], lambda g: (layer, 0, 0)),
            pl.BlockSpec((None,) + w_up.shape[1:], lambda g: (layer, 0, 0)),
            pl.BlockSpec((None,) + w_down.shape[1:], lambda g: (layer, 0, 0)),
        ],
        out_specs=pl.BlockSpec((variants, 1, tokens, channels), lambda g: (0, g, 0, 0)),
        scratch_shapes=[pltpu.VMEM((variants, heads, cells, tokens), jnp.float32)],
        compiler_params=pltpu.CompilerParams(vmem_limit_bytes=48 * 1024 * 1024),
    )(x, labq, labk, bias, w_qkv, w_proj, w_up, w_down)
    out = out.reshape(variants, groups * size, cells, channels)
    return out[:, :count]


def block_on_grid(tokens, region, layer, w_qkv, w_proj, w_up, w_down, bias_grid):
    height, breadth = tokens.shape[1], tokens.shape[2]
    windows = to_windows(tokens)
    region_windows = to_windows(region[None, :, :, None])[0, :, :, 0]
    out = swin_block(windows, region_windows, layer, w_qkv, w_proj, w_up, w_down, bias_grid)
    return from_windows(out, height, breadth)


def normalize(values):
    values = values.astype(jnp.float32)
    average = jnp.mean(values, axis=-1, keepdims=True)
    centred = values - average
    spread = jnp.mean(centred * centred, axis=-1, keepdims=True)
    return centred * lax.rsqrt(spread + EPSILON)


def to_windows(grid):
    leading, height, breadth, channels = grid.shape
    grid = grid.reshape(leading, height // WIN, WIN, breadth // WIN, WIN, channels)
    grid = grid.transpose(0, 1, 3, 2, 4, 5)
    return grid.reshape(leading, height // WIN * (breadth // WIN), WIN * WIN, channels)


def from_windows(windows, height, breadth):
    leading, window_count, cells, channels = windows.shape
    windows = windows.reshape(leading, height // WIN, breadth // WIN, WIN, WIN, channels)
    windows = windows.transpose(0, 1, 3, 2, 4, 5)
    return windows.reshape(leading, height, breadth, channels)


def bias_table(offset_table, variant_codes):
    position = jnp.arange(WIN * WIN, dtype=jnp.int32)
    row_step = (position // WIN)[:, None] - (position // WIN)[None, :]
    across = (position % WIN)[:, None] - (position % WIN)[None, :]
    transpose_bit = (variant_codes // 4)[:, None, None]
    flip_rows = (variant_codes // 2 % 2)[:, None, None]
    flip_cols = (variant_codes % 2)[:, None, None]
    row_moved = jnp.where(flip_rows == 1, -row_step, row_step)
    col_moved = jnp.where(flip_cols == 1, -across, across)
    leading_step = jnp.where(transpose_bit == 1, col_moved, row_moved)
    trailing_step = jnp.where(transpose_bit == 1, row_moved, col_moved)
    table_index = (leading_step + WIN - 1) * (2 * WIN - 1) + trailing_step + WIN - 1
    slots = jnp.arange((2 * WIN - 1) * (2 * WIN - 1), dtype=jnp.int32)
    one_hot = (table_index[..., None] == slots).astype(jnp.bfloat16)
    high = lax.reduce_precision(offset_table, exponent_bits=8, mantissa_bits=7)
    rest = offset_table - high
    middle = lax.reduce_precision(rest, exponent_bits=8, mantissa_bits=7)
    low = rest - middle
    parts = jnp.concatenate([high, middle, low], axis=0).astype(jnp.bfloat16)
    picked = jnp.einsum("vqkt,ht->vhqk", one_hot, parts, preferred_element_type=jnp.float32)
    heads = offset_table.shape[0]
    return (picked[:, :heads] + picked[:, heads : 2 * heads]) + picked[:, 2 * heads :]


def variant_kernels(kernel, variant_codes):
    transpose_bit = (variant_codes // 4)[:, None]
    flip_rows = (variant_codes // 2 % 2)[:, None]
    flip_cols = (variant_codes % 2)[:, None]
    kernel_spot = jnp.arange(9, dtype=jnp.int32)
    step_row = (kernel_spot // 3 - 1)[None, :]
    step_col = (kernel_spot % 3 - 1)[None, :]
    row_moved = jnp.where(flip_rows == 1, -step_row, step_row)
    col_moved = jnp.where(flip_cols == 1, -step_col, step_col)
    source_row = jnp.where(transpose_bit == 1, col_moved, row_moved)
    source_col = jnp.where(transpose_bit == 1, row_moved, col_moved)
    source = (source_row + 1) * 3 + source_col + 1
    pick_place = (source[:, :, None] == kernel_spot[None, None, :]).astype(jnp.bfloat16)
    channel = jnp.arange(kernel.shape[-1], dtype=jnp.int32)
    colour = (channel // (SCALE * SCALE))[None, :]
    sub_row = (channel % (SCALE * SCALE) // SCALE)[None, :]
    sub_col = (channel % SCALE)[None, :]
    sub_row_moved = jnp.where(flip_rows == 1, SCALE - 1 - sub_row, sub_row)
    sub_col_moved = jnp.where(flip_cols == 1, SCALE - 1 - sub_col, sub_col)
    anchor_row = jnp.where(transpose_bit == 1, sub_col_moved, sub_row_moved)
    anchor_col = jnp.where(transpose_bit == 1, sub_row_moved, sub_col_moved)
    anchor = colour * SCALE * SCALE + anchor_row * SCALE + anchor_col
    pick_channel = (channel[None, :, None] == anchor[:, None, :]).astype(jnp.bfloat16)
    placed = jnp.einsum(
        "vpq,qcs->vpcs", pick_place, kernel, preferred_element_type=jnp.float32
    ).astype(jnp.bfloat16)
    return jnp.einsum(
        "vpcs,vso->vpco", placed, pick_channel, preferred_element_type=jnp.float32
    ).astype(jnp.bfloat16)


def attend(normed, region, w_qkv, w_proj, bias_grid):
    head_count = bias_grid.shape[1]
    leading, window_count, cells, channels = normed.shape
    head_width = channels // head_count
    projected = jnp.einsum(
        "lnsc,ce->lnse", normed, w_qkv, preferred_element_type=jnp.float32
    ).astype(jnp.bfloat16)
    projected = projected.reshape(leading, window_count, cells, 3, head_count, head_width)
    queries = projected[:, :, :, 0]
    key_part = projected[:, :, :, 1]
    value_part = projected[:, :, :, 2]
    scores = jnp.einsum("lnqhd,lnkhd->lnhqk", queries, key_part, preferred_element_type=jnp.float32)
    scores = scores * head_width ** (-0.5) + bias_grid[:, None]
    matches = region[:, None, :, None] == region[:, None, None, :]
    scores = jnp.where(matches[None], scores, MASKED)
    largest = jnp.max(scores, axis=-1, keepdims=True)
    weights = jnp.exp(scores - largest)
    probabilities = (weights / jnp.sum(weights, axis=-1, keepdims=True)).astype(jnp.bfloat16)
    value_part = jnp.broadcast_to(value_part, (probabilities.shape[0],) + value_part.shape[1:])
    mixed = jnp.einsum(
        "lnhqk,lnkhd->lnqhd", probabilities, value_part, preferred_element_type=jnp.float32
    ).astype(jnp.bfloat16)
    mixed = mixed.reshape(probabilities.shape[0], window_count, cells, channels)
    return jnp.einsum("lnsc,ce->lnse", mixed, w_proj, preferred_element_type=jnp.float32)


def attention_half(tokens, region, w_qkv, w_proj, bias_grid):
    height, breadth = (tokens.shape[1], tokens.shape[2])
    windows = to_windows(tokens)
    region_windows = to_windows(region[None, :, :, None])[0, :, :, 0]
    normed = normalize(windows).astype(jnp.bfloat16)
    branch = attend(normed, region_windows, w_qkv, w_proj, bias_grid)
    result = (windows.astype(jnp.float32) + branch).astype(jnp.bfloat16)
    return from_windows(result, height, breadth)


def feed_forward(tokens, w_up, w_down):
    normed = normalize(tokens).astype(jnp.bfloat16)
    hidden = jnp.einsum("...c,ce->...e", normed, w_up, preferred_element_type=jnp.float32)
    hidden = jax.nn.gelu(hidden, approximate=False).astype(jnp.bfloat16)
    output = tokens.astype(jnp.float32) + jnp.einsum(
        "...e,ec->...c", hidden, w_down, preferred_element_type=jnp.float32
    )
    return output.astype(jnp.bfloat16)


def reconstruct(padded, kernels, height, breadth):
    accumulated = jnp.zeros((padded.shape[0], height, breadth, kernels.shape[-1]), jnp.float32)
    for kernel_spot in range(9):
        spot_row, spot_col = (kernel_spot // 3, kernel_spot % 3)
        window = padded[:, spot_row : spot_row + height, spot_col : spot_col + breadth]
        accumulated = accumulated + jnp.einsum(
            "vrcd,vde->vrce", window, kernels[:, kernel_spot], preferred_element_type=jnp.float32
        )
    return accumulated


def refine(average, region, w_qkv, w_proj, bias_grid):
    normed = normalize(average).astype(jnp.bfloat16)[None]
    return average + attend(normed, region, w_qkv, w_proj, bias_grid)[0]


def local(
    features,
    labels,
    qkv_weight,
    proj_weight,
    up_weight,
    down_weight,
    swin_bias,
    recon_weight,
    refine_qkv,
    refine_proj,
    refine_bias,
):
    height, breadth, channels = features.shape
    variant_codes = lax.axis_index("var") * VAR_DEV + jnp.arange(VAR_DEV, dtype=jnp.int32)
    first_bias = bias_table(swin_bias[0], variant_codes)
    second_bias = bias_table(swin_bias[1], variant_codes)
    block_one = block_on_grid(
        features[None], labels, 0, qkv_weight, proj_weight, up_weight, down_weight, first_bias
    )
    tagged = jnp.broadcast_to(labels.astype(jnp.bfloat16)[None, :, :, None], block_one.shape[:3] + (1,))
    carried = extended(jnp.concatenate([block_one, tagged], axis=-1), (("tx", 2), ("ty", 1)), SHIFT)
    shifted = carried[..., :channels]
    region = carried[0, :, :, channels].astype(jnp.int32)
    block_two = block_on_grid(
        shifted, region, 1, qkv_weight, proj_weight, up_weight, down_weight, second_bias
    )
    padded = block_two[:, SHIFT - 1 : SHIFT + height + 1, SHIFT - 1 : SHIFT + breadth + 1]
    row = lax.axis_index("ty") * height - 1 + jnp.arange(height + 2)
    col = lax.axis_index("tx") * breadth - 1 + jnp.arange(breadth + 2)
    inside = ((row >= 0) & (row < lax.axis_size("ty") * height))[:, None] & (
        (col >= 0) & (col < lax.axis_size("tx") * breadth)
    )[None, :]
    padded = jnp.where(inside[None, :, :, None], padded, jnp.zeros_like(padded))
    kernels = variant_kernels(recon_weight, variant_codes)
    summed = jnp.sum(reconstruct(padded, kernels, height, breadth), axis=0)
    region_windows = to_windows(labels[None, :, :, None])[0, :, :, 0]
    refine_grid = bias_table(refine_bias, jnp.zeros((1,), jnp.int32))
    rows, cols, depth = summed.shape
    combined = var_sum(summed.astype(jnp.bfloat16).reshape(rows, cols * depth)).reshape(rows, cols, depth)
    refined = refine(
        to_windows(combined[None])[0] / 8.0, region_windows, refine_qkv, refine_proj, refine_grid
    )
    refined = lax.optimization_barrier(refined)
    colours = refined.shape[-1] // (SCALE * SCALE)
    picture = refined.reshape(
        height // WIN, breadth // WIN, WIN, WIN, colours * SCALE, SCALE
    ).transpose(4, 0, 2, 1, 3, 5)
    picture = picture.reshape(colours, SCALE, height, breadth * SCALE).transpose(0, 2, 1, 3)
    return picture.reshape(colours, SCALE * height, SCALE * breadth)


def solution(mesh):
    placed = (P("ty", "tx", None), P("ty", "tx"), P(), P(), P(), P(), P(), P(), P(), P(), P())
    return jax.shard_map(
        local, mesh=mesh, in_specs=placed, out_specs=P(None, "ty", "tx"), check_vma=False
    )
```

```python
import functools

import jax
import jax.numpy as jnp
from jax import lax
from jax.experimental import pallas as pl
from jax.experimental.pallas import tpu as pltpu
from jax.sharding import PartitionSpec as P

MESH = pl.DeviceIdType.MESH

WIN = 8
SHIFT = 4
SCALE = 4
VAR_DEV = 2


EPSILON = 1e-05
MASKED = -1e30


def extended(cells, sides, width):
    for axis, dim in sides:
        count = lax.axis_size(axis)
        ends = count - 1
        head = lax.slice_in_dim(cells, 0, width, axis=dim)
        tail = lax.slice_in_dim(cells, cells.shape[dim] - width, cells.shape[dim], axis=dim)
        cells = jnp.concatenate(
            [
                lax.ppermute(tail, axis, [(i, (i + 1) % count) for i in range(ends)]),
                cells,
                lax.ppermute(head, axis, [((i + 1) % count, i) for i in range(ends)]),
            ],
            axis=dim,
        )
    return cells


def var_sum_kernel(count, part_ref, out_ref, held, send_sem, recv_sem, own_sem):
    me = lax.axis_index("var")
    barrier = pltpu.get_barrier_semaphore()
    for step in range(1, count):
        peer = lax.rem(me + step, count)
        pl.semaphore_signal(barrier, inc=1, device_id={"var": peer}, device_id_type=MESH)
    pl.semaphore_wait(barrier, count - 1)
    own = pltpu.make_async_copy(part_ref, held.at[me], own_sem)
    own.start()
    sends = []
    for step in range(1, count):
        peer = lax.rem(me + step, count)
        copy = pltpu.make_async_remote_copy(
            src_ref=part_ref,
            dst_ref=held.at[me],
            send_sem=send_sem.at[step - 1],
            recv_sem=recv_sem.at[me],
            device_id={"var": peer},
            device_id_type=MESH,
        )
        copy.start()
        sends.append(copy)
    own.wait()
    for copy in sends:
        copy.wait_send()
    for step in range(1, count):
        source = lax.rem(me + count - step, count)
        pltpu.make_async_remote_copy(
            src_ref=part_ref,
            dst_ref=held.at[source],
            send_sem=send_sem.at[step - 1],
            recv_sem=recv_sem.at[source],
            device_id={"var": source},
            device_id_type=MESH,
        ).wait_recv()
    total = held[0].astype(jnp.float32)
    for index in range(1, count):
        total = total + held[index].astype(jnp.float32)
    out_ref[...] = total


def var_sum(part):
    count = lax.axis_size("var")
    return pl.pallas_call(
        functools.partial(var_sum_kernel, count),
        out_shape=jax.ShapeDtypeStruct(part.shape, jnp.float32),
        in_specs=[pl.BlockSpec(memory_space=pltpu.VMEM)],
        out_specs=pl.BlockSpec(memory_space=pltpu.VMEM),
        scratch_shapes=[
            pltpu.VMEM((count,) + part.shape, part.dtype),
            pltpu.SemaphoreType.DMA((count - 1,)),
            pltpu.SemaphoreType.DMA((count,)),
            pltpu.SemaphoreType.DMA(()),
        ],
        compiler_params=pltpu.CompilerParams(collective_id=0, has_side_effects=True),
    )(part)


GROUP = 4
LANE = 128


def block_kernel(
    variants, heads, scale, x_ref, labq_ref, labk_ref, bias_ref, wqkv_ref, wp_ref, wup_ref, wdown_ref, out_ref, wide_ref
):
    @pl.when(pl.program_id(0) == 0)
    def _():
        for variant in range(variants):
            for head in range(heads):
                wide_ref[variant, head] = jnp.concatenate([bias_ref[variant, head]] * (wide_ref.shape[-1] // (WIN * WIN)), axis=1)

    inputs = x_ref.shape[0]
    tokens = x_ref.shape[2]
    labq = labq_ref[0]
    labk = labk_ref[0]
    slot_q = lax.broadcasted_iota(jnp.int32, (tokens, tokens), 0) // (WIN * WIN)
    slot_k = lax.broadcasted_iota(jnp.int32, (tokens, tokens), 1) // (WIN * WIN)
    match = (labq == labk) & (slot_q == slot_k)
    projected = []
    for index in range(inputs):
        normed = normalize(x_ref[index, 0]).astype(jnp.bfloat16)
        projected.append(
            jnp.dot(normed, wqkv_ref[...], preferred_element_type=jnp.float32).astype(jnp.bfloat16)
        )
    span = wp_ref.shape[0]
    width = wup_ref.shape[0] // heads
    lane = lax.broadcasted_iota(jnp.int32, (1, span), 1)
    for variant in range(variants):
        source = variant if inputs > 1 else 0
        qkv = projected[source]
        query = qkv[:, :span]
        key = qkv[:, span : 2 * span]
        value = qkv[:, 2 * span :]
        mixed = jnp.zeros((tokens, span), jnp.float32)
        for head in range(heads):
            mine = (lane >= head * width) & (lane < (head + 1) * width)
            scores = lax.dot_general(
                jnp.where(mine, query, jnp.zeros_like(query)),
                key,
                (((1,), (1,)), ((), ())),
                preferred_element_type=jnp.float32,
            )
            scores = scores * scale
            scores = (scores.reshape(tokens // (WIN * WIN), WIN * WIN, tokens) + wide_ref[variant, head][None]).reshape(
                tokens, tokens
            )
            scores = jnp.where(match, scores, MASKED)
            largest = jnp.max(scores, axis=-1, keepdims=True)
            weights = jnp.exp(scores - largest)
            probabilities = (weights / jnp.sum(weights, axis=-1, keepdims=True)).astype(jnp.bfloat16)
            mixed = mixed + jnp.dot(
                probabilities, jnp.where(mine, value, jnp.zeros_like(value)), preferred_element_type=jnp.float32
            )
        branch = jnp.dot(mixed.astype(jnp.bfloat16), wp_ref[...], preferred_element_type=jnp.float32)
        own = x_ref[source, 0].astype(jnp.float32)
        hidden_in = (own + branch).astype(jnp.bfloat16)
        normed = normalize(hidden_in).astype(jnp.bfloat16)
        hidden = jnp.dot(normed, wup_ref[...], preferred_element_type=jnp.float32)
        hidden = (0.5 * hidden * (1.0 + lax.erf(hidden * (2.0 ** -0.5)))).astype(jnp.bfloat16)
        result = hidden_in.astype(jnp.float32) + jnp.dot(
            hidden, wdown_ref[...], preferred_element_type=jnp.float32
        )
        out_ref[variant, 0] = result.astype(jnp.bfloat16)


def padded_weights(w_qkv, w_proj, heads):
    channels = w_proj.shape[0]
    span = -(-channels // LANE) * LANE
    columns = jnp.pad(w_qkv.reshape(channels, 3, channels), ((0, 0), (0, 0), (0, span - channels)))
    rows = jnp.pad(w_proj, ((0, span - channels), (0, 0)))
    return columns.reshape(channels, 3 * span), rows


def swin_block(windows, region, layer, w_qkv, w_proj, w_up, w_down, bias_grid):
    inputs, count, cells, channels = windows.shape
    variants, heads = bias_grid.shape[:2]
    size = 5 if count % GROUP and count % 5 == 0 else GROUP
    groups = -(-count // size)
    extra = groups * size - count
    windows = jnp.pad(windows, ((0, 0), (0, extra), (0, 0), (0, 0)))
    region = jnp.pad(region, ((0, extra), (0, 0)))
    tokens = size * cells
    x = windows.reshape(inputs, groups, tokens, channels)
    labq = region.reshape(groups, tokens, 1)
    labk = region.reshape(groups, 1, tokens)
    bias = bias_grid
    scale = (channels // heads) ** (-0.5)
    whole = lambda shape: pl.BlockSpec(shape, lambda g: (0,) * len(shape))
    out = pl.pallas_call(
        functools.partial(block_kernel, variants, heads, scale),
        out_shape=jax.ShapeDtypeStruct((variants, groups, tokens, channels), jnp.bfloat16),
        grid=(groups,),
        in_specs=[
            pl.BlockSpec((inputs, 1, tokens, channels), lambda g: (0, g, 0, 0)),
            pl.BlockSpec((1, tokens, 1), lambda g: (g, 0, 0)),
            pl.BlockSpec((1, 1, tokens), lambda g: (g, 0, 0)),
            whole(bias.shape),
            pl.BlockSpec((None,) + w_qkv.shape[1:], lambda g: (layer, 0, 0)),
            pl.BlockSpec((None,) + w_proj.shape[1:], lambda g: (layer, 0, 0)),
            pl.BlockSpec((None,) + w_up.shape[1:], lambda g: (layer, 0, 0)),
            pl.BlockSpec((None,) + w_down.shape[1:], lambda g: (layer, 0, 0)),
        ],
        out_specs=pl.BlockSpec((variants, 1, tokens, channels), lambda g: (0, g, 0, 0)),
        scratch_shapes=[pltpu.VMEM((variants, heads, cells, tokens), jnp.float32)],
        compiler_params=pltpu.CompilerParams(vmem_limit_bytes=48 * 1024 * 1024),
    )(x, labq, labk, bias, w_qkv, w_proj, w_up, w_down)
    out = out.reshape(variants, groups * size, cells, channels)
    return out[:, :count]


def block_on_grid(tokens, region, layer, w_qkv, w_proj, w_up, w_down, bias_grid):
    height, breadth = tokens.shape[1], tokens.shape[2]
    windows = to_windows(tokens)
    region_windows = to_windows(region[None, :, :, None])[0, :, :, 0]
    out = swin_block(windows, region_windows, layer, w_qkv, w_proj, w_up, w_down, bias_grid)
    return from_windows(out, height, breadth)


def halo(cells, width):
    rows_of, cols_of = lax.axis_size("ty"), lax.axis_size("tx")
    height, breadth = cells.shape[1], cells.shape[2]
    rows = {-1: slice(height - width, height), 0: slice(0, height), 1: slice(0, width)}
    cols = {-1: slice(breadth - width, breadth), 0: slice(0, breadth), 1: slice(0, width)}
    pieces = {}
    for dy in (-1, 0, 1):
        for dx in (-1, 0, 1):
            if dy == 0 and dx == 0:
                pieces[(dy, dx)] = cells
                continue
            pairs = [
                ((y + dy) * cols_of + x + dx, y * cols_of + x)
                for y in range(rows_of)
                for x in range(cols_of)
                if 0 <= y + dy < rows_of and 0 <= x + dx < cols_of
            ]
            pieces[(dy, dx)] = lax.ppermute(cells[:, rows[dy], cols[dx]], ("ty", "tx"), pairs)
    bands = [jnp.concatenate([pieces[(dy, dx)] for dx in (-1, 0, 1)], axis=2) for dy in (-1, 0, 1)]
    return jnp.concatenate(bands, axis=1)


def normalize(values):
    values = values.astype(jnp.float32)
    average = jnp.mean(values, axis=-1, keepdims=True)
    centred = values - average
    spread = jnp.mean(centred * centred, axis=-1, keepdims=True)
    return centred * lax.rsqrt(spread + EPSILON)


def to_windows(grid):
    leading, height, breadth, channels = grid.shape
    grid = grid.reshape(leading, height // WIN, WIN, breadth // WIN, WIN, channels)
    grid = grid.transpose(0, 1, 3, 2, 4, 5)
    return grid.reshape(leading, height // WIN * (breadth // WIN), WIN * WIN, channels)


def from_windows(windows, height, breadth):
    leading, window_count, cells, channels = windows.shape
    windows = windows.reshape(leading, height // WIN, breadth // WIN, WIN, WIN, channels)
    windows = windows.transpose(0, 1, 3, 2, 4, 5)
    return windows.reshape(leading, height, breadth, channels)


def bias_table(offset_table, variant_codes):
    position = jnp.arange(WIN * WIN, dtype=jnp.int32)
    row_step = (position // WIN)[:, None] - (position // WIN)[None, :]
    across = (position % WIN)[:, None] - (position % WIN)[None, :]
    transpose_bit = (variant_codes // 4)[:, None, None]
    flip_rows = (variant_codes // 2 % 2)[:, None, None]
    flip_cols = (variant_codes % 2)[:, None, None]
    row_moved = jnp.where(flip_rows == 1, -row_step, row_step)
    col_moved = jnp.where(flip_cols == 1, -across, across)
    leading_step = jnp.where(transpose_bit == 1, col_moved, row_moved)
    trailing_step = jnp.where(transpose_bit == 1, row_moved, col_moved)
    table_index = (leading_step + WIN - 1) * (2 * WIN - 1) + trailing_step + WIN - 1
    slots = jnp.arange((2 * WIN - 1) * (2 * WIN - 1), dtype=jnp.int32)
    one_hot = (table_index[..., None] == slots).astype(jnp.bfloat16)
    high = lax.reduce_precision(offset_table, exponent_bits=8, mantissa_bits=7)
    rest = offset_table - high
    middle = lax.reduce_precision(rest, exponent_bits=8, mantissa_bits=7)
    low = rest - middle
    parts = jnp.concatenate([high, middle, low], axis=0).astype(jnp.bfloat16)
    picked = jnp.einsum("vqkt,ht->vhqk", one_hot, parts, preferred_element_type=jnp.float32)
    heads = offset_table.shape[0]
    return (picked[:, :heads] + picked[:, heads : 2 * heads]) + picked[:, 2 * heads :]


def variant_kernels(kernel, variant_codes):
    transpose_bit = (variant_codes // 4)[:, None]
    flip_rows = (variant_codes // 2 % 2)[:, None]
    flip_cols = (variant_codes % 2)[:, None]
    kernel_spot = jnp.arange(9, dtype=jnp.int32)
    step_row = (kernel_spot // 3 - 1)[None, :]
    step_col = (kernel_spot % 3 - 1)[None, :]
    row_moved = jnp.where(flip_rows == 1, -step_row, step_row)
    col_moved = jnp.where(flip_cols == 1, -step_col, step_col)
    source_row = jnp.where(transpose_bit == 1, col_moved, row_moved)
    source_col = jnp.where(transpose_bit == 1, row_moved, col_moved)
    source = (source_row + 1) * 3 + source_col + 1
    pick_place = (source[:, :, None] == kernel_spot[None, None, :]).astype(jnp.bfloat16)
    channel = jnp.arange(kernel.shape[-1], dtype=jnp.int32)
    colour = (channel // (SCALE * SCALE))[None, :]
    sub_row = (channel % (SCALE * SCALE) // SCALE)[None, :]
    sub_col = (channel % SCALE)[None, :]
    sub_row_moved = jnp.where(flip_rows == 1, SCALE - 1 - sub_row, sub_row)
    sub_col_moved = jnp.where(flip_cols == 1, SCALE - 1 - sub_col, sub_col)
    anchor_row = jnp.where(transpose_bit == 1, sub_col_moved, sub_row_moved)
    anchor_col = jnp.where(transpose_bit == 1, sub_row_moved, sub_col_moved)
    anchor = colour * SCALE * SCALE + anchor_row * SCALE + anchor_col
    pick_channel = (channel[None, :, None] == anchor[:, None, :]).astype(jnp.bfloat16)
    placed = jnp.einsum(
        "vpq,qcs->vpcs", pick_place, kernel, preferred_element_type=jnp.float32
    ).astype(jnp.bfloat16)
    return jnp.einsum(
        "vpcs,vso->vpco", placed, pick_channel, preferred_element_type=jnp.float32
    ).astype(jnp.bfloat16)


def attend(normed, region, w_qkv, w_proj, bias_grid):
    head_count = bias_grid.shape[1]
    leading, window_count, cells, channels = normed.shape
    head_width = channels // head_count
    projected = jnp.einsum(
        "lnsc,ce->lnse", normed, w_qkv, preferred_element_type=jnp.float32
    ).astype(jnp.bfloat16)
    projected = projected.reshape(leading, window_count, cells, 3, head_count, head_width)
    queries = projected[:, :, :, 0]
    key_part = projected[:, :, :, 1]
    value_part = projected[:, :, :, 2]
    scores = jnp.einsum("lnqhd,lnkhd->lnhqk", queries, key_part, preferred_element_type=jnp.float32)
    scores = scores * head_width ** (-0.5) + bias_grid[:, None]
    matches = region[:, None, :, None] == region[:, None, None, :]
    scores = jnp.where(matches[None], scores, MASKED)
    largest = jnp.max(scores, axis=-1, keepdims=True)
    weights = jnp.exp(scores - largest)
    probabilities = (weights / jnp.sum(weights, axis=-1, keepdims=True)).astype(jnp.bfloat16)
    value_part = jnp.broadcast_to(value_part, (probabilities.shape[0],) + value_part.shape[1:])
    mixed = jnp.einsum(
        "lnhqk,lnkhd->lnqhd", probabilities, value_part, preferred_element_type=jnp.float32
    ).astype(jnp.bfloat16)
    mixed = mixed.reshape(probabilities.shape[0], window_count, cells, channels)
    return jnp.einsum("lnsc,ce->lnse", mixed, w_proj, preferred_element_type=jnp.float32)


def attention_half(tokens, region, w_qkv, w_proj, bias_grid):
    height, breadth = (tokens.shape[1], tokens.shape[2])
    windows = to_windows(tokens)
    region_windows = to_windows(region[None, :, :, None])[0, :, :, 0]
    normed = normalize(windows).astype(jnp.bfloat16)
    branch = attend(normed, region_windows, w_qkv, w_proj, bias_grid)
    result = (windows.astype(jnp.float32) + branch).astype(jnp.bfloat16)
    return from_windows(result, height, breadth)


def feed_forward(tokens, w_up, w_down):
    normed = normalize(tokens).astype(jnp.bfloat16)
    hidden = jnp.einsum("...c,ce->...e", normed, w_up, preferred_element_type=jnp.float32)
    hidden = jax.nn.gelu(hidden, approximate=False).astype(jnp.bfloat16)
    output = tokens.astype(jnp.float32) + jnp.einsum(
        "...e,ec->...c", hidden, w_down, preferred_element_type=jnp.float32
    )
    return output.astype(jnp.bfloat16)


def reconstruct(padded, kernels, height, breadth):
    accumulated = jnp.zeros((padded.shape[0], height, breadth, kernels.shape[-1]), jnp.float32)
    for kernel_spot in range(9):
        spot_row, spot_col = (kernel_spot // 3, kernel_spot % 3)
        window = padded[:, spot_row : spot_row + height, spot_col : spot_col + breadth]
        accumulated = accumulated + jnp.einsum(
            "vrcd,vde->vrce", window, kernels[:, kernel_spot], preferred_element_type=jnp.float32
        )
    return accumulated


def refine(average, region, w_qkv, w_proj, bias_grid):
    normed = normalize(average).astype(jnp.bfloat16)[None]
    return average + attend(normed, region, w_qkv, w_proj, bias_grid)[0]


def local(
    features,
    labels,
    qkv_weight,
    proj_weight,
    up_weight,
    down_weight,
    swin_bias,
    recon_weight,
    refine_qkv,
    refine_proj,
    refine_bias,
):
    height, breadth, channels = features.shape
    variant_codes = lax.axis_index("var") * VAR_DEV + jnp.arange(VAR_DEV, dtype=jnp.int32)
    first_bias = bias_table(swin_bias[0], variant_codes)
    second_bias = bias_table(swin_bias[1], variant_codes)
    block_one = block_on_grid(
        features[None], labels, 0, qkv_weight, proj_weight, up_weight, down_weight, first_bias
    )
    tagged = jnp.broadcast_to(labels.astype(jnp.bfloat16)[None, :, :, None], block_one.shape[:3] + (1,))
    carried = halo(jnp.concatenate([block_one, tagged], axis=-1), SHIFT)
    shifted = carried[..., :channels]
    region = carried[0, :, :, channels].astype(jnp.int32)
    block_two = block_on_grid(
        shifted, region, 1, qkv_weight, proj_weight, up_weight, down_weight, second_bias
    )
    padded = block_two[:, SHIFT - 1 : SHIFT + height + 1, SHIFT - 1 : SHIFT + breadth + 1]
    row = lax.axis_index("ty") * height - 1 + jnp.arange(height + 2)
    col = lax.axis_index("tx") * breadth - 1 + jnp.arange(breadth + 2)
    inside = ((row >= 0) & (row < lax.axis_size("ty") * height))[:, None] & (
        (col >= 0) & (col < lax.axis_size("tx") * breadth)
    )[None, :]
    padded = jnp.where(inside[None, :, :, None], padded, jnp.zeros_like(padded))
    kernels = variant_kernels(recon_weight, variant_codes)
    summed = jnp.sum(reconstruct(padded, kernels, height, breadth), axis=0)
    region_windows = to_windows(labels[None, :, :, None])[0, :, :, 0]
    refine_grid = bias_table(refine_bias, jnp.zeros((1,), jnp.int32))
    rows, cols, depth = summed.shape
    combined = var_sum(summed.astype(jnp.bfloat16).reshape(rows, cols * depth)).reshape(rows, cols, depth)
    refined = refine(
        to_windows(combined[None])[0] / 8.0, region_windows, refine_qkv, refine_proj, refine_grid
    )
    refined = lax.optimization_barrier(refined)
    colours = refined.shape[-1] // (SCALE * SCALE)
    picture = refined.reshape(
        height // WIN, breadth // WIN, WIN, WIN, colours * SCALE, SCALE
    ).transpose(4, 0, 2, 1, 3, 5)
    picture = picture.reshape(colours, SCALE, height, breadth * SCALE).transpose(0, 2, 1, 3)
    return picture.reshape(colours, SCALE * height, SCALE * breadth)


def solution(mesh):
    placed = (P("ty", "tx", None), P("ty", "tx"), P(), P(), P(), P(), P(), P(), P(), P(), P())
    return jax.shard_map(
        local, mesh=mesh, in_specs=placed, out_specs=P(None, "ty", "tx"), check_vma=False
    )
```

```python
import functools

import jax
import jax.numpy as jnp
from jax import lax
from jax.experimental import pallas as pl
from jax.experimental.pallas import tpu as pltpu
from jax.sharding import PartitionSpec as P

MESH = pl.DeviceIdType.MESH

WIN = 8
SHIFT = 4
SCALE = 4
VAR_DEV = 2


EPSILON = 1e-05
MASKED = -1e30


def extended(cells, sides, width):
    for axis, dim in sides:
        count = lax.axis_size(axis)
        ends = count - 1
        head = lax.slice_in_dim(cells, 0, width, axis=dim)
        tail = lax.slice_in_dim(cells, cells.shape[dim] - width, cells.shape[dim], axis=dim)
        cells = jnp.concatenate(
            [
                lax.ppermute(tail, axis, [(i, (i + 1) % count) for i in range(ends)]),
                cells,
                lax.ppermute(head, axis, [((i + 1) % count, i) for i in range(ends)]),
            ],
            axis=dim,
        )
    return cells


def var_sum_kernel(count, part_ref, out_ref, held, send_sem, recv_sem):
    me = lax.axis_index("var")
    barrier = pltpu.get_barrier_semaphore()
    for step in range(1, count):
        peer = lax.rem(me + step, count)
        pl.semaphore_signal(barrier, inc=1, device_id={"var": peer}, device_id_type=MESH)
    pl.semaphore_wait(barrier, count - 1)
    sends = []
    for step in range(1, count):
        peer = lax.rem(me + step, count)
        copy = pltpu.make_async_remote_copy(
            src_ref=part_ref,
            dst_ref=held.at[me],
            send_sem=send_sem.at[step - 1],
            recv_sem=recv_sem.at[me],
            device_id={"var": peer},
            device_id_type=MESH,
        )
        copy.start()
        sends.append(copy)
    held[me] = part_ref[...]
    for copy in sends:
        copy.wait_send()
    for step in range(1, count):
        source = lax.rem(me + count - step, count)
        pltpu.make_async_remote_copy(
            src_ref=part_ref,
            dst_ref=held.at[source],
            send_sem=send_sem.at[step - 1],
            recv_sem=recv_sem.at[source],
            device_id={"var": source},
            device_id_type=MESH,
        ).wait_recv()
    total = held[0].astype(jnp.float32)
    for index in range(1, count):
        total = total + held[index].astype(jnp.float32)
    out_ref[...] = total


def var_sum(part):
    count = lax.axis_size("var")
    return pl.pallas_call(
        functools.partial(var_sum_kernel, count),
        out_shape=jax.ShapeDtypeStruct(part.shape, jnp.float32),
        in_specs=[pl.BlockSpec(memory_space=pltpu.VMEM)],
        out_specs=pl.BlockSpec(memory_space=pltpu.VMEM),
        scratch_shapes=[
            pltpu.VMEM((count,) + part.shape, part.dtype),
            pltpu.SemaphoreType.DMA((count - 1,)),
            pltpu.SemaphoreType.DMA((count,)),
        ],
        compiler_params=pltpu.CompilerParams(collective_id=0, has_side_effects=True),
    )(part)


GROUP = 4
LANE = 128


def block_kernel(
    variants, heads, scale, x_ref, labq_ref, labk_ref, bias_ref, wqkv_ref, wp_ref, wup_ref, wdown_ref, out_ref, wide_ref
):
    @pl.when(pl.program_id(0) == 0)
    def _():
        for variant in range(variants):
            for head in range(heads):
                wide_ref[variant, head] = jnp.concatenate([bias_ref[variant, head]] * (wide_ref.shape[-1] // (WIN * WIN)), axis=1)

    inputs = x_ref.shape[0]
    tokens = x_ref.shape[2]
    labq = labq_ref[0]
    labk = labk_ref[0]
    slot_q = lax.broadcasted_iota(jnp.int32, (tokens, tokens), 0) // (WIN * WIN)
    slot_k = lax.broadcasted_iota(jnp.int32, (tokens, tokens), 1) // (WIN * WIN)
    match = (labq == labk) & (slot_q == slot_k)
    projected = []
    for index in range(inputs):
        normed = normalize(x_ref[index, 0]).astype(jnp.bfloat16)
        projected.append(
            jnp.dot(normed, wqkv_ref[...], preferred_element_type=jnp.float32).astype(jnp.bfloat16)
        )
    span = wp_ref.shape[0]
    width = wup_ref.shape[0] // heads
    lane = lax.broadcasted_iota(jnp.int32, (1, span), 1)
    for variant in range(variants):
        source = variant if inputs > 1 else 0
        qkv = projected[source]
        query = qkv[:, :span]
        key = qkv[:, span : 2 * span]
        value = qkv[:, 2 * span :]
        mixed = jnp.zeros((tokens, span), jnp.float32)
        for head in range(heads):
            mine = (lane >= head * width) & (lane < (head + 1) * width)
            scores = lax.dot_general(
                jnp.where(mine, query, jnp.zeros_like(query)),
                key,
                (((1,), (1,)), ((), ())),
                preferred_element_type=jnp.float32,
            )
            scores = scores * scale
            scores = (scores.reshape(tokens // (WIN * WIN), WIN * WIN, tokens) + wide_ref[variant, head][None]).reshape(
                tokens, tokens
            )
            scores = jnp.where(match, scores, MASKED)
            largest = jnp.max(scores, axis=-1, keepdims=True)
            weights = jnp.exp(scores - largest)
            probabilities = (weights / jnp.sum(weights, axis=-1, keepdims=True)).astype(jnp.bfloat16)
            mixed = mixed + jnp.dot(
                probabilities, jnp.where(mine, value, jnp.zeros_like(value)), preferred_element_type=jnp.float32
            )
        branch = jnp.dot(mixed.astype(jnp.bfloat16), wp_ref[...], preferred_element_type=jnp.float32)
        own = x_ref[source, 0].astype(jnp.float32)
        hidden_in = (own + branch).astype(jnp.bfloat16)
        normed = normalize(hidden_in).astype(jnp.bfloat16)
        hidden = jnp.dot(normed, wup_ref[...], preferred_element_type=jnp.float32)
        hidden = (0.5 * hidden * (1.0 + lax.erf(hidden * (2.0 ** -0.5)))).astype(jnp.bfloat16)
        result = hidden_in.astype(jnp.float32) + jnp.dot(
            hidden, wdown_ref[...], preferred_element_type=jnp.float32
        )
        out_ref[variant, 0] = result.astype(jnp.bfloat16)


def padded_weights(w_qkv, w_proj, heads):
    channels = w_proj.shape[0]
    span = -(-channels // LANE) * LANE
    columns = jnp.pad(w_qkv.reshape(channels, 3, channels), ((0, 0), (0, 0), (0, span - channels)))
    rows = jnp.pad(w_proj, ((0, span - channels), (0, 0)))
    return columns.reshape(channels, 3 * span), rows


def swin_block(windows, region, layer, w_qkv, w_proj, w_up, w_down, bias_grid):
    inputs, count, cells, channels = windows.shape
    variants, heads = bias_grid.shape[:2]
    size = 5 if count % GROUP and count % 5 == 0 else GROUP
    groups = -(-count // size)
    extra = groups * size - count
    windows = jnp.pad(windows, ((0, 0), (0, extra), (0, 0), (0, 0)))
    region = jnp.pad(region, ((0, extra), (0, 0)))
    tokens = size * cells
    x = windows.reshape(inputs, groups, tokens, channels)
    labq = region.reshape(groups, tokens, 1)
    labk = region.reshape(groups, 1, tokens)
    bias = bias_grid
    scale = (channels // heads) ** (-0.5)
    whole = lambda shape: pl.BlockSpec(shape, lambda g: (0,) * len(shape))
    out = pl.pallas_call(
        functools.partial(block_kernel, variants, heads, scale),
        out_shape=jax.ShapeDtypeStruct((variants, groups, tokens, channels), jnp.bfloat16),
        grid=(groups,),
        in_specs=[
            pl.BlockSpec((inputs, 1, tokens, channels), lambda g: (0, g, 0, 0)),
            pl.BlockSpec((1, tokens, 1), lambda g: (g, 0, 0)),
            pl.BlockSpec((1, 1, tokens), lambda g: (g, 0, 0)),
            whole(bias.shape),
            pl.BlockSpec((None,) + w_qkv.shape[1:], lambda g: (layer, 0, 0)),
            pl.BlockSpec((None,) + w_proj.shape[1:], lambda g: (layer, 0, 0)),
            pl.BlockSpec((None,) + w_up.shape[1:], lambda g: (layer, 0, 0)),
            pl.BlockSpec((None,) + w_down.shape[1:], lambda g: (layer, 0, 0)),
        ],
        out_specs=pl.BlockSpec((variants, 1, tokens, channels), lambda g: (0, g, 0, 0)),
        scratch_shapes=[pltpu.VMEM((variants, heads, cells, tokens), jnp.float32)],
        compiler_params=pltpu.CompilerParams(vmem_limit_bytes=48 * 1024 * 1024),
    )(x, labq, labk, bias, w_qkv, w_proj, w_up, w_down)
    out = out.reshape(variants, groups * size, cells, channels)
    return out[:, :count]


def block_on_grid(tokens, region, layer, w_qkv, w_proj, w_up, w_down, bias_grid):
    height, breadth = tokens.shape[1], tokens.shape[2]
    windows = to_windows(tokens)
    region_windows = to_windows(region[None, :, :, None])[0, :, :, 0]
    out = swin_block(windows, region_windows, layer, w_qkv, w_proj, w_up, w_down, bias_grid)
    return from_windows(out, height, breadth)


def normalize(values):
    values = values.astype(jnp.float32)
    average = jnp.mean(values, axis=-1, keepdims=True)
    centred = values - average
    spread = jnp.mean(centred * centred, axis=-1, keepdims=True)
    return centred * lax.rsqrt(spread + EPSILON)


def to_windows(grid):
    leading, height, breadth, channels = grid.shape
    grid = grid.reshape(leading, height // WIN, WIN, breadth // WIN, WIN, channels)
    grid = grid.transpose(0, 1, 3, 2, 4, 5)
    return grid.reshape(leading, height // WIN * (breadth // WIN), WIN * WIN, channels)


def from_windows(windows, height, breadth):
    leading, window_count, cells, channels = windows.shape
    windows = windows.reshape(leading, height // WIN, breadth // WIN, WIN, WIN, channels)
    windows = windows.transpose(0, 1, 3, 2, 4, 5)
    return windows.reshape(leading, height, breadth, channels)


def bias_table(offset_table, variant_codes):
    position = jnp.arange(WIN * WIN, dtype=jnp.int32)
    row_step = (position // WIN)[:, None] - (position // WIN)[None, :]
    across = (position % WIN)[:, None] - (position % WIN)[None, :]
    transpose_bit = (variant_codes // 4)[:, None, None]
    flip_rows = (variant_codes // 2 % 2)[:, None, None]
    flip_cols = (variant_codes % 2)[:, None, None]
    row_moved = jnp.where(flip_rows == 1, -row_step, row_step)
    col_moved = jnp.where(flip_cols == 1, -across, across)
    leading_step = jnp.where(transpose_bit == 1, col_moved, row_moved)
    trailing_step = jnp.where(transpose_bit == 1, row_moved, col_moved)
    table_index = (leading_step + WIN - 1) * (2 * WIN - 1) + trailing_step + WIN - 1
    slots = jnp.arange((2 * WIN - 1) * (2 * WIN - 1), dtype=jnp.int32)
    one_hot = (table_index[..., None] == slots).astype(jnp.bfloat16)
    high = lax.reduce_precision(offset_table, exponent_bits=8, mantissa_bits=7)
    rest = offset_table - high
    middle = lax.reduce_precision(rest, exponent_bits=8, mantissa_bits=7)
    low = rest - middle
    parts = jnp.concatenate([high, middle, low], axis=0).astype(jnp.bfloat16)
    picked = jnp.einsum("vqkt,ht->vhqk", one_hot, parts, preferred_element_type=jnp.float32)
    heads = offset_table.shape[0]
    return (picked[:, :heads] + picked[:, heads : 2 * heads]) + picked[:, 2 * heads :]


def variant_kernels(kernel, variant_codes):
    transpose_bit = (variant_codes // 4)[:, None]
    flip_rows = (variant_codes // 2 % 2)[:, None]
    flip_cols = (variant_codes % 2)[:, None]
    kernel_spot = jnp.arange(9, dtype=jnp.int32)
    step_row = (kernel_spot // 3 - 1)[None, :]
    step_col = (kernel_spot % 3 - 1)[None, :]
    row_moved = jnp.where(flip_rows == 1, -step_row, step_row)
    col_moved = jnp.where(flip_cols == 1, -step_col, step_col)
    source_row = jnp.where(transpose_bit == 1, col_moved, row_moved)
    source_col = jnp.where(transpose_bit == 1, row_moved, col_moved)
    source = (source_row + 1) * 3 + source_col + 1
    pick_place = (source[:, :, None] == kernel_spot[None, None, :]).astype(jnp.bfloat16)
    channel = jnp.arange(kernel.shape[-1], dtype=jnp.int32)
    colour = (channel // (SCALE * SCALE))[None, :]
    sub_row = (channel % (SCALE * SCALE) // SCALE)[None, :]
    sub_col = (channel % SCALE)[None, :]
    sub_row_moved = jnp.where(flip_rows == 1, SCALE - 1 - sub_row, sub_row)
    sub_col_moved = jnp.where(flip_cols == 1, SCALE - 1 - sub_col, sub_col)
    anchor_row = jnp.where(transpose_bit == 1, sub_col_moved, sub_row_moved)
    anchor_col = jnp.where(transpose_bit == 1, sub_row_moved, sub_col_moved)
    anchor = colour * SCALE * SCALE + anchor_row * SCALE + anchor_col
    pick_channel = (channel[None, :, None] == anchor[:, None, :]).astype(jnp.bfloat16)
    placed = jnp.einsum(
        "vpq,qcs->vpcs", pick_place, kernel, preferred_element_type=jnp.float32
    ).astype(jnp.bfloat16)
    return jnp.einsum(
        "vpcs,vso->vpco", placed, pick_channel, preferred_element_type=jnp.float32
    ).astype(jnp.bfloat16)


def attend(normed, region, w_qkv, w_proj, bias_grid):
    head_count = bias_grid.shape[1]
    leading, window_count, cells, channels = normed.shape
    head_width = channels // head_count
    projected = jnp.einsum(
        "lnsc,ce->lnse", normed, w_qkv, preferred_element_type=jnp.float32
    ).astype(jnp.bfloat16)
    projected = projected.reshape(leading, window_count, cells, 3, head_count, head_width)
    queries = projected[:, :, :, 0]
    key_part = projected[:, :, :, 1]
    value_part = projected[:, :, :, 2]
    scores = jnp.einsum("lnqhd,lnkhd->lnhqk", queries, key_part, preferred_element_type=jnp.float32)
    scores = scores * head_width ** (-0.5) + bias_grid[:, None]
    matches = region[:, None, :, None] == region[:, None, None, :]
    scores = jnp.where(matches[None], scores, MASKED)
    largest = jnp.max(scores, axis=-1, keepdims=True)
    weights = jnp.exp(scores - largest)
    probabilities = (weights / jnp.sum(weights, axis=-1, keepdims=True)).astype(jnp.bfloat16)
    value_part = jnp.broadcast_to(value_part, (probabilities.shape[0],) + value_part.shape[1:])
    mixed = jnp.einsum(
        "lnhqk,lnkhd->lnqhd", probabilities, value_part, preferred_element_type=jnp.float32
    ).astype(jnp.bfloat16)
    mixed = mixed.reshape(probabilities.shape[0], window_count, cells, channels)
    return jnp.einsum("lnsc,ce->lnse", mixed, w_proj, preferred_element_type=jnp.float32)


def attention_half(tokens, region, w_qkv, w_proj, bias_grid):
    height, breadth = (tokens.shape[1], tokens.shape[2])
    windows = to_windows(tokens)
    region_windows = to_windows(region[None, :, :, None])[0, :, :, 0]
    normed = normalize(windows).astype(jnp.bfloat16)
    branch = attend(normed, region_windows, w_qkv, w_proj, bias_grid)
    result = (windows.astype(jnp.float32) + branch).astype(jnp.bfloat16)
    return from_windows(result, height, breadth)


def feed_forward(tokens, w_up, w_down):
    normed = normalize(tokens).astype(jnp.bfloat16)
    hidden = jnp.einsum("...c,ce->...e", normed, w_up, preferred_element_type=jnp.float32)
    hidden = jax.nn.gelu(hidden, approximate=False).astype(jnp.bfloat16)
    output = tokens.astype(jnp.float32) + jnp.einsum(
        "...e,ec->...c", hidden, w_down, preferred_element_type=jnp.float32
    )
    return output.astype(jnp.bfloat16)


def reconstruct(padded, kernels, height, breadth):
    accumulated = jnp.zeros((padded.shape[0], height, breadth, kernels.shape[-1]), jnp.float32)
    for kernel_spot in range(9):
        spot_row, spot_col = (kernel_spot // 3, kernel_spot % 3)
        window = padded[:, spot_row : spot_row + height, spot_col : spot_col + breadth]
        accumulated = accumulated + jnp.einsum(
            "vrcd,vde->vrce", window, kernels[:, kernel_spot], preferred_element_type=jnp.float32
        )
    return accumulated


def refine(average, region, w_qkv, w_proj, bias_grid):
    normed = normalize(average).astype(jnp.bfloat16)[None]
    return average + attend(normed, region, w_qkv, w_proj, bias_grid)[0]


def local(
    features,
    labels,
    qkv_weight,
    proj_weight,
    up_weight,
    down_weight,
    swin_bias,
    recon_weight,
    refine_qkv,
    refine_proj,
    refine_bias,
):
    height, breadth, channels = features.shape
    variant_codes = lax.axis_index("var") * VAR_DEV + jnp.arange(VAR_DEV, dtype=jnp.int32)
    first_bias = bias_table(swin_bias[0], variant_codes)
    second_bias = bias_table(swin_bias[1], variant_codes)
    block_one = block_on_grid(
        features[None], labels, 0, qkv_weight, proj_weight, up_weight, down_weight, first_bias
    )
    tagged = jnp.broadcast_to(labels.astype(jnp.bfloat16)[None, :, :, None], block_one.shape[:3] + (1,))
    carried = extended(jnp.concatenate([block_one, tagged], axis=-1), (("tx", 2), ("ty", 1)), SHIFT)
    shifted = carried[..., :channels]
    region = carried[0, :, :, channels].astype(jnp.int32)
    block_two = block_on_grid(
        shifted, region, 1, qkv_weight, proj_weight, up_weight, down_weight, second_bias
    )
    padded = block_two[:, SHIFT - 1 : SHIFT + height + 1, SHIFT - 1 : SHIFT + breadth + 1]
    row = lax.axis_index("ty") * height - 1 + jnp.arange(height + 2)
    col = lax.axis_index("tx") * breadth - 1 + jnp.arange(breadth + 2)
    inside = ((row >= 0) & (row < lax.axis_size("ty") * height))[:, None] & (
        (col >= 0) & (col < lax.axis_size("tx") * breadth)
    )[None, :]
    padded = jnp.where(inside[None, :, :, None], padded, jnp.zeros_like(padded))
    kernels = variant_kernels(recon_weight, variant_codes)
    summed = jnp.sum(reconstruct(padded, kernels, height, breadth), axis=0)
    region_windows = to_windows(labels[None, :, :, None])[0, :, :, 0]
    refine_grid = bias_table(refine_bias, jnp.zeros((1,), jnp.int32))
    rows, cols, depth = summed.shape
    combined = var_sum(summed.astype(jnp.bfloat16).reshape(rows, cols * depth)).reshape(rows, cols, depth)
    refined = refine(
        to_windows(combined[None])[0] / 8.0, region_windows, refine_qkv, refine_proj, refine_grid
    )
    refined = lax.optimization_barrier(refined)
    colours = refined.shape[-1] // (SCALE * SCALE)
    picture = refined.reshape(
        height // WIN, breadth // WIN, WIN, WIN, colours * SCALE, SCALE
    ).transpose(4, 0, 2, 1, 3, 5)
    picture = picture.reshape(colours, SCALE, height, breadth * SCALE).transpose(0, 2, 1, 3)
    return picture.reshape(colours, SCALE * height, SCALE * breadth)


def solution(mesh):
    placed = (P("ty", "tx", None), P("ty", "tx"), P(), P(), P(), P(), P(), P(), P(), P(), P())
    return jax.shard_map(
        local, mesh=mesh, in_specs=placed, out_specs=P(None, "ty", "tx"), check_vma=False
    )
```
